32 devices in a mesh: period: 8 (over z, y), refinery: 4 (over x, core).
Axes of the slice: x: 2, y: 2, z: 4, core: 2. Of those that a mesh axis runs over, the one named last changes fastest.
Arguments:
- local_blocks: bfloat16 [3072, 128, 128], P(('period', 'refinery')), may hold values from -0.15625 to 0.15625
- local_rows: int32 [3072], P(('period', 'refinery')), may hold values from 0 to 7
- local_cols: int32 [3072], P(('period', 'refinery')), may hold values from 0 to 7
- band_count: int32 [32], P(('period', 'refinery')), may hold values from 12 to 96, as said below
- swing_blocks: bfloat16 [256, 128, 128], P(('period', 'refinery')), may hold values from -0.5 to 0.5
- swing_rows: int32 [256], P(('period', 'refinery')), may hold values from 0 to 7
- swing_src: int32 [256], P(('period', 'refinery')), may hold values from 0 to 7
- carry_blocks: bfloat16 [32, 128, 128], P(('period', 'refinery')), may hold values from -0.5 to 0.5
- annual_blocks: bfloat16 [256, 128, 128], P(('period', 'refinery')), may hold values from -0.1875 to 0.1875
- annual_ids: int32 [256], P(('period', 'refinery')), may hold values from 0 to 7
- annual_cols: int32 [256], P(('period', 'refinery')), may hold values from 0 to 7
- cost: float32 [32768, 128], P(('period', 'refinery')), may hold values from -6 to 6
- upper: float32 [32768], P(('period', 'refinery')), may hold values from 0.25 to 1.5
- demand: float32 [32768], P(('period', 'refinery')), may hold values from -6 to 6
- annual_bound: float32 [4096], P(('period', 'refinery')), may hold values from -6 to 6
- x_start: float32 [32768, 128], P(('period', 'refinery')), may hold values from 0 to 1
- y_start: float32 [32768, 128], P(('period', 'refinery')), may hold values from 0 to 1
- annual_start: float32 [4096, 128], P(('period', 'refinery')), may hold values from 0 to 1
Outputs:
- primal: float32 [32768, 128], P(('period', 'refinery'))
- dual_rows: float32 [32768, 128], P(('period', 'refinery'))
- annual_dual: float32 [4096, 128], P(('period', 'refinery'))
The draws below stay inside these ranges and needn't reach their ends.
Inputs may be any that keep to these rules, and one draw needn't show every extreme that they name: `band_count`: live block slots of a group; exactly 96 on one or more groups in every draw.
All inputs are finite; a program needn't handle non-finite values.
Results may differ from the reference program's by a relative error of at most 0.0027.
Values may be sent and summed in bfloat16 or wider, within the bound.
No kernel may reach another device: no remote copies, remote signals or barrier semaphores. Data moves between devices by JAX's collectives and lax.ppermute only.
A program may use at most 128 MiB of HBM per device.

```python
import jax
import jax.numpy as jnp
from jax import lax

S = 128
BS = 128
CB = 8
RB = 8
NL = 96
SW = 8
SC = 2
NA = 8
ITERS = 2
WEEKS = 8
PLANTS = 4


def draw_band_count(key, part):
    first_key, second_key = jax.random.split(jax.random.fold_in(key, 17))
    groups = WEEKS * PLANTS
    divisor = jax.random.randint(first_key, (groups,), 1, 9)
    counts = NL // divisor
    chosen = jax.random.randint(second_key, (), 0, groups)
    return jnp.where(jnp.arange(groups, dtype=jnp.int32) == chosen, NL, counts).astype(jnp.int32)


def place_ends(entries, key, least, high):
    shape = entries.shape
    index_at = [jax.random.randint(jax.random.fold_in(key, axis), (), 0, shape[axis]) for axis in range(len(shape))]
    entries = entries.at[tuple(index_at)].set(least)
    longest = shape.index(max(shape))
    index_at[longest] = (index_at[longest] + 1) % shape[longest]
    return entries.at[tuple(index_at)].set(high)


def steps_of(rng, dims, pieces, low, largest):
    factor_of = 1.0
    for dim, parts in pieces:
        draws = jax.random.uniform(jax.random.fold_in(jax.random.fold_in(rng, 6), dim), (parts,), jnp.float32, low / len(pieces), largest / len(pieces))
        factor_of = factor_of * jnp.repeat(jnp.exp(draws), dims[dim] // parts).reshape((-1,) + (1,) * (len(dims) - 1 - dim))
    return factor_of


def centred(key, shape, scale, most, cuts=(), held_as=jnp.bfloat16):
    level = steps_of(key, shape, cuts, -0.22, 0.18) if cuts else 1.0
    entries = jax.random.normal(key, shape, jnp.float32) * scale * level
    return jnp.minimum(jnp.maximum(entries, -most), most).astype(held_as)


def setup_inputs(seed: int = 0) -> dict:
    streams_of = jax.random.split(jax.random.key(seed), 19)
    local_blocks = centred(streams_of[0], (WEEKS * PLANTS * NL, BS, BS), (NL // RB * BS) ** -0.5, 0.15625, ((0, 32),))
    local_rows = place_ends(jax.random.randint(streams_of[1], (WEEKS * PLANTS * NL,), 0, RB), jax.random.fold_in(streams_of[1], 1), 0, RB - 1).astype(jnp.int32)
    local_cols = place_ends(jax.random.randint(streams_of[2], (WEEKS * PLANTS * NL,), 0, CB), jax.random.fold_in(streams_of[2], 1), 0, CB - 1).astype(jnp.int32)
    band_count = draw_band_count(jax.random.fold_in(streams_of[18], 71), 0)
    swing_blocks = centred(streams_of[4], (WEEKS * PLANTS * SW, BS, BS), BS ** -0.5, 0.5, ((0, 32),))
    swing_rows = place_ends(jax.random.randint(streams_of[5], (WEEKS * PLANTS * SW,), 0, RB), jax.random.fold_in(streams_of[5], 1), 0, RB - 1).astype(jnp.int32)
    swing_src = place_ends(jax.random.randint(streams_of[6], (WEEKS * PLANTS * SW,), 0, PLANTS * SC), jax.random.fold_in(streams_of[6], 1), 0, (PLANTS * SC) - 1).astype(jnp.int32)
    carry_blocks = centred(streams_of[7], (WEEKS * PLANTS, BS, BS), BS ** -0.5, 0.5, ((0, 32),))
    annual_blocks = centred(streams_of[8], (WEEKS * PLANTS * NA, BS, BS), (NA * BS) ** -0.5, 0.1875, ((0, 32),))
    annual_ids = place_ends(jax.random.randint(streams_of[9], (WEEKS * PLANTS * NA,), 0, WEEKS), jax.random.fold_in(streams_of[9], 1), 0, WEEKS - 1).astype(jnp.int32)
    annual_cols = place_ends(jax.random.randint(streams_of[10], (WEEKS * PLANTS * NA,), 0, CB), jax.random.fold_in(streams_of[10], 1), 0, CB - 1).astype(jnp.int32)
    cost = centred(streams_of[11], (WEEKS * PLANTS * CB * BS, S), 1.0, 6.0, ((0, 32),), jnp.float32)
    upper = jnp.clip(0.25 + 1.25 * jax.random.uniform(streams_of[12], (WEEKS * PLANTS * CB * BS,), jnp.float32) ** steps_of(streams_of[12], (WEEKS * PLANTS * CB * BS,), ((0, 32),), -0.2, 0.2), 0.25, 1.5)
    demand = centred(streams_of[13], (WEEKS * PLANTS * RB * BS,), 1.0, 6.0, ((0, 32),), jnp.float32)
    annual_bound = centred(streams_of[14], (WEEKS * PLANTS * BS,), 1.0, 6.0, ((0, 32),), jnp.float32)
    x_start = jnp.clip(1.0 * jax.random.uniform(streams_of[15], (WEEKS * PLANTS * CB * BS, S), jnp.float32) ** steps_of(streams_of[15], (WEEKS * PLANTS * CB * BS, S), ((0, 32),), -0.2, 0.2), 0.0, 1.0)
    y_start = jnp.clip(1.0 * jax.random.uniform(streams_of[16], (WEEKS * PLANTS * RB * BS, S), jnp.float32) ** steps_of(streams_of[16], (WEEKS * PLANTS * RB * BS, S), ((0, 32),), -0.2, 0.2), 0.0, 1.0)
    annual_start = jnp.clip(1.0 * jax.random.uniform(streams_of[17], (WEEKS * PLANTS * BS, S), jnp.float32) ** steps_of(streams_of[17], (WEEKS * PLANTS * BS, S), ((0, 32),), -0.2, 0.2), 0.0, 1.0)
    return dict(local_blocks=local_blocks, local_rows=local_rows, local_cols=local_cols, band_count=band_count, swing_blocks=swing_blocks, swing_rows=swing_rows, swing_src=swing_src, carry_blocks=carry_blocks, annual_blocks=annual_blocks, annual_ids=annual_ids, annual_cols=annual_cols, cost=cost, upper=upper, demand=demand, annual_bound=annual_bound, x_start=x_start, y_start=y_start, annual_start=annual_start)


PRIMAL_STEP = 0.5
DUAL_STEP = 0.5
PRECISE = lax.Precision.HIGHEST


def selector(index, number):
    return (index[None, :] == jnp.arange(number, dtype=jnp.int32)[:, None]).astype(jnp.float32)


def collect(select, products):
    return jnp.einsum('rn,nas->ras', select, products, precision=PRECISE)


def forward_part(blocks, vectors):
    return jnp.einsum('nab,nbs->nas', blocks.astype(jnp.float32), vectors.astype(jnp.float32), precision=PRECISE)


def adjoint_part(blocks, vectors):
    return jnp.einsum('nab,nas->nbs', blocks.astype(jnp.float32), vectors.astype(jnp.float32), precision=PRECISE)


def reference(local_blocks, local_rows, local_cols, band_count, swing_blocks, swing_rows, swing_src, carry_blocks, annual_blocks, annual_ids, annual_cols, cost, upper, demand, annual_bound, x_start, y_start, annual_start):
    devices = WEEKS * PLANTS
    scenarios = cost.shape[1]
    local_set = local_blocks.reshape(devices, NL, BS, BS)
    swing_set = swing_blocks.reshape(devices, SW, BS, BS)
    annual_set = annual_blocks.reshape(devices, NA, BS, BS)
    row_ids = local_rows.reshape(devices, NL)
    col_ids = local_cols.reshape(devices, NL)
    swing_row_ids = swing_rows.reshape(devices, SW)
    swing_src_ids = swing_src.reshape(devices, SW)
    annual_row_ids = annual_ids.reshape(devices, NA)
    annual_col_ids = annual_cols.reshape(devices, NA)
    slot_index = jnp.arange(NL, dtype=jnp.int32)
    device_index = jnp.arange(devices, dtype=jnp.int32)

    def apply_forward(extrap):
        streams = extrap[:, :SC].reshape(WEEKS, PLANTS * SC, BS, scenarios)
        previous = jnp.roll(extrap[:, CB - 1].reshape(WEEKS, PLANTS, BS, scenarios), 1, axis=0).reshape(devices, BS, scenarios)

        def one_device(device):
            owned = extrap[device]
            live_mask = (slot_index < band_count[device]).astype(jnp.float32)
            mapped = collect(selector(row_ids[device], RB) * live_mask[None, :], forward_part(local_set[device], owned[col_ids[device]]))
            week_streams = streams[device // PLANTS]
            mapped = mapped + collect(selector(swing_row_ids[device], RB), forward_part(swing_set[device], week_streams[swing_src_ids[device]]))
            mapped = mapped.at[0].add(jnp.dot(carry_blocks[device], previous[device], preferred_element_type=jnp.float32))
            annual_products = forward_part(annual_set[device], owned[annual_col_ids[device]])
            return mapped, annual_products

        mapped, annual_products = lax.map(one_device, device_index)
        targets = annual_row_ids * PLANTS + (device_index % PLANTS)[:, None]
        annual_image = jnp.zeros((devices, BS, scenarios), jnp.float32).at[targets.reshape(-1)].add(annual_products.reshape(-1, BS, scenarios))
        return mapped, annual_image

    def apply_adjoint(dual_q, annual_q):
        annual_by_plant = annual_q.reshape(WEEKS, PLANTS, BS, scenarios)

        def one_device(device):
            owned = dual_q[device]
            live_mask = (slot_index < band_count[device]).astype(jnp.float32)
            mapped = collect(selector(col_ids[device], CB) * live_mask[None, :], adjoint_part(local_set[device], owned[row_ids[device]]))
            plant_duals = annual_by_plant[:, device % PLANTS]
            mapped = mapped + collect(selector(annual_col_ids[device], CB), adjoint_part(annual_set[device], plant_duals[annual_row_ids[device]]))
            swing_products = adjoint_part(swing_set[device], owned[swing_row_ids[device]])
            carried = jnp.dot(carry_blocks[device].T, owned[0], preferred_element_type=jnp.float32)
            return mapped, swing_products, carried

        mapped, swing_products, carried = lax.map(one_device, device_index)
        week_ids = device_index // PLANTS
        targets = (week_ids[:, None] * PLANTS + swing_src_ids // SC) * CB + swing_src_ids % SC
        mapped = mapped.reshape(devices * CB, BS, scenarios).at[targets.reshape(-1)].add(swing_products.reshape(-1, BS, scenarios))
        mapped = mapped.reshape(devices, CB, BS, scenarios)
        returned = jnp.roll(carried.reshape(WEEKS, PLANTS, BS, scenarios), -1, axis=0).reshape(devices, BS, scenarios)
        return mapped.at[:, CB - 1].add(returned)

    primal = x_start.reshape(devices, CB, BS, scenarios)
    dual_state = y_start.reshape(devices, RB, BS, scenarios)
    annual = annual_start.reshape(devices, BS, scenarios)
    bound_up = upper.reshape(devices, CB, BS, 1)
    prices = cost.reshape(devices, CB, BS, scenarios)
    demand_col = demand.reshape(devices, RB, BS, 1)
    annual_need = annual_bound.reshape(devices, BS, 1)
    for iteration in range(ITERS):
        adjoint = apply_adjoint(dual_state.astype(jnp.bfloat16), annual.astype(jnp.bfloat16))
        updated = jnp.clip(primal - PRIMAL_STEP * (prices - adjoint), 0.0, bound_up)
        extrap = (2.0 * updated - primal).astype(jnp.bfloat16)
        mapped, annual_image = apply_forward(extrap)
        dual_state = jnp.maximum(dual_state + DUAL_STEP * (demand_col - mapped), 0.0)
        annual = jnp.maximum(annual + DUAL_STEP * (annual_need - annual_image), 0.0)
        primal = updated
    return primal.reshape(-1, scenarios), dual_state.reshape(-1, scenarios), annual.reshape(-1, scenarios)
```

```python
import functools

import jax
import jax.numpy as jnp
from jax import lax
from jax.experimental import pallas as pl
from jax.experimental.pallas import tpu as pltpu
from jax.sharding import PartitionSpec as P

SC = 2
ITERS = 2

PRIMAL_STEP = 0.5
DUAL_STEP = 0.5
F32 = jnp.float32
BF16 = jnp.bfloat16
VMEM = pl.BlockSpec(memory_space=pltpu.VMEM)
SMEM = pl.BlockSpec(memory_space=pltpu.SMEM)


def shape(dims, dtype):
    return jax.ShapeDtypeStruct(dims, dtype)


def call(kernel, name, specs, outs, scratch, flops, moved, mib=24):
    return pl.pallas_call(
        kernel,
        name=name,
        in_specs=specs,
        out_specs=tuple(VMEM for _ in outs),
        out_shape=tuple(outs),
        scratch_shapes=scratch,
        compiler_params=pltpu.CompilerParams(vmem_limit_bytes=mib << 20),
        cost_estimate=pl.CostEstimate(flops=flops, bytes_accessed=moved, transcendentals=0),
    )


def dot(a, b):
    return jnp.dot(a, b, preferred_element_type=F32)


def dot_transposed(a, b):
    return dot(a.T, b)


def column_of(row_vector, width):
    return jnp.broadcast_to(row_vector, (width, row_vector.shape[1])).T


def wrap(value, number):
    return jnp.where(value >= number, value - number, value)


def send_duals(refineries, dual_q, me, rows, src, swing, carry, own, sends, carried, acc):
    acc[...] = jnp.zeros_like(acc)
    for m in range(swing.shape[0]):
        acc[src[m]] += dot_transposed(swing[m], dual_q[rows[m]])
    own[...] = acc[pl.ds(me * SC, SC)]
    for d, send in enumerate(sends, 1):
        send[...] = acc[pl.ds(wrap(me + d, refineries) * SC, SC)].astype(BF16)
    carried[...] = dot_transposed(carry[0], dual_q[0]).astype(BF16)


def first_duals_kernel(refineries, me, rows, src, swing, carry, dual, *refs):
    sends = refs[1:refineries]
    own, carried, dual_q, acc = refs[0], *refs[refineries:]
    size = swing.shape[1]
    for i in range(dual_q.shape[0]):
        dual_q[i] = dual[i * size : (i + 1) * size].astype(BF16)
    send_duals(refineries, dual_q, me[0], rows, src, swing, carry, own, sends, carried, acc)


def dense_kernel(count, rows, cols, blocks, upper, high, low, upper_full, acc):
    size = blocks.shape[1]
    width = upper_full.shape[1]
    tiles = high.shape[1] // size
    acc[...] = jnp.zeros_like(acc)

    def step(n, _):
        acc[rows[n] * tiles + cols[n]] += blocks[n].astype(F32)
        return 0

    lax.fori_loop(0, count[0], step, 0)
    for i in range(high.shape[0] // size):
        for j in range(tiles):
            whole = acc[i * tiles + j]
            top = whole.astype(BF16)
            high[i * size : (i + 1) * size, j * size : (j + 1) * size] = top
            low[i * size : (i + 1) * size, j * size : (j + 1) * size] = (
                whole - top.astype(F32)
            ).astype(BF16)
    for j in range(tiles):
        upper_full[j * size : (j + 1) * size] = column_of(upper[j : j + 1], width)


def adjoint_kernel(high, low, dual_q, primal, prices, out):
    blocks, size, _ = dual_q.shape
    turned = jnp.concatenate([dual_q[i].T for i in range(blocks)], axis=1)
    step = 2 * size
    for j in range(high.shape[1] // step):
        part = dot(turned, high[:, j * step : (j + 1) * step]) + dot(
            turned, low[:, j * step : (j + 1) * step]
        )
        for h in range(2):
            at = slice(j * step + h * size, j * step + (h + 1) * size)
            out[at] = primal[at] - PRIMAL_STEP * (
                prices[at] - part[:, h * size : (h + 1) * size].T
            )


def primal_kernel(
    refineries, ids, cols, annual, annual_q, own, carried, partial, primal, upper_full, *refs
):
    arrived = refs[: refineries - 1]
    updated, extrap, streams, last, image, acc, image_acc = refs[refineries - 1 :]
    blocks, size, _ = extrap.shape
    acc[...] = jnp.zeros_like(acc)
    image_acc[...] = jnp.zeros_like(image_acc)
    slots = annual.shape[0]
    for k in range(slots):
        acc[cols[k]] += dot_transposed(annual[k], annual_q[ids[k]])
    total = own[...]
    for piece in arrived:
        total = total + piece[...].astype(F32)
    acc[:SC] += total
    acc[blocks - 1] += carried[...].astype(F32)
    for j in range(blocks):
        at = slice(j * size, (j + 1) * size)
        new = jnp.clip(partial[at] + PRIMAL_STEP * acc[j], 0.0, upper_full[at])
        updated[at] = new
        ahead = (2.0 * new - primal[at]).astype(BF16)
        extrap[j] = ahead
        if j < SC:
            streams[j] = ahead
        if j == blocks - 1:
            last[...] = ahead
    for k in range(slots):
        image_acc[ids[k]] += dot(annual[k], extrap[cols[k]])
    image[...] = image_acc[...].astype(BF16)


def forward_kernel(high, low, extrap, dual, demand, out):
    blocks, size, width = extrap.shape
    right = jnp.concatenate([extrap[j] for j in range(blocks)], axis=0)
    step = 2 * size
    for i in range(high.shape[0] // step):
        part = dot(high[i * step : (i + 1) * step], right) + dot(
            low[i * step : (i + 1) * step], right
        )
        for h in range(2):
            at = slice(i * step + h * size, i * step + (h + 1) * size)
            row = 2 * i + h
            out[at] = dual[at] + DUAL_STEP * (
                column_of(demand[row : row + 1], width) - part[h * size : (h + 1) * size]
            )


def dual_kernel(
    refineries, more, me, rows, src, swing, carry, partial, previous, streams, *refs
):
    arrived = refs[: refineries - 1]
    refs = refs[refineries - 1 :]
    dual = refs[0]
    gathered, acc = refs[-2:]
    size = swing.shape[1]
    blocks = dual.shape[0] // size
    mine = me[0]
    gathered[pl.ds(mine * SC, SC)] = streams[...]
    for d, piece in enumerate(arrived, 1):
        gathered[pl.ds(wrap(mine + refineries - d, refineries) * SC, SC)] = piece[...]
    acc[...] = jnp.zeros_like(acc)
    for m in range(swing.shape[0]):
        acc[rows[m]] += dot(swing[m], gathered[src[m]])
    acc[0] += dot(carry[0], previous[...])
    for i in range(blocks):
        at = slice(i * size, (i + 1) * size)
        dual[at] = jnp.maximum(partial[at] - DUAL_STEP * acc[i], 0.0)
    if more:
        own = refs[1]
        sends = refs[2 : refineries + 1]
        carried, dual_q, stream_acc = refs[refineries + 1 : refineries + 4]
        for i in range(blocks):
            dual_q[i] = dual[i * size : (i + 1) * size].astype(BF16)
        send_duals(refineries, dual_q, mine, rows, src, swing, carry, own, sends, carried, stream_acc)


def annual_kernel(more, annual, need, parts, *outs):
    total = parts[0].astype(F32)
    for w in range(1, parts.shape[0]):
        total = total + parts[w].astype(F32)
    new = jnp.maximum(
        annual[...] + DUAL_STEP * (column_of(need[...], annual.shape[1]) - total), 0.0
    )
    outs[0][...] = new
    if more:
        rounded = new.astype(BF16)
        for w in range(outs[1].shape[0]):
            outs[1][w] = rounded


def shifted(block, axis, distance):
    number = lax.axis_size(axis)
    route = [((i - distance) % number, i) for i in range(number)]
    return lax.ppermute(block, axis, route)


def body(
    local_blocks,
    local_rows,
    local_cols,
    band_count,
    swing_blocks,
    swing_rows,
    swing_src,
    carry_blocks,
    annual_blocks,
    annual_ids,
    annual_cols,
    cost,
    upper,
    demand,
    annual_bound,
    x_start,
    y_start,
    annual_start,
):
    scenarios = cost.shape[1]
    size = local_blocks.shape[1]
    columns = cost.shape[0] // size
    rows = y_start.shape[0] // size
    weeks = lax.axis_size("period")
    refineries = lax.axis_size("refinery")
    others = refineries - 1
    streams_total = refineries * SC
    me = lax.axis_index("refinery").astype(jnp.int32).reshape(1)
    block = size * scenarios
    tile = shape((size, scenarios), BF16)
    pair_q = shape((SC, size, scenarios), BF16)
    pair = shape((SC, size, scenarios), F32)
    state_x = shape((columns * size, scenarios), F32)
    state_y = shape((rows * size, scenarios), F32)
    blocks_x = shape((columns, size, scenarios), BF16)
    blocks_y = shape((rows, size, scenarios), BF16)
    weekly = shape((weeks, size, scenarios), BF16)
    swings = swing_blocks.shape[0]
    annuals = annual_blocks.shape[0]
    unit = 2 * size * size * scenarios
    duals_scratch = pltpu.VMEM((streams_total, size, scenarios), F32)

    first_duals = call(
        functools.partial(first_duals_kernel, refineries),
        "first_duals",
        [SMEM] * 3 + [VMEM] * 3,
        [pair] + [pair_q] * others + [tile, blocks_y],
        [duals_scratch],
        (swings + 1) * unit,
        2_000_000,
    )
    dense = call(
        dense_kernel,
        "dense",
        [SMEM] * 3 + [VMEM] * 2,
        [shape((rows * size, columns * size), BF16)] * 2 + [state_x],
        [pltpu.VMEM((rows * columns, size, size), F32)],
        unit,
        8_000_000,
    )
    adjoint = call(
        adjoint_kernel,
        "adjoint",
        [VMEM] * 5,
        [state_x],
        [],
        2 * rows * columns * unit,
        5_000_000,
    )
    primal_step = call(
        functools.partial(primal_kernel, refineries),
        "primal_step",
        [SMEM] * 2 + [VMEM] * (7 + others),
        [state_x, blocks_x, pair_q, tile, weekly],
        [pltpu.VMEM((columns, size, scenarios), F32), pltpu.VMEM((weeks, size, scenarios), F32)],
        2 * annuals * unit,
        3_000_000,
    )
    forward = call(
        forward_kernel,
        "forward",
        [VMEM] * 5,
        [state_y],
        [],
        2 * rows * columns * unit,
        5_000_000,
    )

    def dual_step(more):
        sends = [pair] + [pair_q] * others + [tile, blocks_y] if more else []
        scratch = [pltpu.VMEM((streams_total, size, scenarios), BF16), pltpu.VMEM((rows, size, scenarios), F32)]
        return call(
            functools.partial(dual_kernel, refineries, more),
            "dual_step",
            [SMEM] * 3 + [VMEM] * (5 + others),
            [state_y] + sends,
            ([duals_scratch] if more else []) + scratch,
            2 * swings * unit,
            2_000_000,
        )

    def annual_step(more):
        return call(
            functools.partial(annual_kernel, more),
            "annual_step",
            [VMEM] * 3,
            [shape((size, scenarios), F32)] + ([weekly] if more else []),
            [],
            block,
            1_000_000,
        )

    upper_rows = upper.reshape(columns, size)
    demand_rows = demand.reshape(rows, size)
    need = annual_bound.reshape(1, size)
    primal, dual, annual = x_start, y_start, annual_start
    annual_send = jnp.broadcast_to(annual.astype(BF16)[None], (weeks, size, scenarios))
    own, *rest = first_duals(me, swing_rows, swing_src, swing_blocks, carry_blocks, dual)
    sends, carried, dual_q = rest[:others], rest[others], rest[others + 1]
    high, low, upper_full = dense(band_count, local_rows, local_cols, local_blocks, upper_rows)
    for iteration in range(ITERS):
        more = iteration + 1 < ITERS
        annual_q = lax.all_to_all(annual_send, "period", 0, 0, tiled=True)
        arrived = [shifted(send, "refinery", d) for d, send in enumerate(sends, 1)]
        carried_back = shifted(carried, "period", -1)
        (partial_x,) = adjoint(high, low, dual_q, primal, cost)
        updated, extrap, streams, last, image = primal_step(
            annual_ids, annual_cols, annual_blocks, annual_q, own, carried_back,
            partial_x, primal, upper_full, *arrived,
        )
        parts = lax.all_to_all(image, "period", 0, 0, tiled=True)
        others_streams = [shifted(streams, "refinery", d) for d in range(1, refineries)]
        previous = shifted(last, "period", 1)
        (partial_y,) = forward(high, low, extrap, dual, demand_rows)
        dual, *rest = dual_step(more)(
            me, swing_rows, swing_src, swing_blocks, carry_blocks,
            partial_y, previous, streams, *others_streams,
        )
        if more:
            own, sends, carried, dual_q = rest[0], rest[1:refineries], rest[refineries], rest[refineries + 1]
            annual, annual_send = annual_step(more)(annual, need, parts)
        else:
            (annual,) = annual_step(more)(annual, need, parts)
        primal = updated
    return primal, dual, annual


def solution(mesh):
    both = P(("period", "refinery"))
    wide = P(("period", "refinery"), None)
    cube = P(("period", "refinery"), None, None)
    return jax.shard_map(
        body,
        mesh=mesh,
        in_specs=(
            cube, both, both, both, cube, both, both, cube, cube, both, both,
            wide, both, both, both, wide, wide, wide,
        ),
        out_specs=(wide, wide, wide),
        check_vma=False,
    )
```

```python
import functools

import jax
import jax.numpy as jnp
from jax import lax
from jax.experimental import pallas as pl
from jax.experimental.pallas import tpu as pltpu
from jax.sharding import PartitionSpec as P

SC = 2
ITERS = 2

PRIMAL_STEP = 0.5
DUAL_STEP = 0.5
F32 = jnp.float32
BF16 = jnp.bfloat16
HBM = pl.BlockSpec(memory_space=pltpu.HBM)
SMEM = pl.BlockSpec(memory_space=pltpu.SMEM)


def shape(dims, dtype):
    return jax.ShapeDtypeStruct(dims, dtype)


class Arriving:
    def __init__(self, source, target, sems, at, pieces):
        length = source.shape[0] // pieces
        self.target = target
        self.copies = []
        for p in range(pieces):
            rows = pl.ds(p * length, length)
            self.copies.append(
                pltpu.make_async_copy(source.at[rows], target.at[rows], sems.at[at + p])
            )
        for copy in self.copies:
            copy.start()

    def piece(self):
        self.copies.pop(0).wait()
        return self.target

    def __call__(self):
        while self.copies:
            self.piece()
        return self.target


class Leaving:
    def __init__(self, source, target, sem):
        self.ref = source
        self.copy = pltpu.make_async_copy(source, target, sem)
        self.sent = False

    def send(self):
        self.copy.start()
        self.sent = True


def run(body, name, scalars, arrays, outs, scratch, flops, pieces={}):
    counts = [pieces.get(i, 1) for i in range(len(arrays))]
    ns, na, no = len(scalars), len(arrays), len(outs)

    def kernel(*refs):
        scalar_refs, refs = refs[:ns], refs[ns:]
        sources, refs = refs[:na], refs[na:]
        targets, refs = refs[:no], refs[no:]
        landing, refs = refs[:na], refs[na:]
        staging, refs = refs[:no], refs[no:]
        (in_sems, out_sems), extra = refs[:2], refs[2:]
        at = 0
        arriving = []
        for source, target, count in zip(sources, landing, counts):
            arriving.append(Arriving(source, target, in_sems, at, count))
            at += count
        leaving = [
            Leaving(source, target, out_sems.at[i])
            for i, (source, target) in enumerate(zip(staging, targets))
        ]
        body(scalar_refs, arriving, leaving, *extra)
        for item in arriving:
            item()
        for item in leaving:
            if not item.sent:
                item.send()
        for item in leaving:
            item.copy.wait()

    moved = sum(a.size * a.dtype.itemsize for a in (*arrays, *outs))
    return pl.pallas_call(
        kernel,
        name=name,
        in_specs=[SMEM] * ns + [HBM] * na,
        out_specs=(HBM,) * no,
        out_shape=tuple(outs),
        scratch_shapes=[pltpu.VMEM(a.shape, a.dtype) for a in (*arrays, *outs)]
        + [pltpu.SemaphoreType.DMA((sum(counts),)), pltpu.SemaphoreType.DMA((no,))]
        + scratch,
        compiler_params=pltpu.CompilerParams(vmem_limit_bytes=64 << 20),
        cost_estimate=pl.CostEstimate(flops=flops, bytes_accessed=moved, transcendentals=0),
    )(*scalars, *arrays)


def dot(a, b):
    return jnp.dot(a, b, preferred_element_type=F32)


def dot_transposed(a, b):
    return dot(a.T, b)


def column_of(row_vector, width):
    return jnp.broadcast_to(row_vector, (width, row_vector.shape[1])).T


def wrap(value, number):
    return jnp.where(value >= number, value - number, value)


def send_duals(refineries, dual_q, me, rows, src, swing, carry, outs, acc):
    own, *sends, carried = outs
    acc[...] = jnp.zeros_like(acc)
    carried.ref[...] = dot_transposed(carry[0], dual_q[0]).astype(BF16)
    carried.send()
    for m in range(swing.shape[0]):
        acc[src[m]] += dot_transposed(swing[m], dual_q[rows[m]])
    for d, send in enumerate(sends, 1):
        send.ref[...] = acc[pl.ds(wrap(me + d, refineries) * SC, SC)].astype(BF16)
        send.send()
    own.ref[...] = acc[pl.ds(me * SC, SC)]
    own.send()


def first_duals_body(refineries, scalars, ins, outs, acc):
    me, rows, src = scalars
    annual, dual, carry, swing = ins
    weekly, dual_q = outs[0], outs[1]
    rounded = annual()[...].astype(BF16)
    for w in range(weekly.ref.shape[0]):
        weekly.ref[w] = rounded
    weekly.send()
    size = rounded.shape[0]
    dual = dual()
    for i in range(dual_q.ref.shape[0]):
        dual_q.ref[i] = dual[i * size : (i + 1) * size].astype(BF16)
    dual_q.send()
    send_duals(refineries, dual_q.ref, me[0], rows, src, swing(), carry(), outs[2:], acc)


def adjoint(high, low, dual_q, primal, prices, out):
    blocks, size, _ = dual_q.shape
    turned = jnp.concatenate([dual_q[i].T for i in range(blocks)], axis=1)
    step = 2 * size
    for j in range(high.shape[1] // step):
        part = dot(turned, high[:, j * step : (j + 1) * step]) + dot(
            turned, low[:, j * step : (j + 1) * step]
        )
        for h in range(2):
            at = slice(j * step + h * size, j * step + (h + 1) * size)
            out[at] = primal[at] - PRIMAL_STEP * (
                prices[at] - part[:, h * size : (h + 1) * size].T
            )


def dense_body(chunks, scalars, ins, outs, acc):
    count, rows, cols = scalars
    blocks, upper, dual_q, primal, prices = ins
    high, low, upper_full, out = outs
    size = upper.target.shape[1]
    width = upper_full.ref.shape[1]
    tiles = high.ref.shape[1] // size
    acc[...] = jnp.zeros_like(acc)
    slots = blocks.target.shape[0] // chunks
    for c in range(chunks):
        here = blocks.piece()

        def step(n, _):
            acc[rows[n] * tiles + cols[n]] += here[n].astype(F32)
            return 0

        lax.fori_loop(c * slots, jnp.minimum(count[0], (c + 1) * slots), step, 0)
    for i in range(high.ref.shape[0] // size):
        for j in range(tiles):
            whole = acc[i * tiles + j]
            top = whole.astype(BF16)
            at = (slice(i * size, (i + 1) * size), slice(j * size, (j + 1) * size))
            high.ref[at] = top
            low.ref[at] = (whole - top.astype(F32)).astype(BF16)
    high.send()
    low.send()
    upper = upper()
    for j in range(tiles):
        upper_full.ref[j * size : (j + 1) * size] = column_of(upper[j : j + 1], width)
    upper_full.send()
    adjoint(high.ref, low.ref, dual_q(), primal(), prices(), out.ref)


def adjoint_body(scalars, ins, outs):
    dual_q, primal, prices, high, low = ins
    adjoint(high(), low(), dual_q(), primal(), prices(), outs[0].ref)


def primal_body(scalars, ins, outs, acc, image_acc):
    ids, cols = scalars
    annual_q, annual, own, carried, primal, upper_full, partial, *arrived = ins
    image, streams, last, extrap, updated = outs
    blocks, size, _ = extrap.ref.shape
    acc[...] = jnp.zeros_like(acc)
    image_acc[...] = jnp.zeros_like(image_acc)
    annual, annual_q = annual(), annual_q()
    slots = annual.shape[0]
    for k in range(slots):
        acc[cols[k]] += dot_transposed(annual[k], annual_q[ids[k]])
    total = own()[...]
    for piece in arrived:
        total = total + piece()[...].astype(F32)
    acc[:SC] += total
    acc[blocks - 1] += carried()[...].astype(F32)
    partial, primal, upper_full = partial(), primal(), upper_full()
    for j in range(blocks):
        at = slice(j * size, (j + 1) * size)
        new = jnp.clip(partial[at] + PRIMAL_STEP * acc[j], 0.0, upper_full[at])
        updated.ref[at] = new
        ahead = (2.0 * new - primal[at]).astype(BF16)
        extrap.ref[j] = ahead
        if j < SC:
            streams.ref[j] = ahead
        if j == SC - 1:
            streams.send()
        if j == blocks - 1:
            last.ref[...] = ahead
            last.send()
    extrap.send()
    updated.send()
    for k in range(slots):
        image_acc[ids[k]] += dot(annual[k], extrap.ref[cols[k]])
    image.ref[...] = image_acc[...].astype(BF16)


def forward_body(scalars, ins, outs):
    extrap, dual, demand, high, low = ins
    out = outs[0].ref
    extrap, dual, demand = extrap(), dual(), demand()
    blocks, size, width = extrap.shape
    right = jnp.concatenate([extrap[j] for j in range(blocks)], axis=0)
    high, low = high(), low()
    step = 2 * size
    for i in range(high.shape[0] // step):
        part = dot(high[i * step : (i + 1) * step], right) + dot(
            low[i * step : (i + 1) * step], right
        )
        for h in range(2):
            at = slice(i * step + h * size, i * step + (h + 1) * size)
            row = 2 * i + h
            out[at] = dual[at] + DUAL_STEP * (
                column_of(demand[row : row + 1], width) - part[h * size : (h + 1) * size]
            )


def dual_body(refineries, more, scalars, ins, outs, gathered, acc, *stream_acc):
    me, rows, src = scalars
    swing, carry, streams, partial, previous, *arrived = ins
    dual = outs[0]
    swing, carry = swing(), carry()
    size = swing.shape[1]
    mine = me[0]
    gathered[pl.ds(mine * SC, SC)] = streams()[...]
    for d, piece in enumerate(arrived, 1):
        gathered[pl.ds(wrap(mine + refineries - d, refineries) * SC, SC)] = piece()[...]
    acc[...] = jnp.zeros_like(acc)
    for m in range(swing.shape[0]):
        acc[rows[m]] += dot(swing[m], gathered[src[m]])
    acc[0] += dot(carry[0], previous()[...])
    partial = partial()
    for i in range(acc.shape[0]):
        at = slice(i * size, (i + 1) * size)
        new = jnp.maximum(partial[at] - DUAL_STEP * acc[i], 0.0)
        dual.ref[at] = new
        if more:
            outs[1].ref[i] = new.astype(BF16)
    dual.send()
    if more:
        outs[1].send()
        send_duals(
            refineries, outs[1].ref, mine, rows, src, swing, carry, outs[2:], *stream_acc
        )


def annual_body(more, scalars, ins, outs):
    annual, need, parts, *_ = ins
    parts = parts()
    total = parts[0].astype(F32)
    for w in range(1, parts.shape[0]):
        total = total + parts[w].astype(F32)
    annual = annual()
    new = jnp.maximum(
        annual[...] + DUAL_STEP * (column_of(need()[...], annual.shape[1]) - total), 0.0
    )
    outs[-1].ref[...] = new
    if more:
        rounded = new.astype(BF16)
        for w in range(parts.shape[0]):
            outs[0].ref[w] = rounded


def shifted(block, axis, distance):
    number = lax.axis_size(axis)
    route = [((i - distance) % number, i) for i in range(number)]
    return lax.ppermute(block, axis, route)


def body(
    local_blocks,
    local_rows,
    local_cols,
    band_count,
    swing_blocks,
    swing_rows,
    swing_src,
    carry_blocks,
    annual_blocks,
    annual_ids,
    annual_cols,
    cost,
    upper,
    demand,
    annual_bound,
    x_start,
    y_start,
    annual_start,
):
    scenarios = cost.shape[1]
    size = local_blocks.shape[1]
    columns = cost.shape[0] // size
    rows = y_start.shape[0] // size
    slots = local_blocks.shape[0]
    weeks = lax.axis_size("period")
    refineries = lax.axis_size("refinery")
    others = refineries - 1
    me = lax.axis_index("refinery").astype(jnp.int32).reshape(1)
    tile = shape((size, scenarios), BF16)
    pair_q = shape((SC, size, scenarios), BF16)
    pair = shape((SC, size, scenarios), F32)
    state_x = shape((columns * size, scenarios), F32)
    state_y = shape((rows * size, scenarios), F32)
    blocks_x = shape((columns, size, scenarios), BF16)
    blocks_y = shape((rows, size, scenarios), BF16)
    weekly = shape((weeks, size, scenarios), BF16)
    matrix = shape((rows * size, columns * size), BF16)
    swings = swing_blocks.shape[0]
    annuals = annual_blocks.shape[0]
    unit = 2 * size * size * scenarios
    stream_scratch = pltpu.VMEM((refineries * SC, size, scenarios), F32)
    sends_shape = [pair] + [pair_q] * others + [tile]
    chunks = 4 if slots % 4 == 0 else 1

    upper_rows = upper.reshape(columns, size)
    demand_rows = demand.reshape(rows, size)
    need = annual_bound.reshape(1, size)
    primal, dual, annual = x_start, y_start, annual_start
    annual_send, dual_q, own, *rest = run(
        functools.partial(first_duals_body, refineries),
        "first_duals",
        [me, swing_rows, swing_src],
        [annual, dual, carry_blocks, swing_blocks],
        [weekly, blocks_y] + sends_shape,
        [stream_scratch],
        (swings + 1) * unit,
    )
    for iteration in range(ITERS):
        more = iteration + 1 < ITERS
        sends, carried = rest[:others], rest[others]
        annual_q = lax.all_to_all(annual_send, "period", 0, 0, tiled=True)
        arrived = [shifted(send, "refinery", d) for d, send in enumerate(sends, 1)]
        carried_back = shifted(carried, "period", -1)
        if iteration == 0:
            high, low, upper_full, partial_x = run(
                functools.partial(dense_body, chunks),
                "dense",
                [band_count, local_rows, local_cols],
                [local_blocks, upper_rows, dual_q, primal, cost],
                [matrix, matrix, state_x, state_x],
                [pltpu.VMEM((rows * columns, size, size), F32)],
                3 * rows * columns * unit,
                {0: chunks},
            )
        else:
            (partial_x,) = run(
                adjoint_body,
                "adjoint",
                [],
                [dual_q, primal, cost, high, low],
                [state_x],
                [],
                2 * rows * columns * unit,
            )
        image, streams, last, extrap, updated = run(
            primal_body,
            "primal_step",
            [annual_ids, annual_cols],
            [annual_q, annual_blocks, own, carried_back, primal, upper_full, partial_x, *arrived],
            [weekly, pair_q, tile, blocks_x, state_x],
            [
                pltpu.VMEM((columns, size, scenarios), F32),
                pltpu.VMEM((weeks, size, scenarios), F32),
            ],
            2 * annuals * unit,
        )
        parts = lax.all_to_all(image, "period", 0, 0, tiled=True)
        others_streams = [shifted(streams, "refinery", d) for d in range(1, refineries)]
        previous = shifted(last, "period", 1)
        (partial_y,) = run(
            forward_body,
            "forward",
            [],
            [extrap, dual, demand_rows, high, low],
            [state_y],
            [],
            2 * rows * columns * unit,
        )
        dual, *rest = run(
            functools.partial(dual_body, refineries, more),
            "dual_step",
            [me, swing_rows, swing_src],
            [swing_blocks, carry_blocks, streams, partial_y, previous, *others_streams],
            [state_y] + ([blocks_y] + sends_shape if more else []),
            [
                pltpu.VMEM((refineries * SC, size, scenarios), BF16),
                pltpu.VMEM((rows, size, scenarios), F32),
            ]
            + ([stream_scratch] if more else []),
            2 * swings * unit,
        )
        if more:
            dual_q, own, *rest = rest
        *next_send, annual = run(
            functools.partial(annual_body, more),
            "annual_step",
            [],
            [annual, need, parts] + ([own] if more else []),
            ([weekly] if more else []) + [shape((size, scenarios), F32)],
            [],
            size * scenarios * weeks,
        )
        if more:
            (annual_send,) = next_send
        primal = updated
    return primal, dual, annual


def solution(mesh):
    both = P(("period", "refinery"))
    wide = P(("period", "refinery"), None)
    cube = P(("period", "refinery"), None, None)
    return jax.shard_map(
        body,
        mesh=mesh,
        in_specs=(
            cube, both, both, both, cube, both, both, cube, cube, both, both,
            wide, both, both, both, wide, wide, wide,
        ),
        out_specs=(wide, wide, wide),
        check_vma=False,
    )
```

```python
import functools

import jax
import jax.numpy as jnp
from jax import lax
from jax.experimental import pallas as pl
from jax.experimental.pallas import tpu as pltpu
from jax.sharding import PartitionSpec as P

SC = 2
ITERS = 2

PRIMAL_STEP = 0.5
DUAL_STEP = 0.5
F32 = jnp.float32
BF16 = jnp.bfloat16
HBM = pl.BlockSpec(memory_space=pltpu.HBM)
SMEM = pl.BlockSpec(memory_space=pltpu.SMEM)


def shape(dims, dtype):
    return jax.ShapeDtypeStruct(dims, dtype)


class Arriving:
    def __init__(self, source, target, sems, at, pieces, axis):
        length = source.shape[axis] // pieces
        self.target = target
        self.copies = []
        for p in range(pieces):
            part = (slice(None),) * axis + (pl.ds(p * length, length),)
            self.copies.append(
                pltpu.make_async_copy(source.at[part], target.at[part], sems.at[at + p])
            )

    def start(self, piece):
        if piece < len(self.copies):
            self.copies[piece].start()

    def piece(self):
        self.copies.pop(0).wait()
        return self.target

    def __call__(self):
        while self.copies:
            self.piece()
        return self.target


class Leaving:
    def __init__(self, source, target, sems, at, pieces):
        length = source.shape[0] // pieces
        self.ref = source
        self.waiting = []
        for p in range(pieces):
            part = pl.ds(p * length, length)
            self.waiting.append(
                pltpu.make_async_copy(source.at[part], target.at[part], sems.at[at + p])
            )
        self.flying = []

    def send(self):
        copy = self.waiting.pop(0)
        copy.start()
        self.flying.append(copy)

    def finish(self):
        for copy in self.flying:
            copy.wait()


def run(body, name, scalars, arrays, outs, scratch, flops, pieces={}, out_pieces={}):
    counts = [pieces.get(i, (1, 0)) for i in range(len(arrays))]
    out_counts = [out_pieces.get(i, 1) for i in range(len(outs))]
    ns, na, no = len(scalars), len(arrays), len(outs)
    most = max(count for count, _ in counts)

    def kernel(*refs):
        scalar_refs, refs = refs[:ns], refs[ns:]
        sources, refs = refs[:na], refs[na:]
        targets, refs = refs[:no], refs[no:]
        landing, refs = refs[:na], refs[na:]
        staging, refs = refs[:no], refs[no:]
        (in_sems, out_sems), extra = refs[:2], refs[2:]
        at = 0
        arriving = []
        for source, target, (count, axis) in zip(sources, landing, counts):
            arriving.append(Arriving(source, target, in_sems, at, count, axis))
            at += count
        for p in range(most):
            for item in arriving:
                item.start(p)
        at = 0
        leaving = []
        for source, target, count in zip(staging, targets, out_counts):
            leaving.append(Leaving(source, target, out_sems, at, count))
            at += count
        body(scalar_refs, arriving, leaving, *extra)
        for item in arriving:
            item()
        for item in leaving:
            while item.waiting:
                item.send()
        for item in leaving:
            item.finish()

    moved = sum(a.size * a.dtype.itemsize for a in (*arrays, *outs))
    return pl.pallas_call(
        kernel,
        name=name,
        in_specs=[SMEM] * ns + [HBM] * na,
        out_specs=(HBM,) * no,
        out_shape=tuple(outs),
        scratch_shapes=[pltpu.VMEM(a.shape, a.dtype) for a in (*arrays, *outs)]
        + [
            pltpu.SemaphoreType.DMA((sum(count for count, _ in counts),)),
            pltpu.SemaphoreType.DMA((sum(out_counts),)),
        ]
        + scratch,
        compiler_params=pltpu.CompilerParams(vmem_limit_bytes=64 << 20),
        cost_estimate=pl.CostEstimate(flops=flops, bytes_accessed=moved, transcendentals=0),
    )(*scalars, *arrays)


def dot(a, b):
    return jnp.dot(a, b, preferred_element_type=F32)


def dot_transposed(a, b):
    return dot(a.T, b)


def column_of(row_vector, width):
    return jnp.broadcast_to(row_vector, (width, row_vector.shape[1])).T


def partner(me, d, number, receive):
    if number & (number - 1) == 0:
        return me ^ d
    other = me + (number - d if receive else d)
    return jnp.where(other >= number, other - number, other)


def send_duals(refineries, dual_q, me, rows, src, swing, carry, outs, acc):
    own, *sends, carried = outs
    acc[...] = jnp.zeros_like(acc)
    carried.ref[...] = dot_transposed(carry[0], dual_q[0]).astype(BF16)
    carried.send()
    for m in range(swing.shape[0]):
        acc[src[m]] += dot_transposed(swing[m], dual_q[rows[m]])
    for d, send in enumerate(sends, 1):
        send.ref[...] = acc[pl.ds(partner(me, d, refineries, False) * SC, SC)].astype(BF16)
        send.send()
    own.ref[...] = acc[pl.ds(me * SC, SC)]
    own.send()


def first_duals_body(refineries, scalars, ins, outs, acc):
    me, rows, src = scalars
    annual, dual, carry, swing = ins
    weekly, dual_q = outs[0], outs[1]
    rounded = annual()[...].astype(BF16)
    for w in range(weekly.ref.shape[0]):
        weekly.ref[w] = rounded
    weekly.send()
    size = rounded.shape[0]
    dual = dual()
    for i in range(dual_q.ref.shape[0]):
        dual_q.ref[i] = dual[i * size : (i + 1) * size].astype(BF16)
    dual_q.send()
    send_duals(refineries, dual_q.ref, me[0], rows, src, swing(), carry(), outs[2:], acc)


def adjoint(high, low, dual_q, primal, prices, out, chunks):
    blocks, size, _ = dual_q.shape
    turned = jnp.concatenate([dual_q[i].T for i in range(blocks)], axis=1)
    step = out.ref.shape[0] // chunks
    for j in range(chunks):
        columns = slice(j * step, (j + 1) * step)
        part = dot(turned, high()[:, columns]) + dot(turned, low()[:, columns])
        if j == 0:
            primal, prices = primal(), prices()
        for h in range(step // size):
            at = slice(j * step + h * size, j * step + (h + 1) * size)
            out.ref[at] = primal[at] - PRIMAL_STEP * (
                prices[at] - part[:, h * size : (h + 1) * size].T
            )
        out.send()


def dense_body(chunks, scalars, ins, outs, acc):
    count, rows, cols = scalars
    blocks, upper, dual_q, primal, prices = ins
    high, low, upper_full, out = outs
    size = upper.target.shape[1]
    width = upper_full.ref.shape[1]
    tiles = high.ref.shape[1] // size
    acc[...] = jnp.zeros_like(acc)
    slots = blocks.target.shape[0] // chunks
    for c in range(chunks):
        here = blocks.piece()

        def step(n, _):
            acc[rows[n] * tiles + cols[n]] += here[n].astype(F32)
            return 0

        lax.fori_loop(c * slots, jnp.minimum(count[0], (c + 1) * slots), step, 0)
    for i in range(high.ref.shape[0] // size):
        for j in range(tiles):
            whole = acc[i * tiles + j]
            top = whole.astype(BF16)
            at = (slice(i * size, (i + 1) * size), slice(j * size, (j + 1) * size))
            high.ref[at] = top
            low.ref[at] = (whole - top.astype(F32)).astype(BF16)
    high.send()
    low.send()
    upper = upper()
    for j in range(tiles):
        upper_full.ref[j * size : (j + 1) * size] = column_of(upper[j : j + 1], width)
    upper_full.send()
    adjoint(lambda: high.ref, lambda: low.ref, dual_q(), primal, prices, out, chunks)


def adjoint_body(chunks, scalars, ins, outs):
    dual_q, high, low, primal, prices = ins
    adjoint(high.piece, low.piece, dual_q(), primal, prices, outs[0], chunks)


def primal_body(scalars, ins, outs, acc, image_acc):
    ids, cols = scalars
    annual_q, annual, own, carried, primal, upper_full, partial, *arrived = ins
    image, streams, last, extrap, updated = outs
    blocks, size, _ = extrap.ref.shape
    acc[...] = jnp.zeros_like(acc)
    image_acc[...] = jnp.zeros_like(image_acc)
    annual, annual_q = annual(), annual_q()
    slots = annual.shape[0]
    for k in range(slots):
        acc[cols[k]] += dot_transposed(annual[k], annual_q[ids[k]])
    total = own()[...]
    for piece in arrived:
        total = total + piece()[...].astype(F32)
    acc[:SC] += total
    acc[blocks - 1] += carried()[...].astype(F32)
    partial, primal, upper_full = partial(), primal(), upper_full()
    for j in range(blocks):
        at = slice(j * size, (j + 1) * size)
        new = jnp.clip(partial[at] + PRIMAL_STEP * acc[j], 0.0, upper_full[at])
        updated.ref[at] = new
        ahead = (2.0 * new - primal[at]).astype(BF16)
        extrap.ref[j] = ahead
        if j < SC:
            streams.ref[j] = ahead
        if j == SC - 1:
            streams.send()
        if j == blocks - 1:
            last.ref[...] = ahead
            last.send()
    extrap.send()
    updated.send()
    for k in range(slots):
        image_acc[ids[k]] += dot(annual[k], extrap.ref[cols[k]])
    image.ref[...] = image_acc[...].astype(BF16)


def forward_body(chunks, scalars, ins, outs):
    extrap, high, low, dual, demand = ins
    out = outs[0]
    extrap = extrap()
    blocks, size, width = extrap.shape
    right = jnp.concatenate([extrap[j] for j in range(blocks)], axis=0)
    step = out.ref.shape[0] // chunks
    for i in range(chunks):
        lines = slice(i * step, (i + 1) * step)
        part = dot(high.piece()[lines], right) + dot(low.piece()[lines], right)
        if i == 0:
            dual, demand = dual(), demand()
        for h in range(step // size):
            at = slice(i * step + h * size, i * step + (h + 1) * size)
            row = i * (step // size) + h
            out.ref[at] = dual[at] + DUAL_STEP * (
                column_of(demand[row : row + 1], width) - part[h * size : (h + 1) * size]
            )
        out.send()


def dual_body(refineries, more, scalars, ins, outs, gathered, acc, *stream_acc):
    me, rows, src = scalars
    swing, carry, streams, partial, previous, parts, annual, need, *arrived = ins
    dual, annual_out = outs[0], outs[1]
    swing, carry = swing(), carry()
    size = swing.shape[1]
    mine = me[0]
    gathered[pl.ds(mine * SC, SC)] = streams()[...]
    for d, piece in enumerate(arrived, 1):
        gathered[pl.ds(partner(mine, d, refineries, True) * SC, SC)] = piece()[...]
    acc[...] = jnp.zeros_like(acc)
    for m in range(swing.shape[0]):
        acc[rows[m]] += dot(swing[m], gathered[src[m]])
    acc[0] += dot(carry[0], previous()[...])
    parts, annual = parts(), annual()
    total = parts[0].astype(F32)
    for w in range(1, parts.shape[0]):
        total = total + parts[w].astype(F32)
    new_annual = jnp.maximum(
        annual[...] + DUAL_STEP * (column_of(need()[...], annual.shape[1]) - total), 0.0
    )
    annual_out.ref[...] = new_annual
    annual_out.send()
    if more:
        rounded = new_annual.astype(BF16)
        for w in range(parts.shape[0]):
            outs[2].ref[w] = rounded
        outs[2].send()
    partial = partial()
    for i in range(acc.shape[0]):
        at = slice(i * size, (i + 1) * size)
        new = jnp.maximum(partial[at] - DUAL_STEP * acc[i], 0.0)
        dual.ref[at] = new
        if more:
            outs[3].ref[i] = new.astype(BF16)
    dual.send()
    if more:
        outs[3].send()
        send_duals(
            refineries, outs[3].ref, mine, rows, src, swing, carry, outs[4:], *stream_acc
        )


def shifted(block, axis, distance):
    number = lax.axis_size(axis)
    route = [((i - distance) % number, i) for i in range(number)]
    return lax.ppermute(block, axis, route)


def exchanged(block, axis, d):
    number = lax.axis_size(axis)
    if number & (number - 1) == 0:
        return lax.ppermute(block, axis, [(i, i ^ d) for i in range(number)])
    return shifted(block, axis, d)


def body(
    local_blocks,
    local_rows,
    local_cols,
    band_count,
    swing_blocks,
    swing_rows,
    swing_src,
    carry_blocks,
    annual_blocks,
    annual_ids,
    annual_cols,
    cost,
    upper,
    demand,
    annual_bound,
    x_start,
    y_start,
    annual_start,
):
    scenarios = cost.shape[1]
    size = local_blocks.shape[1]
    columns = cost.shape[0] // size
    rows = y_start.shape[0] // size
    slots = local_blocks.shape[0]
    weeks = lax.axis_size("period")
    refineries = lax.axis_size("refinery")
    others = refineries - 1
    me = lax.axis_index("refinery").astype(jnp.int32).reshape(1)
    tile = shape((size, scenarios), BF16)
    pair_q = shape((SC, size, scenarios), BF16)
    pair = shape((SC, size, scenarios), F32)
    state_x = shape((columns * size, scenarios), F32)
    state_y = shape((rows * size, scenarios), F32)
    blocks_x = shape((columns, size, scenarios), BF16)
    blocks_y = shape((rows, size, scenarios), BF16)
    weekly = shape((weeks, size, scenarios), BF16)
    matrix = shape((rows * size, columns * size), BF16)
    swings = swing_blocks.shape[0]
    annuals = annual_blocks.shape[0]
    unit = 2 * size * size * scenarios
    stream_scratch = pltpu.VMEM((refineries * SC, size, scenarios), F32)
    sends_shape = [pair] + [pair_q] * others + [tile]
    chunks = 4 if slots % 4 == 0 and columns % 4 == 0 else 1
    parts_x = 4 if columns % 4 == 0 else 1
    parts_y = 4 if rows % 4 == 0 else 1

    upper_rows = upper.reshape(columns, size)
    demand_rows = demand.reshape(rows, size)
    need = annual_bound.reshape(1, size)
    primal, dual, annual = x_start, y_start, annual_start
    annual_send, dual_q, own, *rest = run(
        functools.partial(first_duals_body, refineries),
        "first_duals",
        [me, swing_rows, swing_src],
        [annual, dual, carry_blocks, swing_blocks],
        [weekly, blocks_y] + sends_shape,
        [stream_scratch],
        (swings + 1) * unit,
    )
    for iteration in range(ITERS):
        more = iteration + 1 < ITERS
        sends, carried = rest[:others], rest[others]
        annual_q = lax.all_to_all(annual_send, "period", 0, 0, tiled=True)
        arrived = [exchanged(send, "refinery", d) for d, send in enumerate(sends, 1)]
        carried_back = shifted(carried, "period", -1)
        if iteration == 0:
            high, low, upper_full, partial_x = run(
                functools.partial(dense_body, chunks),
                "dense",
                [band_count, local_rows, local_cols],
                [local_blocks, upper_rows, dual_q, primal, cost],
                [matrix, matrix, state_x, state_x],
                [pltpu.VMEM((rows * columns, size, size), F32)],
                3 * rows * columns * unit,
                {0: (chunks, 0)},
                {3: chunks},
            )
        else:
            (partial_x,) = run(
                functools.partial(adjoint_body, parts_x),
                "adjoint",
                [],
                [dual_q, high, low, primal, cost],
                [state_x],
                [],
                2 * rows * columns * unit,
                {1: (parts_x, 1), 2: (parts_x, 1)},
                {0: parts_x},
            )
        image, streams, last, extrap, updated = run(
            primal_body,
            "primal_step",
            [annual_ids, annual_cols],
            [annual_q, annual_blocks, own, carried_back, primal, upper_full, partial_x, *arrived],
            [weekly, pair_q, tile, blocks_x, state_x],
            [
                pltpu.VMEM((columns, size, scenarios), F32),
                pltpu.VMEM((weeks, size, scenarios), F32),
            ],
            2 * annuals * unit,
        )
        parts = lax.all_to_all(image, "period", 0, 0, tiled=True)
        others_streams = [exchanged(streams, "refinery", d) for d in range(1, refineries)]
        previous = shifted(last, "period", 1)
        (partial_y,) = run(
            functools.partial(forward_body, parts_y),
            "forward",
            [],
            [extrap, high, low, dual, demand_rows],
            [state_y],
            [],
            2 * rows * columns * unit,
            {1: (parts_y, 0), 2: (parts_y, 0)},
            {0: parts_y},
        )
        sent = [weekly, blocks_y] + sends_shape if more else []
        dual, annual, *rest = run(
            functools.partial(dual_body, refineries, more),
            "dual_step",
            [me, swing_rows, swing_src],
            [
                swing_blocks, carry_blocks, streams, partial_y, previous, parts, annual, need,
                *others_streams,
            ],
            [state_y, shape((size, scenarios), F32)] + sent,
            [
                pltpu.VMEM((refineries * SC, size, scenarios), BF16),
                pltpu.VMEM((rows, size, scenarios), F32),
            ]
            + ([stream_scratch] if more else []),
            2 * swings * unit,
        )
        if more:
            annual_send, dual_q, own, *rest = rest
        primal = updated
    return primal, dual, annual


def solution(mesh):
    both = P(("period", "refinery"))
    wide = P(("period", "refinery"), None)
    cube = P(("period", "refinery"), None, None)
    return jax.shard_map(
        body,
        mesh=mesh,
        in_specs=(
            cube, both, both, both, cube, both, both, cube, cube, both, both,
            wide, both, both, both, wide, wide, wide,
        ),
        out_specs=(wide, wide, wide),
        check_vma=False,
    )
```

```python
import functools

import jax
import jax.numpy as jnp
from jax import lax
from jax.experimental import pallas as pl
from jax.experimental.pallas import tpu as pltpu
from jax.sharding import PartitionSpec as P

SC = 2
ITERS = 2

PRIMAL_STEP = 0.5
DUAL_STEP = 0.5
F32 = jnp.float32
BF16 = jnp.bfloat16
HBM = pl.BlockSpec(memory_space=pltpu.HBM)
SMEM = pl.BlockSpec(memory_space=pltpu.SMEM)


def shape(dims, dtype):
    return jax.ShapeDtypeStruct(dims, dtype)


class Arriving:
    def __init__(self, source, target, sems, at, pieces, axis):
        length = source.shape[axis] // pieces
        self.target = target
        self.copies = []
        for p in range(pieces):
            part = (slice(None),) * axis + (pl.ds(p * length, length),)
            self.copies.append(
                pltpu.make_async_copy(source.at[part], target.at[part], sems.at[at + p])
            )

    def start(self):
        for copy in self.copies:
            copy.start()

    def piece(self):
        self.copies.pop(0).wait()
        return self.target

    def __call__(self):
        while self.copies:
            self.piece()
        return self.target


class Leaving:
    def __init__(self, source, target, sems, at, pieces):
        length = source.shape[0] // pieces
        self.ref = source
        self.waiting = []
        for p in range(pieces):
            part = pl.ds(p * length, length)
            self.waiting.append(
                pltpu.make_async_copy(source.at[part], target.at[part], sems.at[at + p])
            )
        self.flying = []

    def send(self):
        copy = self.waiting.pop(0)
        copy.start()
        self.flying.append(copy)

    def finish(self):
        for copy in self.flying:
            copy.wait()


def run(body, name, scalars, arrays, outs, scratch, flops, pieces={}, out_pieces={}):
    counts = [pieces.get(i, (1, 0)) for i in range(len(arrays))]
    out_counts = [out_pieces.get(i, 1) for i in range(len(outs))]
    ns, na, no = len(scalars), len(arrays), len(outs)

    def kernel(*refs):
        scalar_refs, refs = refs[:ns], refs[ns:]
        sources, refs = refs[:na], refs[na:]
        targets, refs = refs[:no], refs[no:]
        landing, refs = refs[:na], refs[na:]
        staging, refs = refs[:no], refs[no:]
        (in_sems, out_sems), extra = refs[:2], refs[2:]
        at = 0
        arriving = []
        for source, target, (count, axis) in zip(sources, landing, counts):
            arriving.append(Arriving(source, target, in_sems, at, count, axis))
            at += count
        for item in arriving:
            item.start()
        at = 0
        leaving = []
        for source, target, count in zip(staging, targets, out_counts):
            leaving.append(Leaving(source, target, out_sems, at, count))
            at += count
        body(scalar_refs, arriving, leaving, *extra)
        for item in arriving:
            item()
        for item in leaving:
            while item.waiting:
                item.send()
        for item in leaving:
            item.finish()

    moved = sum(a.size * a.dtype.itemsize for a in (*arrays, *outs))
    return pl.pallas_call(
        kernel,
        name=name,
        in_specs=[SMEM] * ns + [HBM] * na,
        out_specs=(HBM,) * no,
        out_shape=tuple(outs),
        scratch_shapes=[pltpu.VMEM(a.shape, a.dtype) for a in (*arrays, *outs)]
        + [
            pltpu.SemaphoreType.DMA((sum(count for count, _ in counts),)),
            pltpu.SemaphoreType.DMA((sum(out_counts),)),
        ]
        + scratch,
        compiler_params=pltpu.CompilerParams(vmem_limit_bytes=64 << 20),
        cost_estimate=pl.CostEstimate(flops=flops, bytes_accessed=moved, transcendentals=0),
    )(*scalars, *arrays)


def dot(a, b):
    return jnp.dot(a, b, preferred_element_type=F32)


def dot_transposed(a, b):
    return dot(a.T, b)


def column_of(row_vector, width):
    return jnp.broadcast_to(row_vector, (width, row_vector.shape[1])).T


def partner(me, d, number, receive):
    if number & (number - 1) == 0:
        return me ^ d
    other = me + (number - d if receive else d)
    return jnp.where(other >= number, other - number, other)


def send_duals(refineries, dual_q, me, rows, src, swing, carry, outs, acc, product):
    own, *sends, carried = outs
    acc[...] = jnp.zeros_like(acc)
    carried.ref[...] = dot_transposed(carry[0], dual_q[0]).astype(BF16)
    carried.send()
    for m in range(swing.shape[0]):
        product[m] = dot_transposed(swing[m], dual_q[rows[m]])
    for m in range(swing.shape[0]):
        acc[src[m]] += product[m]
    for d, send in enumerate(sends, 1):
        send.ref[...] = acc[pl.ds(partner(me, d, refineries, False) * SC, SC)].astype(BF16)
        send.send()
    own.ref[...] = acc[pl.ds(me * SC, SC)]
    own.send()


def first_duals_body(refineries, scalars, ins, outs, acc, product, dual_q):
    me, rows, src = scalars
    annual, dual, carry, swing = ins
    weekly = outs[0]
    rounded = annual()[...].astype(BF16)
    for w in range(weekly.ref.shape[0]):
        weekly.ref[w] = rounded
    weekly.send()
    size = rounded.shape[0]
    dual = dual()
    for i in range(dual_q.shape[0]):
        dual_q[i] = dual[i * size : (i + 1) * size].astype(BF16)
    send_duals(
        refineries, dual_q, me[0], rows, src, swing(), carry(), outs[1:], acc, product
    )


def adjoint(matrix, turned, size, primal, prices, out, chunks):
    step = out.ref.shape[0] // chunks
    for j in range(chunks):
        columns = slice(j * step, (j + 1) * step)
        part = dot(turned, matrix()[:, columns])
        if j == 0:
            primal, prices = primal(), prices()
        for h in range(step // size):
            at = slice(j * step + h * size, j * step + (h + 1) * size)
            out.ref[at] = primal[at] - PRIMAL_STEP * (
                prices[at] - part[:, h * size : (h + 1) * size].T
            )
        out.send()


def dense_body(chunks, scalars, ins, outs, acc):
    count, rows, cols = scalars
    blocks, upper, dual, primal, prices = ins
    matrix, upper_full, out = outs
    size = upper.target.shape[1]
    width = upper_full.ref.shape[1]
    tiles = matrix.ref.shape[1] // size
    acc[...] = jnp.zeros_like(acc)
    slots = blocks.target.shape[0] // chunks
    for c in range(chunks):
        here = blocks.piece()

        def step(n, _):
            acc[rows[n] * tiles + cols[n]] += here[n].astype(F32)
            return 0

        lax.fori_loop(c * slots, jnp.minimum(count[0], (c + 1) * slots), step, 0)
    for i in range(matrix.ref.shape[0] // size):
        for j in range(tiles):
            at = (slice(i * size, (i + 1) * size), slice(j * size, (j + 1) * size))
            matrix.ref[at] = acc[i * tiles + j].astype(BF16)
    matrix.send()
    upper = upper()
    for j in range(tiles):
        upper_full.ref[j * size : (j + 1) * size] = column_of(upper[j : j + 1], width)
    upper_full.send()
    dual = dual()
    turned = jnp.concatenate(
        [dual[i * size : (i + 1) * size].astype(BF16).T for i in range(dual.shape[0] // size)], axis=1
    )
    adjoint(lambda: matrix.ref, turned, size, primal, prices, out, chunks)


def adjoint_body(chunks, scalars, ins, outs):
    dual_q, matrix, primal, prices = ins
    dual_q = dual_q()
    blocks, size, _ = dual_q.shape
    turned = jnp.concatenate([dual_q[i].T for i in range(blocks)], axis=1)
    adjoint(matrix.piece, turned, size, primal, prices, outs[0], chunks)


def primal_body(scalars, ins, outs, acc, image_acc, product):
    ids, cols = scalars
    annual_q, annual, own, carried, primal, upper_full, partial, *arrived = ins
    image, streams, last, extrap, updated = outs
    blocks, size, _ = extrap.ref.shape
    acc[...] = jnp.zeros_like(acc)
    image_acc[...] = jnp.zeros_like(image_acc)
    annual, annual_q = annual(), annual_q()
    slots = annual.shape[0]
    for k in range(slots):
        product[k] = dot_transposed(annual[k], annual_q[ids[k]])
    for k in range(slots):
        acc[cols[k]] += product[k]
    total = own()[...]
    for piece in arrived:
        total = total + piece()[...].astype(F32)
    acc[:SC] += total
    acc[blocks - 1] += carried()[...].astype(F32)
    partial, primal, upper_full = partial(), primal(), upper_full()
    for j in range(blocks):
        at = slice(j * size, (j + 1) * size)
        new = jnp.clip(partial[at] + PRIMAL_STEP * acc[j], 0.0, upper_full[at])
        updated.ref[at] = new
        ahead = (2.0 * new - primal[at]).astype(BF16)
        extrap.ref[j] = ahead
        if j < SC:
            streams.ref[j] = ahead
        if j == SC - 1:
            streams.send()
        if j == blocks - 1:
            last.ref[...] = ahead
            last.send()
    extrap.send()
    updated.send()
    for k in range(slots):
        product[k] = dot(annual[k], extrap.ref[cols[k]])
    for k in range(slots):
        image_acc[ids[k]] += product[k]
    image.ref[...] = image_acc[...].astype(BF16)


def forward_body(chunks, scalars, ins, outs):
    extrap, matrix, dual, demand = ins
    out = outs[0]
    extrap = extrap()
    blocks, size, width = extrap.shape
    right = jnp.concatenate([extrap[j] for j in range(blocks)], axis=0)
    step = out.ref.shape[0] // chunks
    for i in range(chunks):
        lines = slice(i * step, (i + 1) * step)
        part = dot(matrix.piece()[lines], right)
        if i == 0:
            dual, demand = dual(), demand()
        for h in range(step // size):
            at = slice(i * step + h * size, i * step + (h + 1) * size)
            row = i * (step // size) + h
            out.ref[at] = dual[at] + DUAL_STEP * (
                column_of(demand[row : row + 1], width) - part[h * size : (h + 1) * size]
            )
        out.send()


def dual_body(refineries, more, scalars, ins, outs, gathered, acc, product, *stream_acc):
    me, rows, src = scalars
    swing, carry, streams, partial, previous, parts, annual, need, *arrived = ins
    dual, annual_out = outs[0], outs[1]
    swing, carry = swing(), carry()
    size = swing.shape[1]
    mine = me[0]
    gathered[pl.ds(mine * SC, SC)] = streams()[...]
    for d, piece in enumerate(arrived, 1):
        gathered[pl.ds(partner(mine, d, refineries, True) * SC, SC)] = piece()[...]
    acc[...] = jnp.zeros_like(acc)
    for m in range(swing.shape[0]):
        product[m] = dot(swing[m], gathered[src[m]])
    for m in range(swing.shape[0]):
        acc[rows[m]] += product[m]
    acc[0] += dot(carry[0], previous()[...])
    parts, annual = parts(), annual()
    total = parts[0].astype(F32)
    for w in range(1, parts.shape[0]):
        total = total + parts[w].astype(F32)
    new_annual = jnp.maximum(
        annual[...] + DUAL_STEP * (column_of(need()[...], annual.shape[1]) - total), 0.0
    )
    annual_out.ref[...] = new_annual
    annual_out.send()
    if more:
        rounded = new_annual.astype(BF16)
        for w in range(parts.shape[0]):
            outs[2].ref[w] = rounded
        outs[2].send()
    partial = partial()
    for i in range(acc.shape[0]):
        at = slice(i * size, (i + 1) * size)
        new = jnp.maximum(partial[at] - DUAL_STEP * acc[i], 0.0)
        dual.ref[at] = new
        if more:
            outs[3].ref[i] = new.astype(BF16)
    dual.send()
    if more:
        outs[3].send()
        send_duals(
            refineries, outs[3].ref, mine, rows, src, swing, carry, outs[4:], *stream_acc, product
        )


def shifted(block, axis, distance):
    number = lax.axis_size(axis)
    route = [((i - distance) % number, i) for i in range(number)]
    return lax.ppermute(block, axis, route)


def exchanged(block, axis, d):
    number = lax.axis_size(axis)
    if number & (number - 1) == 0:
        return lax.ppermute(block, axis, [(i, i ^ d) for i in range(number)])
    return shifted(block, axis, d)


def body(
    local_blocks,
    local_rows,
    local_cols,
    band_count,
    swing_blocks,
    swing_rows,
    swing_src,
    carry_blocks,
    annual_blocks,
    annual_ids,
    annual_cols,
    cost,
    upper,
    demand,
    annual_bound,
    x_start,
    y_start,
    annual_start,
):
    scenarios = cost.shape[1]
    size = local_blocks.shape[1]
    columns = cost.shape[0] // size
    rows = y_start.shape[0] // size
    slots = local_blocks.shape[0]
    weeks = lax.axis_size("period")
    refineries = lax.axis_size("refinery")
    others = refineries - 1
    me = lax.axis_index("refinery").astype(jnp.int32).reshape(1)
    tile = shape((size, scenarios), BF16)
    pair_q = shape((SC, size, scenarios), BF16)
    pair = shape((SC, size, scenarios), F32)
    state_x = shape((columns * size, scenarios), F32)
    state_y = shape((rows * size, scenarios), F32)
    blocks_x = shape((columns, size, scenarios), BF16)
    blocks_y = shape((rows, size, scenarios), BF16)
    weekly = shape((weeks, size, scenarios), BF16)
    matrix = shape((rows * size, columns * size), BF16)
    swings = swing_blocks.shape[0]
    annuals = annual_blocks.shape[0]
    unit = 2 * size * size * scenarios
    stream_scratch = pltpu.VMEM((refineries * SC, size, scenarios), F32)
    swing_scratch = pltpu.VMEM((swings, size, scenarios), F32)
    annual_scratch = pltpu.VMEM((annuals, size, scenarios), F32)
    sends_shape = [pair] + [pair_q] * others + [tile]
    chunks = 4 if slots % 4 == 0 and columns % 4 == 0 else 1
    parts_x = 4 if columns % 4 == 0 else 1
    parts_y = 4 if rows % 4 == 0 else 1

    upper_rows = upper.reshape(columns, size)
    demand_rows = demand.reshape(rows, size)
    need = annual_bound.reshape(1, size)
    primal, dual, annual = x_start, y_start, annual_start
    annual_send, own, *rest = run(
        functools.partial(first_duals_body, refineries),
        "first_duals",
        [me, swing_rows, swing_src],
        [annual, dual, carry_blocks, swing_blocks],
        [weekly] + sends_shape,
        [stream_scratch, swing_scratch, pltpu.VMEM(blocks_y.shape, BF16)],
        (swings + 1) * unit,
    )
    for iteration in range(ITERS):
        more = iteration + 1 < ITERS
        sends, carried = rest[:others], rest[others]
        annual_q = lax.all_to_all(annual_send, "period", 0, 0, tiled=True)
        carried_back = shifted(carried, "period", -1)
        arrived = [exchanged(send, "refinery", d) for d, send in enumerate(sends, 1)]
        if iteration == 0:
            matrix_q, upper_full, partial_x = run(
                functools.partial(dense_body, chunks),
                "dense",
                [band_count, local_rows, local_cols],
                [local_blocks, upper_rows, dual, primal, cost],
                [matrix, state_x, state_x],
                [pltpu.VMEM((rows * columns, size, size), F32)],
                3 * rows * columns * unit,
                {0: (chunks, 0)},
                {2: chunks},
            )
        else:
            (partial_x,) = run(
                functools.partial(adjoint_body, parts_x),
                "adjoint",
                [],
                [dual_q, matrix_q, primal, cost],
                [state_x],
                [],
                2 * rows * columns * unit,
                {1: (parts_x, 1)},
                {0: parts_x},
            )
        image, streams, last, extrap, updated = run(
            primal_body,
            "primal_step",
            [annual_ids, annual_cols],
            [annual_q, annual_blocks, own, carried_back, primal, upper_full, partial_x, *arrived],
            [weekly, pair_q, tile, blocks_x, state_x],
            [
                pltpu.VMEM((columns, size, scenarios), F32),
                pltpu.VMEM((weeks, size, scenarios), F32),
                annual_scratch,
            ],
            2 * annuals * unit,
        )
        parts = lax.all_to_all(image, "period", 0, 0, tiled=True)
        previous = shifted(last, "period", 1)
        others_streams = [exchanged(streams, "refinery", d) for d in range(1, refineries)]
        (partial_y,) = run(
            functools.partial(forward_body, parts_y),
            "forward",
            [],
            [extrap, matrix_q, dual, demand_rows],
            [state_y],
            [],
            2 * rows * columns * unit,
            {1: (parts_y, 0)},
            {0: parts_y},
        )
        sent = [weekly, blocks_y] + sends_shape if more else []
        dual, annual, *rest = run(
            functools.partial(dual_body, refineries, more),
            "dual_step",
            [me, swing_rows, swing_src],
            [
                swing_blocks, carry_blocks, streams, partial_y, previous, parts, annual, need,
                *others_streams,
            ],
            [state_y, shape((size, scenarios), F32)] + sent,
            [
                pltpu.VMEM((refineries * SC, size, scenarios), BF16),
                pltpu.VMEM((rows, size, scenarios), F32),
                swing_scratch,
            ]
            + ([stream_scratch] if more else []),
            2 * swings * unit,
        )
        if more:
            annual_send, dual_q, own, *rest = rest
        primal = updated
    return primal, dual, annual


def solution(mesh):
    both = P(("period", "refinery"))
    wide = P(("period", "refinery"), None)
    cube = P(("period", "refinery"), None, None)
    return jax.shard_map(
        body,
        mesh=mesh,
        in_specs=(
            cube, both, both, both, cube, both, both, cube, cube, both, both,
            wide, both, both, both, wide, wide, wide,
        ),
        out_specs=(wide, wide, wide),
        check_vma=False,
    )
```

```python
import functools

import jax
import jax.numpy as jnp
from jax import lax
from jax.experimental import pallas as pl
from jax.experimental.pallas import tpu as pltpu
from jax.sharding import PartitionSpec as P

SC = 2
ITERS = 2

PRIMAL_STEP = 0.5
DUAL_STEP = 0.5
F32 = jnp.float32
BF16 = jnp.bfloat16
HBM = pl.BlockSpec(memory_space=pltpu.HBM)
SMEM = pl.BlockSpec(memory_space=pltpu.SMEM)


def shape(dims, dtype):
    return jax.ShapeDtypeStruct(dims, dtype)


class Arriving:
    def __init__(self, source, target, sems, at, pieces, axis):
        length = source.shape[axis] // pieces
        self.target = target
        self.copies = []
        for p in range(pieces):
            part = (slice(None),) * axis + (pl.ds(p * length, length),)
            self.copies.append(
                pltpu.make_async_copy(source.at[part], target.at[part], sems.at[at + p])
            )

    def start(self):
        for copy in self.copies:
            copy.start()

    def piece(self):
        self.copies.pop(0).wait()
        return self.target

    def __call__(self):
        while self.copies:
            self.piece()
        return self.target


class Leaving:
    def __init__(self, source, target, sems, at, pieces):
        length = source.shape[0] // pieces
        self.ref = source
        self.waiting = []
        for p in range(pieces):
            part = pl.ds(p * length, length)
            self.waiting.append(
                pltpu.make_async_copy(source.at[part], target.at[part], sems.at[at + p])
            )
        self.flying = []

    def send(self):
        copy = self.waiting.pop(0)
        copy.start()
        self.flying.append(copy)

    def finish(self):
        for copy in self.flying:
            copy.wait()


def run(body, name, scalars, arrays, outs, scratch, flops, pieces={}, out_pieces={}):
    counts = [pieces.get(i, (1, 0)) for i in range(len(arrays))]
    out_counts = [out_pieces.get(i, 1) for i in range(len(outs))]
    ns, na, no = len(scalars), len(arrays), len(outs)

    def kernel(*refs):
        scalar_refs, refs = refs[:ns], refs[ns:]
        sources, refs = refs[:na], refs[na:]
        targets, refs = refs[:no], refs[no:]
        landing, refs = refs[:na], refs[na:]
        staging, refs = refs[:no], refs[no:]
        (in_sems, out_sems), extra = refs[:2], refs[2:]
        at = 0
        arriving = []
        for source, target, (count, axis) in zip(sources, landing, counts):
            arriving.append(Arriving(source, target, in_sems, at, count, axis))
            at += count
        for item in arriving:
            item.start()
        at = 0
        leaving = []
        for source, target, count in zip(staging, targets, out_counts):
            leaving.append(Leaving(source, target, out_sems, at, count))
            at += count
        body(scalar_refs, arriving, leaving, *extra)
        for item in arriving:
            item()
        for item in leaving:
            while item.waiting:
                item.send()
        for item in leaving:
            item.finish()

    moved = sum(a.size * a.dtype.itemsize for a in (*arrays, *outs))
    return pl.pallas_call(
        kernel,
        name=name,
        in_specs=[SMEM] * ns + [HBM] * na,
        out_specs=(HBM,) * no,
        out_shape=tuple(outs),
        scratch_shapes=[pltpu.VMEM(a.shape, a.dtype) for a in (*arrays, *outs)]
        + [
            pltpu.SemaphoreType.DMA((sum(count for count, _ in counts),)),
            pltpu.SemaphoreType.DMA((sum(out_counts),)),
        ]
        + scratch,
        compiler_params=pltpu.CompilerParams(vmem_limit_bytes=64 << 20),
        cost_estimate=pl.CostEstimate(flops=flops, bytes_accessed=moved, transcendentals=0),
    )(*scalars, *arrays)


def dot(a, b):
    return jnp.dot(a, b, preferred_element_type=F32)


def dot_transposed(a, b):
    return dot(a.T, b)


def column_of(row_vector, width):
    return jnp.broadcast_to(row_vector, (width, row_vector.shape[1])).T


def partner(me, d, number, receive):
    if number & (number - 1) == 0:
        return me ^ d
    other = me + (number - d if receive else d)
    return jnp.where(other >= number, other - number, other)


def send_duals(refineries, dual_q, me, rows, src, swing, carry, outs, acc, product):
    own, *sends, carried = outs
    acc[...] = jnp.zeros_like(acc)
    carried.ref[...] = dot_transposed(carry[0], dual_q[0]).astype(BF16)
    carried.send()
    for m in range(swing.shape[0]):
        product[m] = dot_transposed(swing[m], dual_q[rows[m]])
    for m in range(swing.shape[0]):
        acc[src[m]] += product[m]
    for d, send in enumerate(sends, 1):
        send.ref[...] = acc[pl.ds(partner(me, d, refineries, False) * SC, SC)].astype(BF16)
        send.send()
    own.ref[...] = acc[pl.ds(me * SC, SC)]
    own.send()


def first_duals_body(refineries, scalars, ins, outs, acc, product, dual_q):
    me, rows, src = scalars
    annual, dual, carry, swing = ins
    weekly = outs[0]
    rounded = annual()[...].astype(BF16)
    for w in range(weekly.ref.shape[0]):
        weekly.ref[w] = rounded
    weekly.send()
    size = rounded.shape[0]
    dual = dual()
    for i in range(dual_q.shape[0]):
        dual_q[i] = dual[i * size : (i + 1) * size].astype(BF16)
    send_duals(
        refineries, dual_q, me[0], rows, src, swing(), carry(), outs[1:], acc, product
    )


def adjoint(matrix, turned, size, primal, prices, out, chunks):
    step = out.ref.shape[0] // chunks
    for j in range(chunks):
        columns = slice(j * step, (j + 1) * step)
        part = dot(turned, matrix()[:, columns])
        if j == 0:
            primal, prices = primal(), prices()
        for h in range(step // size):
            at = slice(j * step + h * size, j * step + (h + 1) * size)
            out.ref[at] = primal[at] - PRIMAL_STEP * (
                prices[at] - part[:, h * size : (h + 1) * size].T
            )
        out.send()


def dense_body(chunks, parts, scalars, ins, outs, acc):
    count, rows, cols = scalars
    blocks, upper, dual, primal, prices = ins
    matrix, upper_full, out = outs
    size = upper.target.shape[1]
    width = upper_full.ref.shape[1]
    tiles = matrix.ref.shape[1] // size
    acc[...] = jnp.zeros_like(acc)
    slots = blocks.target.shape[0] // chunks
    for c in range(chunks):
        here = blocks.piece()

        def step(n, _):
            acc[rows[n] * tiles + cols[n]] += here[n].astype(F32)
            return 0

        lax.fori_loop(c * slots, jnp.minimum(count[0], (c + 1) * slots), step, 0)
    for i in range(matrix.ref.shape[0] // size):
        for j in range(tiles):
            at = (slice(i * size, (i + 1) * size), slice(j * size, (j + 1) * size))
            matrix.ref[at] = acc[i * tiles + j].astype(BF16)
    matrix.send()
    upper = upper()
    for j in range(tiles):
        upper_full.ref[j * size : (j + 1) * size] = column_of(upper[j : j + 1], width)
    upper_full.send()
    dual = dual()
    turned = jnp.concatenate(
        [dual[i * size : (i + 1) * size].astype(BF16).T for i in range(dual.shape[0] // size)], axis=1
    )
    adjoint(lambda: matrix.ref, turned, size, primal, prices, out, parts)


def adjoint_body(chunks, scalars, ins, outs):
    dual_q, matrix, primal, prices = ins
    dual_q = dual_q()
    blocks, size, _ = dual_q.shape
    turned = jnp.concatenate([dual_q[i].T for i in range(blocks)], axis=1)
    adjoint(matrix.piece, turned, size, primal, prices, outs[0], chunks)


def primal_body(scalars, ins, outs, acc, image_acc, product):
    ids, cols = scalars
    annual_q, annual, own, carried, primal, upper_full, partial, *arrived = ins
    image, last, extrap, updated, *streams = outs
    blocks, size, _ = extrap.ref.shape
    acc[...] = jnp.zeros_like(acc)
    image_acc[...] = jnp.zeros_like(image_acc)
    annual, annual_q = annual(), annual_q()
    slots = annual.shape[0]
    for k in range(slots):
        product[k] = dot_transposed(annual[k], annual_q[ids[k]])
    for k in range(slots):
        acc[cols[k]] += product[k]
    total = own()[...]
    for piece in arrived:
        total = total + piece()[...].astype(F32)
    acc[:SC] += total
    acc[blocks - 1] += carried()[...].astype(F32)
    partial, primal, upper_full = partial(), primal(), upper_full()
    for j in range(blocks):
        at = slice(j * size, (j + 1) * size)
        new = jnp.clip(partial[at] + PRIMAL_STEP * acc[j], 0.0, upper_full[at])
        updated.ref[at] = new
        ahead = (2.0 * new - primal[at]).astype(BF16)
        extrap.ref[j] = ahead
        if j < SC:
            for copy in streams:
                copy.ref[j] = ahead
        if j == SC - 1:
            for copy in streams:
                copy.send()
        if j == blocks - 1:
            last.ref[...] = ahead
            last.send()
    extrap.send()
    updated.send()
    for k in range(slots):
        product[k] = dot(annual[k], extrap.ref[cols[k]])
    for k in range(slots):
        image_acc[ids[k]] += product[k]
    image.ref[...] = image_acc[...].astype(BF16)


def forward_body(chunks, scalars, ins, outs):
    extrap, matrix, dual, demand = ins
    out = outs[0]
    extrap = extrap()
    blocks, size, width = extrap.shape
    right = jnp.concatenate([extrap[j] for j in range(blocks)], axis=0)
    step = out.ref.shape[0] // chunks
    for i in range(chunks):
        lines = slice(i * step, (i + 1) * step)
        part = dot(matrix.piece()[lines], right)
        if i == 0:
            dual, demand = dual(), demand()
        for h in range(step // size):
            at = slice(i * step + h * size, i * step + (h + 1) * size)
            row = i * (step // size) + h
            out.ref[at] = dual[at] + DUAL_STEP * (
                column_of(demand[row : row + 1], width) - part[h * size : (h + 1) * size]
            )
        out.send()


def dual_body(refineries, more, scalars, ins, outs, gathered, acc, product, *stream_acc):
    me, rows, src = scalars
    swing, carry, streams, previous, partial, parts, annual, need, *arrived = ins
    dual, annual_out = outs[0], outs[1]
    swing, carry = swing(), carry()
    size = swing.shape[1]
    mine = me[0]
    gathered[pl.ds(mine * SC, SC)] = streams()[...]
    for d, piece in enumerate(arrived, 1):
        gathered[pl.ds(partner(mine, d, refineries, True) * SC, SC)] = piece()[...]
    acc[...] = jnp.zeros_like(acc)
    for m in range(swing.shape[0]):
        product[m] = dot(swing[m], gathered[src[m]])
    for m in range(swing.shape[0]):
        acc[rows[m]] += product[m]
    acc[0] += dot(carry[0], previous()[...])
    parts, annual = parts(), annual()
    total = parts[0].astype(F32)
    for w in range(1, parts.shape[0]):
        total = total + parts[w].astype(F32)
    new_annual = jnp.maximum(
        annual[...] + DUAL_STEP * (column_of(need()[...], annual.shape[1]) - total), 0.0
    )
    annual_out.ref[...] = new_annual
    annual_out.send()
    if more:
        rounded = new_annual.astype(BF16)
        for w in range(parts.shape[0]):
            outs[2].ref[w] = rounded
        outs[2].send()
    partial = partial()
    for i in range(acc.shape[0]):
        at = slice(i * size, (i + 1) * size)
        new = jnp.maximum(partial[at] - DUAL_STEP * acc[i], 0.0)
        dual.ref[at] = new
        if more:
            outs[3].ref[i] = new.astype(BF16)
    dual.send()
    if more:
        outs[3].send()
        send_duals(
            refineries, outs[3].ref, mine, rows, src, swing, carry, outs[4:], *stream_acc, product
        )


def shifted(block, axis, distance):
    number = lax.axis_size(axis)
    route = [((i - distance) % number, i) for i in range(number)]
    return lax.ppermute(block, axis, route)


def exchanged(block, axis, d):
    number = lax.axis_size(axis)
    if number & (number - 1) == 0:
        return lax.ppermute(block, axis, [(i, i ^ d) for i in range(number)])
    return shifted(block, axis, d)


def body(
    local_blocks,
    local_rows,
    local_cols,
    band_count,
    swing_blocks,
    swing_rows,
    swing_src,
    carry_blocks,
    annual_blocks,
    annual_ids,
    annual_cols,
    cost,
    upper,
    demand,
    annual_bound,
    x_start,
    y_start,
    annual_start,
):
    scenarios = cost.shape[1]
    size = local_blocks.shape[1]
    columns = cost.shape[0] // size
    rows = y_start.shape[0] // size
    slots = local_blocks.shape[0]
    weeks = lax.axis_size("period")
    refineries = lax.axis_size("refinery")
    others = refineries - 1
    me = lax.axis_index("refinery").astype(jnp.int32).reshape(1)
    tile = shape((size, scenarios), BF16)
    pair_q = shape((SC, size, scenarios), BF16)
    pair = shape((SC, size, scenarios), F32)
    state_x = shape((columns * size, scenarios), F32)
    state_y = shape((rows * size, scenarios), F32)
    blocks_x = shape((columns, size, scenarios), BF16)
    blocks_y = shape((rows, size, scenarios), BF16)
    weekly = shape((weeks, size, scenarios), BF16)
    matrix = shape((rows * size, columns * size), BF16)
    swings = swing_blocks.shape[0]
    annuals = annual_blocks.shape[0]
    unit = 2 * size * size * scenarios
    stream_scratch = pltpu.VMEM((refineries * SC, size, scenarios), F32)
    swing_scratch = pltpu.VMEM((swings, size, scenarios), F32)
    annual_scratch = pltpu.VMEM((annuals, size, scenarios), F32)
    sends_shape = [pair] + [pair_q] * others + [tile]
    chunks = 4 if slots % 4 == 0 and columns % 4 == 0 else 1
    parts_x, parts_y = 1, 1

    upper_rows = upper.reshape(columns, size)
    demand_rows = demand.reshape(rows, size)
    need = annual_bound.reshape(1, size)
    primal, dual, annual = x_start, y_start, annual_start
    annual_send, own, *rest = run(
        functools.partial(first_duals_body, refineries),
        "first_duals",
        [me, swing_rows, swing_src],
        [annual, dual, carry_blocks, swing_blocks],
        [weekly] + sends_shape,
        [stream_scratch, swing_scratch, pltpu.VMEM(blocks_y.shape, BF16)],
        (swings + 1) * unit,
    )
    for iteration in range(ITERS):
        more = iteration + 1 < ITERS
        sends, carried = rest[:others], rest[others]
        annual_q = lax.all_to_all(annual_send, "period", 0, 0, tiled=True)
        carried_back = shifted(carried, "period", -1)
        arrived = [exchanged(send, "refinery", d) for d, send in enumerate(sends, 1)]
        if iteration == 0:
            matrix_q, upper_full, partial_x = run(
                functools.partial(dense_body, chunks, parts_x),
                "dense",
                [band_count, local_rows, local_cols],
                [local_blocks, upper_rows, dual, primal, cost],
                [matrix, state_x, state_x],
                [pltpu.VMEM((rows * columns, size, size), F32)],
                16 * rows * columns * unit,
                {0: (chunks, 0)},
                {2: parts_x},
            )
        else:
            (partial_x,) = run(
                functools.partial(adjoint_body, parts_x),
                "adjoint",
                [],
                [dual_q, matrix_q, primal, cost],
                [state_x],
                [],
                16 * rows * columns * unit,
                {1: (parts_x, 1)},
                {0: parts_x},
            )
        image, last, extrap, updated, streams, *send_streams = run(
            primal_body,
            "primal_step",
            [annual_ids, annual_cols],
            [annual_q, annual_blocks, own, carried_back, primal, upper_full, partial_x, *arrived],
            [weekly, tile, blocks_x, state_x] + [pair_q] * refineries,
            [
                pltpu.VMEM((columns, size, scenarios), F32),
                pltpu.VMEM((weeks, size, scenarios), F32),
                annual_scratch,
            ],
            2 * annuals * unit,
        )
        parts = lax.all_to_all(image, "period", 0, 0, tiled=True)
        previous = shifted(last, "period", 1)
        others_streams = [exchanged(send, "refinery", d) for d, send in enumerate(send_streams, 1)]
        (partial_y,) = run(
            functools.partial(forward_body, parts_y),
            "forward",
            [],
            [extrap, matrix_q, dual, demand_rows],
            [state_y],
            [],
            16 * rows * columns * unit,
            {1: (parts_y, 0)},
            {0: parts_y},
        )
        sent = [weekly, blocks_y] + sends_shape if more else []
        dual, annual, *rest = run(
            functools.partial(dual_body, refineries, more),
            "dual_step",
            [me, swing_rows, swing_src],
            [
                swing_blocks, carry_blocks, streams, previous, partial_y, parts, annual, need,
                *others_streams,
            ],
            [state_y, shape((size, scenarios), F32)] + sent,
            [
                pltpu.VMEM((refineries * SC, size, scenarios), BF16),
                pltpu.VMEM((rows, size, scenarios), F32),
                swing_scratch,
            ]
            + ([stream_scratch] if more else []),
            2 * swings * unit,
        )
        if more:
            annual_send, dual_q, own, *rest = rest
        primal = updated
    return primal, dual, annual


def solution(mesh):
    both = P(("period", "refinery"))
    wide = P(("period", "refinery"), None)
    cube = P(("period", "refinery"), None, None)
    return jax.shard_map(
        body,
        mesh=mesh,
        in_specs=(
            cube, both, both, both, cube, both, both, cube, cube, both, both,
            wide, both, both, both, wide, wide, wide,
        ),
        out_specs=(wide, wide, wide),
        check_vma=False,
    )
```

```python
import functools

import jax
import jax.numpy as jnp
from jax import lax
from jax.experimental import pallas as pl
from jax.experimental.pallas import tpu as pltpu
from jax.sharding import PartitionSpec as P

SC = 2
ITERS = 2

PRIMAL_STEP = 0.5
DUAL_STEP = 0.5
F32 = jnp.float32
BF16 = jnp.bfloat16
HBM = pl.BlockSpec(memory_space=pltpu.HBM)
SMEM = pl.BlockSpec(memory_space=pltpu.SMEM)


def shape(dims, dtype):
    return jax.ShapeDtypeStruct(dims, dtype)


class Arriving:
    def __init__(self, source, target, sems, at, pieces, axis):
        length = source.shape[axis] // pieces
        self.target = target
        self.copies = []
        for p in range(pieces):
            part = (slice(None),) * axis + (pl.ds(p * length, length),)
            self.copies.append(
                pltpu.make_async_copy(source.at[part], target.at[part], sems.at[at + p])
            )

    def start(self):
        for copy in self.copies:
            copy.start()

    def piece(self):
        self.copies.pop(0).wait()
        return self.target

    def __call__(self):
        while self.copies:
            self.piece()
        return self.target


class Leaving:
    def __init__(self, source, target, sems, at, pieces):
        length = source.shape[0] // pieces
        self.ref = source
        self.waiting = []
        for p in range(pieces):
            part = pl.ds(p * length, length)
            self.waiting.append(
                pltpu.make_async_copy(source.at[part], target.at[part], sems.at[at + p])
            )
        self.flying = []

    def send(self):
        copy = self.waiting.pop(0)
        copy.start()
        self.flying.append(copy)

    def finish(self):
        for copy in self.flying:
            copy.wait()


def run(body, name, scalars, arrays, outs, scratch, flops, pieces={}, out_pieces={}):
    counts = [pieces.get(i, (1, 0)) for i in range(len(arrays))]
    out_counts = [out_pieces.get(i, 1) for i in range(len(outs))]
    ns, na, no = len(scalars), len(arrays), len(outs)

    def kernel(*refs):
        scalar_refs, refs = refs[:ns], refs[ns:]
        sources, refs = refs[:na], refs[na:]
        targets, refs = refs[:no], refs[no:]
        landing, refs = refs[:na], refs[na:]
        staging, refs = refs[:no], refs[no:]
        (in_sems, out_sems), extra = refs[:2], refs[2:]
        at = 0
        arriving = []
        for source, target, (count, axis) in zip(sources, landing, counts):
            arriving.append(Arriving(source, target, in_sems, at, count, axis))
            at += count
        for item in arriving:
            item.start()
        at = 0
        leaving = []
        for source, target, count in zip(staging, targets, out_counts):
            leaving.append(Leaving(source, target, out_sems, at, count))
            at += count
        body(scalar_refs, arriving, leaving, *extra)
        for item in arriving:
            item()
        for item in leaving:
            while item.waiting:
                item.send()
        for item in leaving:
            item.finish()

    moved = sum(a.size * a.dtype.itemsize for a in (*arrays, *outs))
    return pl.pallas_call(
        kernel,
        name=name,
        in_specs=[SMEM] * ns + [HBM] * na,
        out_specs=(HBM,) * no,
        out_shape=tuple(outs),
        scratch_shapes=[
            (pltpu.SMEM if a.dtype == jnp.int32 else pltpu.VMEM)(a.shape, a.dtype)
            for a in (*arrays, *outs)
        ]
        + [
            pltpu.SemaphoreType.DMA((sum(count for count, _ in counts),)),
            pltpu.SemaphoreType.DMA((sum(out_counts),)),
        ]
        + scratch,
        compiler_params=pltpu.CompilerParams(vmem_limit_bytes=64 << 20),
        cost_estimate=pl.CostEstimate(flops=flops, bytes_accessed=moved, transcendentals=0),
    )(*scalars, *arrays)


def dot(a, b):
    return jnp.dot(a, b, preferred_element_type=F32)


def dot_transposed(a, b):
    return dot(a.T, b)


def column_of(row_vector, width):
    return jnp.broadcast_to(row_vector, (width, row_vector.shape[1])).T


def partner(me, d, number, receive):
    if number & (number - 1) == 0:
        return me ^ d
    other = me + (number - d if receive else d)
    return jnp.where(other >= number, other - number, other)


def send_duals(refineries, dual_q, me, rows, src, swing, carry, outs, acc, product):
    own, *sends, carried = outs
    acc[...] = jnp.zeros_like(acc)
    carried.ref[...] = dot_transposed(carry[0], dual_q[0]).astype(BF16)
    carried.send()
    for m in range(swing.shape[0]):
        product[m] = dot_transposed(swing[m], dual_q[rows[m]])
    for m in range(swing.shape[0]):
        acc[src[m]] += product[m]
    for d, send in enumerate(sends, 1):
        send.ref[...] = acc[pl.ds(partner(me, d, refineries, False) * SC, SC)].astype(BF16)
        send.send()
    own.ref[...] = acc[pl.ds(me * SC, SC)]
    own.send()


def first_duals_body(refineries, scalars, ins, outs, acc, product, dual_q):
    me, rows, src = scalars
    annual, dual, carry, swing = ins
    weekly = outs[0]
    rounded = annual()[...].astype(BF16)
    for w in range(weekly.ref.shape[0]):
        weekly.ref[w] = rounded
    weekly.send()
    size = rounded.shape[0]
    dual = dual()
    for i in range(dual_q.shape[0]):
        dual_q[i] = dual[i * size : (i + 1) * size].astype(BF16)
    send_duals(
        refineries, dual_q, me[0], rows, src, swing(), carry(), outs[1:], acc, product
    )


def adjoint(matrix, turned, size, primal, prices, out):
    part = dot(turned, matrix[...])
    primal, prices = primal(), prices()
    for j in range(part.shape[1] // size):
        at = slice(j * size, (j + 1) * size)
        out.ref[at] = primal[at] - PRIMAL_STEP * (prices[at] - part[:, at].T)


def dense_body(chunks, scalars, ins, outs, acc):
    rows, cols = scalars
    count, dual, blocks, primal, prices = ins
    matrix, out = outs
    size = blocks.target.shape[1]
    tiles = matrix.ref.shape[1] // size
    acc[...] = jnp.zeros_like(acc)
    count, dual = count(), dual()
    turned = jnp.concatenate(
        [dual[i * size : (i + 1) * size].astype(BF16).T for i in range(dual.shape[0] // size)], axis=1
    )
    slots = blocks.target.shape[0] // chunks
    for c in range(chunks):
        here = blocks.piece()

        def step(n, _):
            acc[rows[n] * tiles + cols[n]] += here[n].astype(F32)
            return 0

        lax.fori_loop(c * slots, jnp.minimum(count[0], (c + 1) * slots), step, 0)
    for i in range(matrix.ref.shape[0] // size):
        for j in range(tiles):
            at = (slice(i * size, (i + 1) * size), slice(j * size, (j + 1) * size))
            matrix.ref[at] = acc[i * tiles + j].astype(BF16)
        matrix.send()
    adjoint(matrix.ref, turned, size, primal, prices, out)


def adjoint_body(scalars, ins, outs):
    dual_q, matrix, primal, prices = ins
    dual_q = dual_q()
    blocks, size, _ = dual_q.shape
    turned = jnp.concatenate([dual_q[i].T for i in range(blocks)], axis=1)
    adjoint(matrix(), turned, size, primal, prices, outs[0])


def primal_body(scalars, ins, outs, acc, image_acc, product, bound):
    ids, cols = scalars
    upper, annual, annual_q, own, carried, *arrived, partial, primal = ins
    image, last, extrap, updated, streams = outs
    blocks, size, _ = extrap.ref.shape
    acc[...] = jnp.zeros_like(acc)
    image_acc[...] = jnp.zeros_like(image_acc)
    upper = upper()
    for j in range(blocks):
        bound[j] = column_of(upper[j : j + 1], bound.shape[2])
    annual, annual_q = annual(), annual_q()
    slots = annual.shape[0]
    for k in range(slots):
        product[k] = dot_transposed(annual[k], annual_q[ids[k]])
    for k in range(slots):
        acc[cols[k]] += product[k]
    total = own()[...]
    for piece in arrived:
        total = total + piece()[...].astype(F32)
    acc[:SC] += total
    acc[blocks - 1] += carried()[...].astype(F32)
    partial, primal = partial(), primal()
    for j in range(blocks):
        at = slice(j * size, (j + 1) * size)
        new = jnp.clip(partial[at] + PRIMAL_STEP * acc[j], 0.0, bound[j])
        updated.ref[at] = new
        ahead = (2.0 * new - primal[at]).astype(BF16)
        extrap.ref[j] = ahead
        if j < SC:
            streams.ref[j] = ahead
        if j == SC - 1:
            streams.send()
        if j == blocks - 1:
            last.ref[...] = ahead
            last.send()
    extrap.send()
    updated.send()
    for k in range(slots):
        product[k] = dot(annual[k], extrap.ref[cols[k]])
    for k in range(slots):
        image_acc[ids[k]] += product[k]
    image.ref[...] = image_acc[...].astype(BF16)


def forward_body(scalars, ins, outs):
    extrap, demand, dual, matrix = ins
    out = outs[0]
    extrap, demand, dual = extrap(), demand(), dual()
    blocks, size, width = extrap.shape
    right = jnp.concatenate([extrap[j] for j in range(blocks)], axis=0)
    for i in range(demand.shape[0]):
        at = slice(i * size, (i + 1) * size)
        out.ref[at] = dual[at] + DUAL_STEP * column_of(demand[i : i + 1], width)
    out.ref[...] -= DUAL_STEP * dot(matrix()[...], right)


def dual_body(refineries, more, scalars, ins, outs, gathered, acc, product, *stream_acc):
    me, rows, src = scalars
    swing, streams, *arrived, carry, previous, parts, annual, need, partial = ins
    dual, annual_out = outs[0], outs[1]
    swing = swing()
    size = swing.shape[1]
    mine = me[0]
    gathered[pl.ds(mine * SC, SC)] = streams()[...]
    for d, piece in enumerate(arrived, 1):
        gathered[pl.ds(partner(mine, d, refineries, True) * SC, SC)] = piece()[...]
    acc[...] = jnp.zeros_like(acc)
    for m in range(swing.shape[0]):
        product[m] = dot(swing[m], gathered[src[m]])
    for m in range(swing.shape[0]):
        acc[rows[m]] += product[m]
    carry = carry()
    acc[0] += dot(carry[0], previous()[...])
    parts, annual = parts(), annual()
    total = parts[0].astype(F32)
    for w in range(1, parts.shape[0]):
        total = total + parts[w].astype(F32)
    new_annual = jnp.maximum(
        annual[...] + DUAL_STEP * (column_of(need()[...], annual.shape[1]) - total), 0.0
    )
    annual_out.ref[...] = new_annual
    annual_out.send()
    if more:
        rounded = new_annual.astype(BF16)
        for w in range(parts.shape[0]):
            outs[2].ref[w] = rounded
        outs[2].send()
    partial = partial()
    for i in range(acc.shape[0]):
        at = slice(i * size, (i + 1) * size)
        new = jnp.maximum(partial[at] - DUAL_STEP * acc[i], 0.0)
        dual.ref[at] = new
        if more:
            outs[3].ref[i] = new.astype(BF16)
    dual.send()
    if more:
        outs[3].send()
        send_duals(
            refineries, outs[3].ref, mine, rows, src, swing, carry, outs[4:], *stream_acc, product
        )


def shifted(block, axis, distance):
    number = lax.axis_size(axis)
    route = [((i - distance) % number, i) for i in range(number)]
    return lax.ppermute(block, axis, route)


def exchanged(block, axis, d):
    number = lax.axis_size(axis)
    if number & (number - 1) == 0:
        return lax.ppermute(block, axis, [(i, i ^ d) for i in range(number)])
    return shifted(block, axis, d)


def body(
    local_blocks,
    local_rows,
    local_cols,
    band_count,
    swing_blocks,
    swing_rows,
    swing_src,
    carry_blocks,
    annual_blocks,
    annual_ids,
    annual_cols,
    cost,
    upper,
    demand,
    annual_bound,
    x_start,
    y_start,
    annual_start,
):
    scenarios = cost.shape[1]
    size = local_blocks.shape[1]
    columns = cost.shape[0] // size
    rows = y_start.shape[0] // size
    slots = local_blocks.shape[0]
    weeks = lax.axis_size("period")
    refineries = lax.axis_size("refinery")
    others = refineries - 1
    me = lax.axis_index("refinery").astype(jnp.int32).reshape(1)
    tile = shape((size, scenarios), BF16)
    pair_q = shape((SC, size, scenarios), BF16)
    pair = shape((SC, size, scenarios), F32)
    state_x = shape((columns * size, scenarios), F32)
    state_y = shape((rows * size, scenarios), F32)
    blocks_x = shape((columns, size, scenarios), BF16)
    blocks_y = shape((rows, size, scenarios), BF16)
    weekly = shape((weeks, size, scenarios), BF16)
    matrix = shape((rows * size, columns * size), BF16)
    swings = swing_blocks.shape[0]
    annuals = annual_blocks.shape[0]
    unit = 2 * size * size * scenarios
    stream_scratch = pltpu.VMEM((refineries * SC, size, scenarios), F32)
    swing_scratch = pltpu.VMEM((swings, size, scenarios), F32)
    annual_scratch = pltpu.VMEM((annuals, size, scenarios), F32)
    sends_shape = [pair] + [pair_q] * others + [tile]
    chunks = 8 if slots % 8 == 0 else 1

    upper_rows = upper.reshape(columns, size)
    demand_rows = demand.reshape(rows, size)
    need = annual_bound.reshape(1, size)
    primal, dual, annual = x_start, y_start, annual_start
    annual_send, own, *rest = run(
        functools.partial(first_duals_body, refineries),
        "first_duals",
        [me, swing_rows, swing_src],
        [annual, dual, carry_blocks, swing_blocks],
        [weekly] + sends_shape,
        [stream_scratch, swing_scratch, pltpu.VMEM(blocks_y.shape, BF16)],
        (swings + 1) * unit,
    )
    for iteration in range(ITERS):
        more = iteration + 1 < ITERS
        sends, carried = rest[:others], rest[others]
        annual_q = lax.all_to_all(annual_send, "period", 0, 0, tiled=True)
        carried_back = shifted(carried, "period", -1)
        arrived = [exchanged(send, "refinery", d) for d, send in enumerate(sends, 1)]
        if iteration == 0:
            matrix_q, partial_x = run(
                functools.partial(dense_body, chunks),
                "dense",
                [local_rows, local_cols],
                [band_count, dual, local_blocks, primal, cost],
                [matrix, state_x],
                [pltpu.VMEM((rows * columns, size, size), F32)],
                16 * rows * columns * unit,
                {2: (chunks, 0)},
                {0: rows},
            )
        else:
            (partial_x,) = run(
                adjoint_body,
                "adjoint",
                [],
                [dual_q, matrix_q, primal, cost],
                [state_x],
                [],
                16 * rows * columns * unit,
            )
        image, last, extrap, updated, streams = run(
            primal_body,
            "primal_step",
            [annual_ids, annual_cols],
            [upper_rows, annual_blocks, annual_q, own, carried_back, *arrived, partial_x, primal],
            [weekly, tile, blocks_x, state_x, pair_q],
            [
                pltpu.VMEM((columns, size, scenarios), F32),
                pltpu.VMEM((weeks, size, scenarios), F32),
                annual_scratch,
                pltpu.VMEM((columns, size, scenarios), F32),
            ],
            2 * annuals * unit,
        )
        parts = lax.all_to_all(image, "period", 0, 0, tiled=True)
        previous = shifted(last, "period", 1)
        others_streams = [exchanged(streams, "refinery", d) for d in range(1, refineries)]
        (partial_y,) = run(
            forward_body,
            "forward",
            [],
            [extrap, demand_rows, dual, matrix_q],
            [state_y],
            [],
            16 * rows * columns * unit,
        )
        sent = [weekly, blocks_y] + sends_shape if more else []
        dual, annual, *rest = run(
            functools.partial(dual_body, refineries, more),
            "dual_step",
            [me, swing_rows, swing_src],
            [
                swing_blocks, streams, *others_streams, carry_blocks, previous, parts, annual,
                need, partial_y,
            ],
            [state_y, shape((size, scenarios), F32)] + sent,
            [
                pltpu.VMEM((refineries * SC, size, scenarios), BF16),
                pltpu.VMEM((rows, size, scenarios), F32),
                swing_scratch,
            ]
            + ([stream_scratch] if more else []),
            2 * swings * unit,
        )
        if more:
            annual_send, dual_q, own, *rest = rest
        primal = updated
    return primal, dual, annual


def solution(mesh):
    both = P(("period", "refinery"))
    wide = P(("period", "refinery"), None)
    cube = P(("period", "refinery"), None, None)
    return jax.shard_map(
        body,
        mesh=mesh,
        in_specs=(
            cube, both, both, both, cube, both, both, cube, cube, both, both,
            wide, both, both, both, wide, wide, wide,
        ),
        out_specs=(wide, wide, wide),
        check_vma=False,
    )
```

```python
import functools

import jax
import jax.numpy as jnp
from jax import lax
from jax.experimental import pallas as pl
from jax.experimental.pallas import tpu as pltpu
from jax.sharding import PartitionSpec as P

SC = 2
ITERS = 2

PRIMAL_STEP = 0.5
DUAL_STEP = 0.5
F32 = jnp.float32
BF16 = jnp.bfloat16
HBM = pl.BlockSpec(memory_space=pltpu.HBM)
SMEM = pl.BlockSpec(memory_space=pltpu.SMEM)


def shape(dims, dtype):
    return jax.ShapeDtypeStruct(dims, dtype)


class Arriving:
    def __init__(self, source, target, sems, at, pieces, axis):
        length = source.shape[axis] // pieces
        self.target = target
        self.copies = []
        for p in range(pieces):
            part = (slice(None),) * axis + (pl.ds(p * length, length),)
            self.copies.append(
                pltpu.make_async_copy(source.at[part], target.at[part], sems.at[at + p])
            )

    def start(self):
        for copy in self.copies:
            copy.start()

    def piece(self):
        self.copies.pop(0).wait()
        return self.target

    def __call__(self):
        while self.copies:
            self.piece()
        return self.target


class Leaving:
    def __init__(self, source, target, sems, at, pieces):
        length = source.shape[0] // pieces
        self.ref = source
        self.waiting = []
        for p in range(pieces):
            part = pl.ds(p * length, length)
            self.waiting.append(
                pltpu.make_async_copy(source.at[part], target.at[part], sems.at[at + p])
            )
        self.flying = []

    def send(self):
        copy = self.waiting.pop(0)
        copy.start()
        self.flying.append(copy)

    def finish(self):
        for copy in self.flying:
            copy.wait()


def run(body, name, scalars, arrays, outs, scratch, flops, pieces={}, out_pieces={}):
    counts = [pieces.get(i, (1, 0)) for i in range(len(arrays))]
    out_counts = [out_pieces.get(i, 1) for i in range(len(outs))]
    ns, na, no = len(scalars), len(arrays), len(outs)

    def kernel(*refs):
        scalar_refs, refs = refs[:ns], refs[ns:]
        sources, refs = refs[:na], refs[na:]
        targets, refs = refs[:no], refs[no:]
        landing, refs = refs[:na], refs[na:]
        staging, refs = refs[:no], refs[no:]
        (in_sems, out_sems), extra = refs[:2], refs[2:]
        at = 0
        arriving = []
        for source, target, (count, axis) in zip(sources, landing, counts):
            arriving.append(Arriving(source, target, in_sems, at, count, axis))
            at += count
        for item in arriving:
            item.start()
        at = 0
        leaving = []
        for source, target, count in zip(staging, targets, out_counts):
            leaving.append(Leaving(source, target, out_sems, at, count))
            at += count
        body(scalar_refs, arriving, leaving, *extra)
        for item in arriving:
            item()
        for item in leaving:
            while item.waiting:
                item.send()
        for item in leaving:
            item.finish()

    moved = sum(a.size * a.dtype.itemsize for a in (*arrays, *outs))
    return pl.pallas_call(
        kernel,
        name=name,
        in_specs=[SMEM] * ns + [HBM] * na,
        out_specs=(HBM,) * no,
        out_shape=tuple(outs),
        scratch_shapes=[
            (pltpu.SMEM if a.dtype == jnp.int32 else pltpu.VMEM)(a.shape, a.dtype)
            for a in (*arrays, *outs)
        ]
        + [
            pltpu.SemaphoreType.DMA((sum(count for count, _ in counts),)),
            pltpu.SemaphoreType.DMA((sum(out_counts),)),
        ]
        + scratch,
        compiler_params=pltpu.CompilerParams(vmem_limit_bytes=64 << 20),
        cost_estimate=pl.CostEstimate(flops=flops, bytes_accessed=moved, transcendentals=0),
    )(*scalars, *arrays)


def dot(a, b):
    return jnp.dot(a, b, preferred_element_type=F32)


def dot_transposed(a, b):
    return dot(a.T, b)


def column_of(row_vector, width):
    return jnp.broadcast_to(row_vector, (width, row_vector.shape[1])).T


def partner(me, d, number, receive):
    if number & (number - 1) == 0:
        return me ^ d
    other = me + (number - d if receive else d)
    return jnp.where(other >= number, other - number, other)


def send_duals(refineries, dual_q, me, rows, src, swing, carry, outs, acc, product):
    own, *sends, carried = outs
    acc[...] = jnp.zeros_like(acc)
    carried.ref[...] = dot_transposed(carry[0], dual_q[0]).astype(BF16)
    carried.send()
    for m in range(swing.shape[0]):
        product[m] = dot_transposed(swing[m], dual_q[rows[m]])
    for m in range(swing.shape[0]):
        acc[src[m]] += product[m]
    for d, send in enumerate(sends, 1):
        send.ref[...] = acc[pl.ds(partner(me, d, refineries, False) * SC, SC)].astype(BF16)
        send.send()
    own.ref[...] = acc[pl.ds(me * SC, SC)]
    own.send()


def first_duals_body(refineries, scalars, ins, outs, acc, product, dual_q):
    me, rows, src = scalars
    annual, dual, carry, swing = ins
    weekly = outs[0]
    rounded = annual()[...].astype(BF16)
    for w in range(weekly.ref.shape[0]):
        weekly.ref[w] = rounded
    weekly.send()
    size = rounded.shape[0]
    dual = dual()
    for i in range(dual_q.shape[0]):
        dual_q[i] = dual[i * size : (i + 1) * size].astype(BF16)
    send_duals(
        refineries, dual_q, me[0], rows, src, swing(), carry(), outs[1:], acc, product
    )


def adjoint(matrix, turned, size, primal, prices, out):
    part = dot(turned, matrix[...])
    primal, prices = primal(), prices()
    for j in range(part.shape[1] // size):
        at = slice(j * size, (j + 1) * size)
        out.ref[at] = primal[at] - PRIMAL_STEP * (prices[at] - part[:, at].T)


def dense_body(chunks, scalars, ins, outs, acc):
    rows, cols = scalars
    count, dual, blocks, primal, prices = ins
    matrix, out = outs
    size = blocks.target.shape[1]
    tiles = matrix.ref.shape[1] // size
    acc[...] = jnp.zeros_like(acc)
    count, dual = count(), dual()
    turned = jnp.concatenate(
        [dual[i * size : (i + 1) * size].astype(BF16).T for i in range(dual.shape[0] // size)], axis=1
    )
    slots = blocks.target.shape[0] // chunks
    for c in range(chunks):
        here = blocks.piece()

        def step(n, _):
            acc[rows[n] * tiles + cols[n]] += here[n].astype(F32)
            return 0

        lax.fori_loop(c * slots, jnp.minimum(count[0], (c + 1) * slots), step, 0)
    for i in range(matrix.ref.shape[0] // size):
        for j in range(tiles):
            at = (slice(i * size, (i + 1) * size), slice(j * size, (j + 1) * size))
            matrix.ref[at] = acc[i * tiles + j].astype(BF16)
        matrix.send()
    adjoint(matrix.ref, turned, size, primal, prices, out)


def adjoint_body(scalars, ins, outs):
    dual_q, matrix, primal, prices = ins
    dual_q = dual_q()
    blocks, size, _ = dual_q.shape
    turned = jnp.concatenate([dual_q[i].T for i in range(blocks)], axis=1)
    adjoint(matrix(), turned, size, primal, prices, outs[0])


def primal_body(scalars, ins, outs, acc, image_acc, product, bound):
    ids, cols = scalars
    upper, annual, annual_q, own, carried, *arrived, partial, primal = ins
    image, last, extrap, updated, streams = outs
    blocks, size, _ = extrap.ref.shape
    acc[...] = jnp.zeros_like(acc)
    image_acc[...] = jnp.zeros_like(image_acc)
    upper = upper()
    for j in range(blocks):
        bound[j] = column_of(upper[j : j + 1], bound.shape[2])
    annual, annual_q = annual(), annual_q()
    slots = annual.shape[0]
    for k in range(slots):
        product[k] = dot_transposed(annual[k], annual_q[ids[k]])
    for k in range(slots):
        acc[cols[k]] += product[k]
    total = own()[...]
    for piece in arrived:
        total = total + piece()[...].astype(F32)
    acc[:SC] += total
    acc[blocks - 1] += carried()[...].astype(F32)
    partial, primal = partial(), primal()
    for j in range(blocks):
        at = slice(j * size, (j + 1) * size)
        new = jnp.clip(partial[at] + PRIMAL_STEP * acc[j], 0.0, bound[j])
        updated.ref[at] = new
        ahead = (2.0 * new - primal[at]).astype(BF16)
        extrap.ref[j] = ahead
        if j < SC:
            streams.ref[j] = ahead
        if j == SC - 1:
            streams.send()
        if j == blocks - 1:
            last.ref[...] = ahead
            last.send()
    extrap.send()
    updated.send()
    for k in range(slots):
        product[k] = dot(annual[k], extrap.ref[cols[k]])
    for k in range(slots):
        image_acc[ids[k]] += product[k]
    image.ref[...] = image_acc[...].astype(BF16)


def forward_body(scalars, ins, outs):
    extrap, demand, dual, matrix = ins
    out = outs[0]
    extrap, demand, dual = extrap(), demand(), dual()
    blocks, size, width = extrap.shape
    right = jnp.concatenate([extrap[j] for j in range(blocks)], axis=0)
    for i in range(demand.shape[0]):
        at = slice(i * size, (i + 1) * size)
        out.ref[at] = dual[at] + DUAL_STEP * column_of(demand[i : i + 1], width)
    out.ref[...] -= DUAL_STEP * dot(matrix()[...], right)


def dual_body(refineries, scalars, ins, outs, gathered, acc, product, stream_acc):
    me, rows, src = scalars
    swing, streams, *arrived, carry, previous, parts, annual, need, partial = ins
    dual, annual_out = outs[0], outs[1]
    swing = swing()
    size = swing.shape[1]
    mine = me[0]
    gathered[pl.ds(mine * SC, SC)] = streams()[...]
    for d, piece in enumerate(arrived, 1):
        gathered[pl.ds(partner(mine, d, refineries, True) * SC, SC)] = piece()[...]
    acc[...] = jnp.zeros_like(acc)
    for m in range(swing.shape[0]):
        product[m] = dot(swing[m], gathered[src[m]])
    for m in range(swing.shape[0]):
        acc[rows[m]] += product[m]
    carry = carry()
    acc[0] += dot(carry[0], previous()[...])
    parts, annual = parts(), annual()
    total = parts[0].astype(F32)
    for w in range(1, parts.shape[0]):
        total = total + parts[w].astype(F32)
    new_annual = jnp.maximum(
        annual[...] + DUAL_STEP * (column_of(need()[...], annual.shape[1]) - total), 0.0
    )
    annual_out.ref[...] = new_annual
    annual_out.send()
    rounded = new_annual.astype(BF16)
    for w in range(parts.shape[0]):
        outs[2].ref[w] = rounded
    outs[2].send()
    partial = partial()
    for i in range(acc.shape[0]):
        at = slice(i * size, (i + 1) * size)
        new = jnp.maximum(partial[at] - DUAL_STEP * acc[i], 0.0)
        dual.ref[at] = new
        outs[3].ref[i] = new.astype(BF16)
    dual.send()
    outs[3].send()
    send_duals(
        refineries, outs[3].ref, mine, rows, src, swing, carry, outs[4:], stream_acc, product
    )


def last_rows_body(refineries, scalars, ins, outs, gathered, acc, product):
    me, rows, src = scalars
    demand, dual, extrap, matrix, swing, streams, *arrived = ins
    out = outs[0]
    demand, dual, extrap = demand(), dual(), extrap()
    blocks, size, width = extrap.shape
    for i in range(demand.shape[0]):
        at = slice(i * size, (i + 1) * size)
        out.ref[at] = dual[at] + DUAL_STEP * column_of(demand[i : i + 1], width)
    right = jnp.concatenate([extrap[j] for j in range(blocks)], axis=0)
    out.ref[...] -= DUAL_STEP * dot(matrix()[...], right)
    swing, mine = swing(), me[0]
    gathered[pl.ds(mine * SC, SC)] = streams()[...]
    for d, piece in enumerate(arrived, 1):
        gathered[pl.ds(partner(mine, d, refineries, True) * SC, SC)] = piece()[...]
    acc[...] = jnp.zeros_like(acc)
    for m in range(swing.shape[0]):
        product[m] = dot(swing[m], gathered[src[m]])
    for m in range(swing.shape[0]):
        acc[rows[m]] += product[m]
    for i in range(acc.shape[0]):
        at = slice(i * size, (i + 1) * size)
        new = out.ref[at] - DUAL_STEP * acc[i]
        out.ref[at] = jnp.maximum(new, 0.0) if i else new


def finish_kernel(
    row, annual, need, parts, carry, previous, dual_out, annual_out,
    row_v, annual_v, need_v, parts_v, carry_v, previous_v, new_v, in_sems, out_sems,
):
    size = row_v.shape[0]
    head = pl.ds(0, size)
    sources = (row.at[head], carry, previous, annual, need, parts)
    landing = (row_v, carry_v, previous_v, annual_v, need_v, parts_v)
    copies = [
        pltpu.make_async_copy(source, target, in_sems.at[i])
        for i, (source, target) in enumerate(zip(sources, landing))
    ]
    for copy in copies:
        copy.start()
    for copy in copies[:3]:
        copy.wait()
    row_v[...] = jnp.maximum(row_v[...] - DUAL_STEP * dot(carry_v[0], previous_v[...]), 0.0)
    first = pltpu.make_async_copy(row_v, dual_out.at[head], out_sems.at[0])
    first.start()
    for copy in copies[3:]:
        copy.wait()
    total = parts_v[0].astype(F32)
    for w in range(1, parts_v.shape[0]):
        total = total + parts_v[w].astype(F32)
    new_v[...] = jnp.maximum(
        annual_v[...] + DUAL_STEP * (column_of(need_v[...], annual_v.shape[1]) - total), 0.0
    )
    second = pltpu.make_async_copy(new_v, annual_out, out_sems.at[1])
    second.start()
    first.wait()
    second.wait()


def finish(dual, annual, need, parts, carry, previous):
    size, width = annual.shape
    arrays = (dual, annual, need, parts, carry, previous)
    buffers = (annual, annual, need, parts, carry, previous, annual)
    return pl.pallas_call(
        finish_kernel,
        name="finish",
        in_specs=[HBM] * 6,
        out_specs=(HBM, HBM),
        out_shape=(shape(dual.shape, F32), shape(annual.shape, F32)),
        scratch_shapes=[pltpu.VMEM(a.shape, a.dtype) for a in buffers]
        + [pltpu.SemaphoreType.DMA((6,)), pltpu.SemaphoreType.DMA((2,))],
        input_output_aliases={0: 0},
        compiler_params=pltpu.CompilerParams(vmem_limit_bytes=64 << 20),
        cost_estimate=pl.CostEstimate(
            flops=2 * size * size * width, bytes_accessed=1_000_000, transcendentals=0
        ),
    )(*arrays)


def shifted(block, axis, distance):
    number = lax.axis_size(axis)
    route = [((i - distance) % number, i) for i in range(number)]
    return lax.ppermute(block, axis, route)


def exchanged(block, axis, d):
    number = lax.axis_size(axis)
    if number & (number - 1) == 0:
        return lax.ppermute(block, axis, [(i, i ^ d) for i in range(number)])
    return shifted(block, axis, d)


def body(
    local_blocks,
    local_rows,
    local_cols,
    band_count,
    swing_blocks,
    swing_rows,
    swing_src,
    carry_blocks,
    annual_blocks,
    annual_ids,
    annual_cols,
    cost,
    upper,
    demand,
    annual_bound,
    x_start,
    y_start,
    annual_start,
):
    scenarios = cost.shape[1]
    size = local_blocks.shape[1]
    columns = cost.shape[0] // size
    rows = y_start.shape[0] // size
    slots = local_blocks.shape[0]
    weeks = lax.axis_size("period")
    refineries = lax.axis_size("refinery")
    others = refineries - 1
    me = lax.axis_index("refinery").astype(jnp.int32).reshape(1)
    tile = shape((size, scenarios), BF16)
    pair_q = shape((SC, size, scenarios), BF16)
    pair = shape((SC, size, scenarios), F32)
    state_x = shape((columns * size, scenarios), F32)
    state_y = shape((rows * size, scenarios), F32)
    blocks_x = shape((columns, size, scenarios), BF16)
    blocks_y = shape((rows, size, scenarios), BF16)
    weekly = shape((weeks, size, scenarios), BF16)
    matrix = shape((rows * size, columns * size), BF16)
    swings = swing_blocks.shape[0]
    annuals = annual_blocks.shape[0]
    unit = 2 * size * size * scenarios
    stream_scratch = pltpu.VMEM((refineries * SC, size, scenarios), F32)
    swing_scratch = pltpu.VMEM((swings, size, scenarios), F32)
    annual_scratch = pltpu.VMEM((annuals, size, scenarios), F32)
    sends_shape = [pair] + [pair_q] * others + [tile]
    chunks = 8 if slots % 8 == 0 else 1

    upper_rows = upper.reshape(columns, size)
    demand_rows = demand.reshape(rows, size)
    need = annual_bound.reshape(1, size)
    primal, dual, annual = x_start, y_start, annual_start
    annual_send, own, *rest = run(
        functools.partial(first_duals_body, refineries),
        "first_duals",
        [me, swing_rows, swing_src],
        [annual, dual, carry_blocks, swing_blocks],
        [weekly] + sends_shape,
        [stream_scratch, swing_scratch, pltpu.VMEM(blocks_y.shape, BF16)],
        (swings + 1) * unit,
    )
    for iteration in range(ITERS):
        more = iteration + 1 < ITERS
        sends, carried = rest[:others], rest[others]
        annual_q = lax.all_to_all(annual_send, "period", 0, 0, tiled=True)
        carried_back = shifted(carried, "period", -1)
        arrived = [exchanged(send, "refinery", d) for d, send in enumerate(sends, 1)]
        if iteration == 0:
            matrix_q, partial_x = run(
                functools.partial(dense_body, chunks),
                "dense",
                [local_rows, local_cols],
                [band_count, dual, local_blocks, primal, cost],
                [matrix, state_x],
                [pltpu.VMEM((rows * columns, size, size), F32)],
                16 * rows * columns * unit,
                {2: (chunks, 0)},
                {0: rows},
            )
        else:
            (partial_x,) = run(
                adjoint_body,
                "adjoint",
                [],
                [dual_q, matrix_q, primal, cost],
                [state_x],
                [],
                16 * rows * columns * unit,
            )
        image, last, extrap, updated, streams = run(
            primal_body,
            "primal_step",
            [annual_ids, annual_cols],
            [upper_rows, annual_blocks, annual_q, own, carried_back, *arrived, partial_x, primal],
            [weekly, tile, blocks_x, state_x, pair_q],
            [
                pltpu.VMEM((columns, size, scenarios), F32),
                pltpu.VMEM((weeks, size, scenarios), F32),
                annual_scratch,
                pltpu.VMEM((columns, size, scenarios), F32),
            ],
            2 * annuals * unit,
        )
        parts = lax.all_to_all(image, "period", 0, 0, tiled=True)
        previous = shifted(last, "period", 1)
        others_streams = [exchanged(streams, "refinery", d) for d in range(1, refineries)]
        if not more:
            (dual,) = run(
                functools.partial(last_rows_body, refineries),
                "last_rows",
                [me, swing_rows, swing_src],
                [demand_rows, dual, extrap, matrix_q, swing_blocks, streams, *others_streams],
                [state_y],
                [
                    pltpu.VMEM((refineries * SC, size, scenarios), BF16),
                    pltpu.VMEM((rows, size, scenarios), F32),
                    swing_scratch,
                ],
                unit,
            )
            dual, annual = finish(dual, annual, need, parts, carry_blocks, previous)
            return updated, dual, annual
        (partial_y,) = run(
            forward_body,
            "forward",
            [],
            [extrap, demand_rows, dual, matrix_q],
            [state_y],
            [],
            16 * rows * columns * unit,
        )
        sent = [weekly, blocks_y] + sends_shape
        dual, annual, *rest = run(
            functools.partial(dual_body, refineries),
            "dual_step",
            [me, swing_rows, swing_src],
            [
                swing_blocks, streams, *others_streams, carry_blocks, previous, parts, annual,
                need, partial_y,
            ],
            [state_y, shape((size, scenarios), F32)] + sent,
            [
                pltpu.VMEM((refineries * SC, size, scenarios), BF16),
                pltpu.VMEM((rows, size, scenarios), F32),
                swing_scratch,
            ]
            + [stream_scratch],
            2 * swings * unit,
        )
        annual_send, dual_q, own, *rest = rest
        primal = updated


def solution(mesh):
    both = P(("period", "refinery"))
    wide = P(("period", "refinery"), None)
    cube = P(("period", "refinery"), None, None)
    return jax.shard_map(
        body,
        mesh=mesh,
        in_specs=(
            cube, both, both, both, cube, both, both, cube, cube, both, both,
            wide, both, both, both, wide, wide, wide,
        ),
        out_specs=(wide, wide, wide),
        check_vma=False,
    )
```

```python
import functools

import jax
import jax.numpy as jnp
from jax import lax
from jax.experimental import pallas as pl
from jax.experimental.pallas import tpu as pltpu
from jax.sharding import PartitionSpec as P

SC = 2
ITERS = 2

PRIMAL_STEP = 0.5
DUAL_STEP = 0.5
F32 = jnp.float32
BF16 = jnp.bfloat16
HBM = pl.BlockSpec(memory_space=pltpu.HBM)
SMEM = pl.BlockSpec(memory_space=pltpu.SMEM)


def shape(dims, dtype):
    return jax.ShapeDtypeStruct(dims, dtype)


class Arriving:
    def __init__(self, source, target, sems, at, pieces, axis):
        length = source.shape[axis] // pieces
        self.target = target
        self.copies = []
        for p in range(pieces):
            part = (slice(None),) * axis + (pl.ds(p * length, length),)
            self.copies.append(
                pltpu.make_async_copy(source.at[part], target.at[part], sems.at[at + p])
            )

    def start(self):
        for copy in self.copies:
            copy.start()

    def piece(self):
        self.copies.pop(0).wait()
        return self.target

    def __call__(self):
        while self.copies:
            self.piece()
        return self.target


class Leaving:
    def __init__(self, source, target, sems, at, pieces):
        length = source.shape[0] // pieces
        self.ref = source
        self.waiting = []
        for p in range(pieces):
            part = pl.ds(p * length, length)
            self.waiting.append(
                pltpu.make_async_copy(source.at[part], target.at[part], sems.at[at + p])
            )
        self.flying = []

    def send(self):
        copy = self.waiting.pop(0)
        copy.start()
        self.flying.append(copy)

    def finish(self):
        for copy in self.flying:
            copy.wait()


def run(body, name, scalars, arrays, outs, scratch, flops, pieces={}, out_pieces={}):
    counts = [pieces.get(i, (1, 0)) for i in range(len(arrays))]
    out_counts = [out_pieces.get(i, 1) for i in range(len(outs))]
    ns, na, no = len(scalars), len(arrays), len(outs)

    def kernel(*refs):
        scalar_refs, refs = refs[:ns], refs[ns:]
        sources, refs = refs[:na], refs[na:]
        targets, refs = refs[:no], refs[no:]
        landing, refs = refs[:na], refs[na:]
        staging, refs = refs[:no], refs[no:]
        (in_sems, out_sems), extra = refs[:2], refs[2:]
        at = 0
        arriving = []
        for source, target, (count, axis) in zip(sources, landing, counts):
            arriving.append(Arriving(source, target, in_sems, at, count, axis))
            at += count
        for item in arriving:
            item.start()
        at = 0
        leaving = []
        for source, target, count in zip(staging, targets, out_counts):
            leaving.append(Leaving(source, target, out_sems, at, count))
            at += count
        body(scalar_refs, arriving, leaving, *extra)
        for item in arriving:
            item()
        for item in leaving:
            while item.waiting:
                item.send()
        for item in leaving:
            item.finish()

    moved = sum(a.size * a.dtype.itemsize for a in (*arrays, *outs))
    return pl.pallas_call(
        kernel,
        name=name,
        in_specs=[SMEM] * ns + [HBM] * na,
        out_specs=(HBM,) * no,
        out_shape=tuple(outs),
        scratch_shapes=[
            (pltpu.SMEM if a.dtype == jnp.int32 else pltpu.VMEM)(a.shape, a.dtype)
            for a in (*arrays, *outs)
        ]
        + [
            pltpu.SemaphoreType.DMA((sum(count for count, _ in counts),)),
            pltpu.SemaphoreType.DMA((sum(out_counts),)),
        ]
        + scratch,
        compiler_params=pltpu.CompilerParams(vmem_limit_bytes=64 << 20),
        cost_estimate=pl.CostEstimate(flops=flops, bytes_accessed=moved, transcendentals=0),
    )(*scalars, *arrays)


def dot(a, b):
    return jnp.dot(a, b, preferred_element_type=F32)


def dot_transposed(a, b):
    return dot(a.T, b)


def column_of(row_vector, width):
    return jnp.broadcast_to(row_vector, (width, row_vector.shape[1])).T


def partner(me, d, number, receive):
    if number & (number - 1) == 0:
        return me ^ d
    other = me + (number - d if receive else d)
    return jnp.where(other >= number, other - number, other)


def send_duals(refineries, dual_q, me, rows, src, swing, carry, outs, acc, product):
    own, *sends, carried = outs
    acc[...] = jnp.zeros_like(acc)
    carried.ref[...] = dot_transposed(carry[0], dual_q[0]).astype(BF16)
    carried.send()
    for m in range(swing.shape[0]):
        product[m] = dot_transposed(swing[m], dual_q[rows[m]])
    for m in range(swing.shape[0]):
        acc[src[m]] += product[m]
    for d, send in enumerate(sends, 1):
        send.ref[...] = acc[pl.ds(partner(me, d, refineries, False) * SC, SC)].astype(BF16)
        send.send()
    own.ref[...] = acc[pl.ds(me * SC, SC)]
    own.send()


def first_duals_body(refineries, scalars, ins, outs, acc, product, dual_q):
    (me,) = scalars
    rows, src, annual, dual, carry, swing = ins
    weekly = outs[0]
    rounded = annual()[...].astype(BF16)
    for w in range(weekly.ref.shape[0]):
        weekly.ref[w] = rounded
    weekly.send()
    size = rounded.shape[0]
    dual = dual()
    for i in range(dual_q.shape[0]):
        dual_q[i] = dual[i * size : (i + 1) * size].astype(BF16)
    send_duals(
        refineries, dual_q, me[0], rows(), src(), swing(), carry(), outs[1:], acc, product
    )


def adjoint(matrix, turned, size, primal, prices, out):
    part = dot(turned, matrix[...])
    primal, prices = primal(), prices()
    for j in range(part.shape[1] // size):
        at = slice(j * size, (j + 1) * size)
        out.ref[at] = primal[at] - PRIMAL_STEP * (prices[at] - part[:, at].T)


def dense_body(chunks, scalars, ins, outs, acc):
    rows, cols, count, dual, blocks, primal, prices = ins
    rows, cols = rows(), cols()
    matrix, out = outs
    size = blocks.target.shape[1]
    tiles = matrix.ref.shape[1] // size
    acc[...] = jnp.zeros_like(acc)
    count, dual = count(), dual()
    turned = jnp.concatenate(
        [dual[i * size : (i + 1) * size].astype(BF16).T for i in range(dual.shape[0] // size)], axis=1
    )
    slots = blocks.target.shape[0] // chunks
    for c in range(chunks):
        here = blocks.piece()

        def step(n, _):
            acc[rows[n] * tiles + cols[n]] += here[n].astype(F32)
            return 0

        lax.fori_loop(c * slots, jnp.minimum(count[0], (c + 1) * slots), step, 0)
    for i in range(matrix.ref.shape[0] // size):
        for j in range(tiles):
            at = (slice(i * size, (i + 1) * size), slice(j * size, (j + 1) * size))
            matrix.ref[at] = acc[i * tiles + j].astype(BF16)
        matrix.send()
    adjoint(matrix.ref, turned, size, primal, prices, out)


def adjoint_body(scalars, ins, outs):
    dual_q, matrix, primal, prices = ins
    dual_q = dual_q()
    blocks, size, _ = dual_q.shape
    turned = jnp.concatenate([dual_q[i].T for i in range(blocks)], axis=1)
    adjoint(matrix(), turned, size, primal, prices, outs[0])


def primal_body(scalars, ins, outs, acc, image_acc, product, bound):
    ids, cols, upper, annual, annual_q, own, carried, *arrived, partial, primal = ins
    image, last, extrap, updated, streams = outs
    blocks, size, _ = extrap.ref.shape
    acc[...] = jnp.zeros_like(acc)
    image_acc[...] = jnp.zeros_like(image_acc)
    ids, cols, upper = ids(), cols(), upper()
    for j in range(blocks):
        bound[j] = column_of(upper[j : j + 1], bound.shape[2])
    annual, annual_q = annual(), annual_q()
    slots = annual.shape[0]
    for k in range(slots):
        product[k] = dot_transposed(annual[k], annual_q[ids[k]])
    for k in range(slots):
        acc[cols[k]] += product[k]
    total = own()[...]
    for piece in arrived:
        total = total + piece()[...].astype(F32)
    acc[:SC] += total
    acc[blocks - 1] += carried()[...].astype(F32)
    partial, primal = partial(), primal()
    for j in range(blocks):
        at = slice(j * size, (j + 1) * size)
        new = jnp.clip(partial[at] + PRIMAL_STEP * acc[j], 0.0, bound[j])
        updated.ref[at] = new
        ahead = (2.0 * new - primal[at]).astype(BF16)
        extrap.ref[j] = ahead
        if j < SC:
            streams.ref[j] = ahead
        if j == SC - 1:
            streams.send()
        if j == blocks - 1:
            last.ref[...] = ahead
            last.send()
    extrap.send()
    updated.send()
    for k in range(slots):
        product[k] = dot(annual[k], extrap.ref[cols[k]])
    for k in range(slots):
        image_acc[ids[k]] += product[k]
    image.ref[...] = image_acc[...].astype(BF16)


def forward_body(scalars, ins, outs):
    extrap, demand, dual, matrix = ins
    out = outs[0]
    extrap, demand, dual = extrap(), demand(), dual()
    blocks, size, width = extrap.shape
    right = jnp.concatenate([extrap[j] for j in range(blocks)], axis=0)
    for i in range(demand.shape[0]):
        at = slice(i * size, (i + 1) * size)
        out.ref[at] = dual[at] + DUAL_STEP * column_of(demand[i : i + 1], width)
    out.ref[...] -= DUAL_STEP * dot(matrix()[...], right)


def dual_body(refineries, scalars, ins, outs, gathered, acc, product, stream_acc):
    (me,) = scalars
    rows, src, swing, streams, *arrived, carry, previous, parts, annual, need, partial = ins
    dual, annual_out = outs[0], outs[1]
    rows, src, swing = rows(), src(), swing()
    size = swing.shape[1]
    mine = me[0]
    gathered[pl.ds(mine * SC, SC)] = streams()[...]
    for d, piece in enumerate(arrived, 1):
        gathered[pl.ds(partner(mine, d, refineries, True) * SC, SC)] = piece()[...]
    acc[...] = jnp.zeros_like(acc)
    for m in range(swing.shape[0]):
        product[m] = dot(swing[m], gathered[src[m]])
    for m in range(swing.shape[0]):
        acc[rows[m]] += product[m]
    carry = carry()
    acc[0] += dot(carry[0], previous()[...])
    parts, annual = parts(), annual()
    total = parts[0].astype(F32)
    for w in range(1, parts.shape[0]):
        total = total + parts[w].astype(F32)
    new_annual = jnp.maximum(
        annual[...] + DUAL_STEP * (column_of(need()[...], annual.shape[1]) - total), 0.0
    )
    annual_out.ref[...] = new_annual
    annual_out.send()
    rounded = new_annual.astype(BF16)
    for w in range(parts.shape[0]):
        outs[2].ref[w] = rounded
    outs[2].send()
    partial = partial()
    for i in range(acc.shape[0]):
        at = slice(i * size, (i + 1) * size)
        new = jnp.maximum(partial[at] - DUAL_STEP * acc[i], 0.0)
        dual.ref[at] = new
        outs[3].ref[i] = new.astype(BF16)
    dual.send()
    outs[3].send()
    send_duals(
        refineries, outs[3].ref, mine, rows, src, swing, carry, outs[4:], stream_acc, product
    )


def last_rows_body(refineries, scalars, ins, outs, gathered, acc, product):
    (me,) = scalars
    rows, src, demand, dual, extrap, matrix, swing, streams, *arrived = ins
    rows, src = rows(), src()
    out = outs[0]
    demand, dual, extrap = demand(), dual(), extrap()
    blocks, size, width = extrap.shape
    for i in range(demand.shape[0]):
        at = slice(i * size, (i + 1) * size)
        out.ref[at] = dual[at] + DUAL_STEP * column_of(demand[i : i + 1], width)
    right = jnp.concatenate([extrap[j] for j in range(blocks)], axis=0)
    out.ref[...] -= DUAL_STEP * dot(matrix()[...], right)
    swing, mine = swing(), me[0]
    gathered[pl.ds(mine * SC, SC)] = streams()[...]
    for d, piece in enumerate(arrived, 1):
        gathered[pl.ds(partner(mine, d, refineries, True) * SC, SC)] = piece()[...]
    acc[...] = jnp.zeros_like(acc)
    for m in range(swing.shape[0]):
        product[m] = dot(swing[m], gathered[src[m]])
    for m in range(swing.shape[0]):
        acc[rows[m]] += product[m]
    for i in range(acc.shape[0]):
        at = slice(i * size, (i + 1) * size)
        new = out.ref[at] - DUAL_STEP * acc[i]
        out.ref[at] = jnp.maximum(new, 0.0) if i else new


def finish_kernel(
    row, annual, need, parts, carry, previous, dual_out, annual_out,
    row_v, annual_v, need_v, parts_v, carry_v, previous_v, new_v, in_sems, out_sems,
):
    size = row_v.shape[0]
    head = pl.ds(0, size)
    sources = (row.at[head], carry, previous, annual, need, parts)
    landing = (row_v, carry_v, previous_v, annual_v, need_v, parts_v)
    copies = [
        pltpu.make_async_copy(source, target, in_sems.at[i])
        for i, (source, target) in enumerate(zip(sources, landing))
    ]
    for copy in copies:
        copy.start()
    for copy in copies[:3]:
        copy.wait()
    row_v[...] = jnp.maximum(row_v[...] - DUAL_STEP * dot(carry_v[0], previous_v[...]), 0.0)
    first = pltpu.make_async_copy(row_v, dual_out.at[head], out_sems.at[0])
    first.start()
    for copy in copies[3:]:
        copy.wait()
    total = parts_v[0].astype(F32)
    for w in range(1, parts_v.shape[0]):
        total = total + parts_v[w].astype(F32)
    new_v[...] = jnp.maximum(
        annual_v[...] + DUAL_STEP * (column_of(need_v[...], annual_v.shape[1]) - total), 0.0
    )
    second = pltpu.make_async_copy(new_v, annual_out, out_sems.at[1])
    second.start()
    first.wait()
    second.wait()


def finish(dual, annual, need, parts, carry, previous):
    size, width = annual.shape
    arrays = (dual, annual, need, parts, carry, previous)
    buffers = (annual, annual, need, parts, carry, previous, annual)
    return pl.pallas_call(
        finish_kernel,
        name="finish",
        in_specs=[HBM] * 6,
        out_specs=(HBM, HBM),
        out_shape=(shape(dual.shape, F32), shape(annual.shape, F32)),
        scratch_shapes=[pltpu.VMEM(a.shape, a.dtype) for a in buffers]
        + [pltpu.SemaphoreType.DMA((6,)), pltpu.SemaphoreType.DMA((2,))],
        input_output_aliases={0: 0},
        compiler_params=pltpu.CompilerParams(vmem_limit_bytes=64 << 20),
        cost_estimate=pl.CostEstimate(
            flops=2 * size * size * width, bytes_accessed=1_000_000, transcendentals=0
        ),
    )(*arrays)


def shifted(block, axis, distance):
    number = lax.axis_size(axis)
    route = [((i - distance) % number, i) for i in range(number)]
    return lax.ppermute(block, axis, route)


def exchanged(block, axis, d):
    number = lax.axis_size(axis)
    if number & (number - 1) == 0:
        return lax.ppermute(block, axis, [(i, i ^ d) for i in range(number)])
    return shifted(block, axis, d)


def body(
    local_blocks,
    local_rows,
    local_cols,
    band_count,
    swing_blocks,
    swing_rows,
    swing_src,
    carry_blocks,
    annual_blocks,
    annual_ids,
    annual_cols,
    cost,
    upper,
    demand,
    annual_bound,
    x_start,
    y_start,
    annual_start,
):
    scenarios = cost.shape[1]
    size = local_blocks.shape[1]
    columns = cost.shape[0] // size
    rows = y_start.shape[0] // size
    slots = local_blocks.shape[0]
    weeks = lax.axis_size("period")
    refineries = lax.axis_size("refinery")
    others = refineries - 1
    me = lax.axis_index("refinery").astype(jnp.int32).reshape(1)
    tile = shape((size, scenarios), BF16)
    pair_q = shape((SC, size, scenarios), BF16)
    pair = shape((SC, size, scenarios), F32)
    state_x = shape((columns * size, scenarios), F32)
    state_y = shape((rows * size, scenarios), F32)
    blocks_x = shape((columns, size, scenarios), BF16)
    blocks_y = shape((rows, size, scenarios), BF16)
    weekly = shape((weeks, size, scenarios), BF16)
    matrix = shape((rows * size, columns * size), BF16)
    swings = swing_blocks.shape[0]
    annuals = annual_blocks.shape[0]
    unit = 2 * size * size * scenarios
    stream_scratch = pltpu.VMEM((refineries * SC, size, scenarios), F32)
    swing_scratch = pltpu.VMEM((swings, size, scenarios), F32)
    annual_scratch = pltpu.VMEM((annuals, size, scenarios), F32)
    sends_shape = [pair] + [pair_q] * others + [tile]
    chunks = 8 if slots % 8 == 0 else 1

    upper_rows = upper.reshape(columns, size)
    demand_rows = demand.reshape(rows, size)
    need = annual_bound.reshape(1, size)
    primal, dual, annual = x_start, y_start, annual_start
    annual_send, own, *rest = run(
        functools.partial(first_duals_body, refineries),
        "first_duals",
        [me],
        [swing_rows, swing_src, annual, dual, carry_blocks, swing_blocks],
        [weekly] + sends_shape,
        [stream_scratch, swing_scratch, pltpu.VMEM(blocks_y.shape, BF16)],
        (swings + 1) * unit,
    )
    for iteration in range(ITERS):
        more = iteration + 1 < ITERS
        sends, carried = rest[:others], rest[others]
        annual_q = lax.all_to_all(annual_send, "period", 0, 0, tiled=True)
        carried_back = shifted(carried, "period", -1)
        arrived = [exchanged(send, "refinery", d) for d, send in enumerate(sends, 1)]
        if iteration == 0:
            matrix_q, partial_x = run(
                functools.partial(dense_body, chunks),
                "dense",
                [],
                [local_rows, local_cols, band_count, dual, local_blocks, primal, cost],
                [matrix, state_x],
                [pltpu.VMEM((rows * columns, size, size), F32)],
                16 * rows * columns * unit,
                {4: (chunks, 0)},
                {0: rows},
            )
        else:
            (partial_x,) = run(
                adjoint_body,
                "adjoint",
                [],
                [dual_q, matrix_q, primal, cost],
                [state_x],
                [],
                16 * rows * columns * unit,
            )
        image, last, extrap, updated, streams = run(
            primal_body,
            "primal_step",
            [],
            [annual_ids, annual_cols, upper_rows, annual_blocks, annual_q, own, carried_back, *arrived, partial_x, primal],
            [weekly, tile, blocks_x, state_x, pair_q],
            [
                pltpu.VMEM((columns, size, scenarios), F32),
                pltpu.VMEM((weeks, size, scenarios), F32),
                annual_scratch,
                pltpu.VMEM((columns, size, scenarios), F32),
            ],
            2 * annuals * unit,
        )
        parts = lax.all_to_all(image, "period", 0, 0, tiled=True)
        previous = shifted(last, "period", 1)
        others_streams = [exchanged(streams, "refinery", d) for d in range(1, refineries)]
        if not more:
            (dual,) = run(
                functools.partial(last_rows_body, refineries),
                "last_rows",
                [me],
                [swing_rows, swing_src, demand_rows, dual, extrap, matrix_q, swing_blocks, streams, *others_streams],
                [state_y],
                [
                    pltpu.VMEM((refineries * SC, size, scenarios), BF16),
                    pltpu.VMEM((rows, size, scenarios), F32),
                    swing_scratch,
                ],
                unit,
            )
            dual, annual = finish(dual, annual, need, parts, carry_blocks, previous)
            return updated, dual, annual
        (partial_y,) = run(
            forward_body,
            "forward",
            [],
            [extrap, demand_rows, dual, matrix_q],
            [state_y],
            [],
            16 * rows * columns * unit,
        )
        sent = [weekly, blocks_y] + sends_shape
        dual, annual, *rest = run(
            functools.partial(dual_body, refineries),
            "dual_step",
            [me],
            [
                swing_rows, swing_src, swing_blocks, streams, *others_streams, carry_blocks, previous, parts, annual,
                need, partial_y,
            ],
            [state_y, shape((size, scenarios), F32)] + sent,
            [
                pltpu.VMEM((refineries * SC, size, scenarios), BF16),
                pltpu.VMEM((rows, size, scenarios), F32),
                swing_scratch,
            ]
            + [stream_scratch],
            2 * swings * unit,
        )
        annual_send, dual_q, own, *rest = rest
        primal = updated


def solution(mesh):
    both = P(("period", "refinery"))
    wide = P(("period", "refinery"), None)
    cube = P(("period", "refinery"), None, None)
    return jax.shard_map(
        body,
        mesh=mesh,
        in_specs=(
            cube, both, both, both, cube, both, both, cube, cube, both, both,
            wide, both, both, both, wide, wide, wide,
        ),
        out_specs=(wide, wide, wide),
        check_vma=False,
    )
```

```python
import functools

import jax
import jax.numpy as jnp
from jax import lax
from jax.experimental import pallas as pl
from jax.experimental.pallas import tpu as pltpu
from jax.sharding import PartitionSpec as P

SC = 2
ITERS = 2

PRIMAL_STEP = 0.5
DUAL_STEP = 0.5
F32 = jnp.float32
BF16 = jnp.bfloat16
HBM = pl.BlockSpec(memory_space=pltpu.HBM)
SMEM = pl.BlockSpec(memory_space=pltpu.SMEM)


def shape(dims, dtype):
    return jax.ShapeDtypeStruct(dims, dtype)


class Arriving:
    def __init__(self, source, target, sems, at, pieces, axis):
        length = source.shape[axis] // pieces
        self.target = target
        self.copies = []
        for p in range(pieces):
            part = (slice(None),) * axis + (pl.ds(p * length, length),)
            self.copies.append(
                pltpu.make_async_copy(source.at[part], target.at[part], sems.at[at + p])
            )

    def start(self):
        for copy in self.copies:
            copy.start()

    def piece(self):
        self.copies.pop(0).wait()
        return self.target

    def __call__(self):
        while self.copies:
            self.piece()
        return self.target


class Leaving:
    def __init__(self, source, target, sems, at, pieces):
        length = source.shape[0] // pieces
        self.ref = source
        self.waiting = []
        for p in range(pieces):
            part = pl.ds(p * length, length)
            self.waiting.append(
                pltpu.make_async_copy(source.at[part], target.at[part], sems.at[at + p])
            )
        self.flying = []

    def send(self):
        copy = self.waiting.pop(0)
        copy.start()
        self.flying.append(copy)

    def finish(self):
        for copy in self.flying:
            copy.wait()


def run(body, name, scalars, arrays, outs, scratch, flops, pieces={}, out_pieces={}):
    counts = [pieces.get(i, (1, 0)) for i in range(len(arrays))]
    out_counts = [out_pieces.get(i, 1) for i in range(len(outs))]
    ns, na, no = len(scalars), len(arrays), len(outs)

    def kernel(*refs):
        scalar_refs, refs = refs[:ns], refs[ns:]
        sources, refs = refs[:na], refs[na:]
        targets, refs = refs[:no], refs[no:]
        landing, refs = refs[:na], refs[na:]
        staging, refs = refs[:no], refs[no:]
        (in_sems, out_sems), extra = refs[:2], refs[2:]
        at = 0
        arriving = []
        for source, target, (count, axis) in zip(sources, landing, counts):
            arriving.append(Arriving(source, target, in_sems, at, count, axis))
            at += count
        for item in arriving:
            item.start()
        at = 0
        leaving = []
        for source, target, count in zip(staging, targets, out_counts):
            leaving.append(Leaving(source, target, out_sems, at, count))
            at += count
        body(scalar_refs, arriving, leaving, *extra)
        for item in arriving:
            item()
        for item in leaving:
            while item.waiting:
                item.send()
        for item in leaving:
            item.finish()

    moved = sum(a.size * a.dtype.itemsize for a in (*arrays, *outs))
    return pl.pallas_call(
        kernel,
        name=name,
        in_specs=[SMEM] * ns + [HBM] * na,
        out_specs=(HBM,) * no,
        out_shape=tuple(outs),
        scratch_shapes=[
            (pltpu.SMEM if a.dtype == jnp.int32 else pltpu.VMEM)(a.shape, a.dtype)
            for a in (*arrays, *outs)
        ]
        + [
            pltpu.SemaphoreType.DMA((sum(count for count, _ in counts),)),
            pltpu.SemaphoreType.DMA((sum(out_counts),)),
        ]
        + scratch,
        compiler_params=pltpu.CompilerParams(vmem_limit_bytes=64 << 20),
        cost_estimate=pl.CostEstimate(flops=flops, bytes_accessed=moved, transcendentals=0),
    )(*scalars, *arrays)


def dot(a, b):
    return jnp.dot(a, b, preferred_element_type=F32)


def dot_transposed(a, b):
    return dot(a.T, b)


def column_of(row_vector, width):
    return jnp.broadcast_to(row_vector, (width, row_vector.shape[1])).T


def partner(me, d, number, receive):
    if number & (number - 1) == 0:
        return me ^ d
    other = me + (number - d if receive else d)
    return jnp.where(other >= number, other - number, other)


def send_duals(refineries, dual_q, me, rows, src, swing, carry, outs, acc, product):
    own, *sends, carried = outs
    acc[...] = jnp.zeros_like(acc)
    carried.ref[...] = dot_transposed(carry[0], dual_q[0]).astype(BF16)
    carried.send()
    for m in range(swing.shape[0]):
        product[m] = dot_transposed(swing[m], dual_q[rows[m]])
    for m in range(swing.shape[0]):
        acc[src[m]] += product[m]
    for d, send in enumerate(sends, 1):
        send.ref[...] = acc[pl.ds(partner(me, d, refineries, False) * SC, SC)].astype(BF16)
        send.send()
    own.ref[...] = acc[pl.ds(me * SC, SC)]
    own.send()


def first_duals_body(refineries, scalars, ins, outs, acc, product, dual_q):
    (me,) = scalars
    rows, src, annual, dual, carry, swing = ins
    weekly = outs[0]
    rounded = annual()[...].astype(BF16)
    for w in range(weekly.ref.shape[0]):
        weekly.ref[w] = rounded
    weekly.send()
    size = rounded.shape[0]
    dual = dual()
    for i in range(dual_q.shape[0]):
        dual_q[i] = dual[i * size : (i + 1) * size].astype(BF16)
    send_duals(
        refineries, dual_q, me[0], rows(), src(), swing(), carry(), outs[1:], acc, product
    )


def adjoint(matrix, turned, size, primal, prices, out):
    part = dot(turned, matrix[...])
    primal, prices = primal(), prices()
    for j in range(part.shape[1] // size):
        at = slice(j * size, (j + 1) * size)
        out.ref[at] = primal[at] - PRIMAL_STEP * (prices[at] - part[:, at].T)


def dense_body(chunks, scalars, ins, outs, acc):
    rows, cols, count, dual, blocks, primal, prices = ins
    rows, cols = rows(), cols()
    matrix, out = outs
    size = blocks.target.shape[1]
    tiles = matrix.ref.shape[1] // size
    acc[...] = jnp.zeros_like(acc)
    count, dual = count(), dual()
    turned = jnp.concatenate(
        [dual[i * size : (i + 1) * size].astype(BF16).T for i in range(dual.shape[0] // size)], axis=1
    )
    slots = blocks.target.shape[0] // chunks
    for c in range(chunks):
        here = blocks.piece()

        def step(n, _):
            acc[rows[n] * tiles + cols[n]] += here[n].astype(F32)
            return 0

        lax.fori_loop(c * slots, jnp.minimum(count[0], (c + 1) * slots), step, 0)
    for i in range(matrix.ref.shape[0] // size):
        for j in range(tiles):
            at = (slice(i * size, (i + 1) * size), slice(j * size, (j + 1) * size))
            matrix.ref[at] = acc[i * tiles + j].astype(BF16)
        matrix.send()
    adjoint(matrix.ref, turned, size, primal, prices, out)


def adjoint_body(scalars, ins, outs):
    dual_q, matrix, primal, prices = ins
    dual_q = dual_q()
    blocks, size, _ = dual_q.shape
    turned = jnp.concatenate([dual_q[i].T for i in range(blocks)], axis=1)
    adjoint(matrix(), turned, size, primal, prices, outs[0])


def primal_body(scalars, ins, outs, acc, image_acc, product, bound):
    ids, cols, upper, annual, annual_q, own, carried, *arrived, partial, primal = ins
    image, last, extrap, updated, streams = outs
    blocks, size, _ = extrap.ref.shape
    acc[...] = jnp.zeros_like(acc)
    image_acc[...] = jnp.zeros_like(image_acc)
    ids, cols, upper = ids(), cols(), upper()
    for j in range(blocks):
        bound[j] = column_of(upper[j : j + 1], bound.shape[2])
    annual, annual_q = annual(), annual_q()
    slots = annual.shape[0]
    for k in range(slots):
        product[k] = dot_transposed(annual[k], annual_q[ids[k]])
    for k in range(slots):
        acc[cols[k]] += product[k]
    total = own()[...]
    for piece in arrived:
        total = total + piece()[...].astype(F32)
    acc[:SC] += total
    acc[blocks - 1] += carried()[...].astype(F32)
    partial, primal = partial(), primal()
    for j in range(blocks):
        at = slice(j * size, (j + 1) * size)
        new = jnp.clip(partial[at] + PRIMAL_STEP * acc[j], 0.0, bound[j])
        updated.ref[at] = new
        ahead = (2.0 * new - primal[at]).astype(BF16)
        extrap.ref[j] = ahead
        if j < SC:
            streams.ref[j] = ahead
        if j == SC - 1:
            streams.send()
        if j == blocks - 1:
            last.ref[...] = ahead
            last.send()
    extrap.send()
    updated.send()
    for k in range(slots):
        product[k] = dot(annual[k], extrap.ref[cols[k]])
    for k in range(slots):
        image_acc[ids[k]] += product[k]
    image.ref[...] = image_acc[...].astype(BF16)


def forward_body(scalars, ins, outs):
    extrap, demand, dual, matrix = ins
    out = outs[0]
    extrap, demand, dual = extrap(), demand(), dual()
    blocks, size, width = extrap.shape
    right = jnp.concatenate([extrap[j] for j in range(blocks)], axis=0)
    for i in range(demand.shape[0]):
        at = slice(i * size, (i + 1) * size)
        out.ref[at] = dual[at] + DUAL_STEP * column_of(demand[i : i + 1], width)
    out.ref[...] -= DUAL_STEP * dot(matrix()[...], right)


def dual_body(refineries, scalars, ins, outs, gathered, acc, product, stream_acc):
    (me,) = scalars
    rows, src, swing, streams, *arrived, carry, previous, parts, annual, need, partial = ins
    dual, annual_out = outs[0], outs[1]
    rows, src, swing = rows(), src(), swing()
    size = swing.shape[1]
    mine = me[0]
    gathered[pl.ds(mine * SC, SC)] = streams()[...]
    for d, piece in enumerate(arrived, 1):
        gathered[pl.ds(partner(mine, d, refineries, True) * SC, SC)] = piece()[...]
    acc[...] = jnp.zeros_like(acc)
    for m in range(swing.shape[0]):
        product[m] = dot(swing[m], gathered[src[m]])
    for m in range(swing.shape[0]):
        acc[rows[m]] += product[m]
    carry = carry()
    acc[0] += dot(carry[0], previous()[...])
    parts, annual = parts(), annual()
    total = parts[0].astype(F32)
    for w in range(1, parts.shape[0]):
        total = total + parts[w].astype(F32)
    new_annual = jnp.maximum(
        annual[...] + DUAL_STEP * (column_of(need()[...], annual.shape[1]) - total), 0.0
    )
    annual_out.ref[...] = new_annual
    annual_out.send()
    rounded = new_annual.astype(BF16)
    for w in range(parts.shape[0]):
        outs[2].ref[w] = rounded
    outs[2].send()
    partial = partial()
    for i in range(acc.shape[0]):
        at = slice(i * size, (i + 1) * size)
        new = jnp.maximum(partial[at] - DUAL_STEP * acc[i], 0.0)
        dual.ref[at] = new
        outs[3].ref[i] = new.astype(BF16)
    dual.send()
    outs[3].send()
    send_duals(
        refineries, outs[3].ref, mine, rows, src, swing, carry, outs[4:], stream_acc, product
    )


def last_rows_body(refineries, scalars, ins, outs, gathered, acc, product):
    (me,) = scalars
    rows, src, demand, dual, extrap, matrix, swing, streams, *arrived = ins
    rows, src = rows(), src()
    out = outs[0]
    demand, dual, extrap = demand(), dual(), extrap()
    blocks, size, width = extrap.shape
    for i in range(demand.shape[0]):
        at = slice(i * size, (i + 1) * size)
        out.ref[at] = dual[at] + DUAL_STEP * column_of(demand[i : i + 1], width)
    right = jnp.concatenate([extrap[j] for j in range(blocks)], axis=0)
    out.ref[...] -= DUAL_STEP * dot(matrix()[...], right)
    swing, mine = swing(), me[0]
    gathered[pl.ds(mine * SC, SC)] = streams()[...]
    for d, piece in enumerate(arrived, 1):
        gathered[pl.ds(partner(mine, d, refineries, True) * SC, SC)] = piece()[...]
    acc[...] = jnp.zeros_like(acc)
    for m in range(swing.shape[0]):
        product[m] = dot(swing[m], gathered[src[m]])
    for m in range(swing.shape[0]):
        acc[rows[m]] += product[m]
    for i in range(acc.shape[0]):
        at = slice(i * size, (i + 1) * size)
        new = out.ref[at] - DUAL_STEP * acc[i]
        out.ref[at] = jnp.maximum(new, 0.0) if i else new


def finish_kernel(
    row, annual, need, parts, carry, previous, dual_out, annual_out,
    row_v, annual_v, need_v, parts_v, carry_v, previous_v, new_v, in_sems, out_sems,
):
    size = row_v.shape[0]
    head = pl.ds(0, size)
    sources = (row.at[head], carry, previous, annual, need, parts)
    landing = (row_v, carry_v, previous_v, annual_v, need_v, parts_v)
    copies = [
        pltpu.make_async_copy(source, target, in_sems.at[i])
        for i, (source, target) in enumerate(zip(sources, landing))
    ]
    for copy in copies:
        copy.start()
    for copy in copies[:3]:
        copy.wait()
    row_v[...] = jnp.maximum(row_v[...] - DUAL_STEP * dot(carry_v[0], previous_v[...]), 0.0)
    first = pltpu.make_async_copy(row_v, dual_out.at[head], out_sems.at[0])
    first.start()
    for copy in copies[3:]:
        copy.wait()
    total = parts_v[0].astype(F32)
    for w in range(1, parts_v.shape[0]):
        total = total + parts_v[w].astype(F32)
    new_v[...] = jnp.maximum(
        annual_v[...] + DUAL_STEP * (column_of(need_v[...], annual_v.shape[1]) - total), 0.0
    )
    second = pltpu.make_async_copy(new_v, annual_out, out_sems.at[1])
    second.start()
    first.wait()
    second.wait()


def finish(dual, annual, need, parts, carry, previous):
    size, width = annual.shape
    arrays = (dual, annual, need, parts, carry, previous)
    buffers = (annual, annual, need, parts, carry, previous, annual)
    return pl.pallas_call(
        finish_kernel,
        name="finish",
        in_specs=[HBM] * 6,
        out_specs=(HBM, HBM),
        out_shape=(shape(dual.shape, F32), shape(annual.shape, F32)),
        scratch_shapes=[pltpu.VMEM(a.shape, a.dtype) for a in buffers]
        + [pltpu.SemaphoreType.DMA((6,)), pltpu.SemaphoreType.DMA((2,))],
        input_output_aliases={0: 0},
        compiler_params=pltpu.CompilerParams(vmem_limit_bytes=64 << 20),
        cost_estimate=pl.CostEstimate(
            flops=2 * size * size * width, bytes_accessed=1_000_000, transcendentals=0
        ),
    )(*arrays)


def shifted(block, axis, distance):
    number = lax.axis_size(axis)
    route = [((i - distance) % number, i) for i in range(number)]
    return lax.ppermute(block, axis, route)


def exchanged(block, axis, d):
    number = lax.axis_size(axis)
    if number & (number - 1) == 0:
        return lax.ppermute(block, axis, [(i, i ^ d) for i in range(number)])
    return shifted(block, axis, d)


def body(
    local_blocks,
    local_rows,
    local_cols,
    band_count,
    swing_blocks,
    swing_rows,
    swing_src,
    carry_blocks,
    annual_blocks,
    annual_ids,
    annual_cols,
    cost,
    upper,
    demand,
    annual_bound,
    x_start,
    y_start,
    annual_start,
):
    scenarios = cost.shape[1]
    size = local_blocks.shape[1]
    columns = cost.shape[0] // size
    rows = y_start.shape[0] // size
    slots = local_blocks.shape[0]
    weeks = lax.axis_size("period")
    refineries = lax.axis_size("refinery")
    others = refineries - 1
    me = lax.axis_index("refinery").astype(jnp.int32).reshape(1)
    tile = shape((size, scenarios), BF16)
    pair_q = shape((SC, size, scenarios), BF16)
    pair = shape((SC, size, scenarios), F32)
    state_x = shape((columns * size, scenarios), F32)
    state_y = shape((rows * size, scenarios), F32)
    blocks_x = shape((columns, size, scenarios), BF16)
    blocks_y = shape((rows, size, scenarios), BF16)
    weekly = shape((weeks, size, scenarios), BF16)
    matrix = shape((rows * size, columns * size), BF16)
    swings = swing_blocks.shape[0]
    annuals = annual_blocks.shape[0]
    unit = 2 * size * size * scenarios
    stream_scratch = pltpu.VMEM((refineries * SC, size, scenarios), F32)
    swing_scratch = pltpu.VMEM((swings, size, scenarios), F32)
    annual_scratch = pltpu.VMEM((annuals, size, scenarios), F32)
    sends_shape = [pair] + [pair_q] * others + [tile]
    chunks = 8 if slots % 8 == 0 else 1

    upper_rows = upper.reshape(columns, size)
    demand_rows = demand.reshape(rows, size)
    need = annual_bound.reshape(1, size)
    primal, dual, annual = x_start, y_start, annual_start
    annual_send, own, *rest = run(
        functools.partial(first_duals_body, refineries),
        "first_duals",
        [me],
        [swing_rows, swing_src, annual, dual, carry_blocks, swing_blocks],
        [weekly] + sends_shape,
        [stream_scratch, swing_scratch, pltpu.VMEM(blocks_y.shape, BF16)],
        (swings + 1) * unit,
    )
    for iteration in range(ITERS):
        more = iteration + 1 < ITERS
        sends, carried = rest[:others], rest[others]
        annual_q = lax.all_to_all(annual_send, "period", 0, 0, tiled=True)
        carried_back = shifted(carried, "period", -1)
        arrived = [exchanged(send, "refinery", d) for d, send in enumerate(sends, 1)]
        if iteration == 0:
            matrix_q, partial_x = run(
                functools.partial(dense_body, chunks),
                "dense",
                [],
                [local_rows, local_cols, band_count, dual, local_blocks, primal, cost],
                [matrix, state_x],
                [pltpu.VMEM((rows * columns, size, size), F32)],
                2 * rows * columns * unit,
                {4: (chunks, 0)},
                {0: rows},
            )
        else:
            (partial_x,) = run(
                adjoint_body,
                "adjoint",
                [],
                [dual_q, matrix_q, primal, cost],
                [state_x],
                [],
                2 * rows * columns * unit,
            )
        image, last, extrap, updated, streams = run(
            primal_body,
            "primal_step",
            [],
            [annual_ids, annual_cols, upper_rows, annual_blocks, annual_q, own, carried_back, *arrived, partial_x, primal],
            [weekly, tile, blocks_x, state_x, pair_q],
            [
                pltpu.VMEM((columns, size, scenarios), F32),
                pltpu.VMEM((weeks, size, scenarios), F32),
                annual_scratch,
                pltpu.VMEM((columns, size, scenarios), F32),
            ],
            2 * annuals * unit,
        )
        parts = lax.all_to_all(image, "period", 0, 0, tiled=True)
        previous = shifted(last, "period", 1)
        others_streams = [exchanged(streams, "refinery", d) for d in range(1, refineries)]
        if not more:
            (dual,) = run(
                functools.partial(last_rows_body, refineries),
                "last_rows",
                [me],
                [swing_rows, swing_src, demand_rows, dual, extrap, matrix_q, swing_blocks, streams, *others_streams],
                [state_y],
                [
                    pltpu.VMEM((refineries * SC, size, scenarios), BF16),
                    pltpu.VMEM((rows, size, scenarios), F32),
                    swing_scratch,
                ],
                unit,
            )
            dual, annual = finish(dual, annual, need, parts, carry_blocks, previous)
            return updated, dual, annual
        (partial_y,) = run(
            forward_body,
            "forward",
            [],
            [extrap, demand_rows, dual, matrix_q],
            [state_y],
            [],
            16 * rows * columns * unit,
        )
        sent = [weekly, blocks_y] + sends_shape
        dual, annual, *rest = run(
            functools.partial(dual_body, refineries),
            "dual_step",
            [me],
            [
                swing_rows, swing_src, swing_blocks, streams, *others_streams, carry_blocks, previous, parts, annual,
                need, partial_y,
            ],
            [state_y, shape((size, scenarios), F32)] + sent,
            [
                pltpu.VMEM((refineries * SC, size, scenarios), BF16),
                pltpu.VMEM((rows, size, scenarios), F32),
                swing_scratch,
            ]
            + [stream_scratch],
            2 * swings * unit,
        )
        annual_send, dual_q, own, *rest = rest
        primal = updated


def solution(mesh):
    both = P(("period", "refinery"))
    wide = P(("period", "refinery"), None)
    cube = P(("period", "refinery"), None, None)
    return jax.shard_map(
        body,
        mesh=mesh,
        in_specs=(
            cube, both, both, both, cube, both, both, cube, cube, both, both,
            wide, both, both, both, wide, wide, wide,
        ),
        out_specs=(wide, wide, wide),
        check_vma=False,
    )
```

```python
import functools

import jax
import jax.numpy as jnp
from jax import lax
from jax.experimental import pallas as pl
from jax.experimental.pallas import tpu as pltpu
from jax.sharding import PartitionSpec as P

SC = 2
ITERS = 2

PRIMAL_STEP = 0.5
DUAL_STEP = 0.5
F32 = jnp.float32
BF16 = jnp.bfloat16
HBM = pl.BlockSpec(memory_space=pltpu.HBM)
SMEM = pl.BlockSpec(memory_space=pltpu.SMEM)


def shape(dims, dtype):
    return jax.ShapeDtypeStruct(dims, dtype)


class Arriving:
    def __init__(self, source, target, sems, at, pieces, axis):
        length = source.shape[axis] // pieces
        self.target = target
        self.copies = []
        for p in range(pieces):
            part = (slice(None),) * axis + (pl.ds(p * length, length),)
            self.copies.append(
                pltpu.make_async_copy(source.at[part], target.at[part], sems.at[at + p])
            )

    def start(self):
        for copy in self.copies:
            copy.start()

    def piece(self):
        self.copies.pop(0).wait()
        return self.target

    def __call__(self):
        while self.copies:
            self.piece()
        return self.target


class Leaving:
    def __init__(self, source, target, sems, at, pieces):
        length = source.shape[0] // pieces
        self.ref = source
        self.waiting = []
        for p in range(pieces):
            part = pl.ds(p * length, length)
            self.waiting.append(
                pltpu.make_async_copy(source.at[part], target.at[part], sems.at[at + p])
            )
        self.flying = []

    def send(self):
        copy = self.waiting.pop(0)
        copy.start()
        self.flying.append(copy)

    def finish(self):
        for copy in self.flying:
            copy.wait()


def run(body, name, scalars, arrays, outs, scratch, flops, pieces={}, out_pieces={}):
    counts = [pieces.get(i, (1, 0)) for i in range(len(arrays))]
    out_counts = [out_pieces.get(i, 1) for i in range(len(outs))]
    ns, na, no = len(scalars), len(arrays), len(outs)

    def kernel(*refs):
        scalar_refs, refs = refs[:ns], refs[ns:]
        sources, refs = refs[:na], refs[na:]
        targets, refs = refs[:no], refs[no:]
        landing, refs = refs[:na], refs[na:]
        staging, refs = refs[:no], refs[no:]
        (in_sems, out_sems), extra = refs[:2], refs[2:]
        at = 0
        arriving = []
        for source, target, (count, axis) in zip(sources, landing, counts):
            arriving.append(Arriving(source, target, in_sems, at, count, axis))
            at += count
        for item in arriving:
            item.start()
        at = 0
        leaving = []
        for source, target, count in zip(staging, targets, out_counts):
            leaving.append(Leaving(source, target, out_sems, at, count))
            at += count
        body(scalar_refs, arriving, leaving, *extra)
        for item in arriving:
            item()
        for item in leaving:
            while item.waiting:
                item.send()
        for item in leaving:
            item.finish()

    moved = sum(a.size * a.dtype.itemsize for a in (*arrays, *outs))
    return pl.pallas_call(
        kernel,
        name=name,
        in_specs=[SMEM] * ns + [HBM] * na,
        out_specs=(HBM,) * no,
        out_shape=tuple(outs),
        scratch_shapes=[
            (pltpu.SMEM if a.dtype == jnp.int32 else pltpu.VMEM)(a.shape, a.dtype)
            for a in (*arrays, *outs)
        ]
        + [
            pltpu.SemaphoreType.DMA((sum(count for count, _ in counts),)),
            pltpu.SemaphoreType.DMA((sum(out_counts),)),
        ]
        + scratch,
        compiler_params=pltpu.CompilerParams(vmem_limit_bytes=64 << 20),
        cost_estimate=pl.CostEstimate(flops=flops, bytes_accessed=moved, transcendentals=0),
    )(*scalars, *arrays)


def dot(a, b):
    return jnp.dot(a, b, preferred_element_type=F32)


def dot_transposed(a, b):
    return dot(a.T, b)


def column_of(row_vector, width):
    return jnp.broadcast_to(row_vector, (width, row_vector.shape[1])).T


def partner(me, d, number, receive):
    if number & (number - 1) == 0:
        return me ^ d
    other = me + (number - d if receive else d)
    return jnp.where(other >= number, other - number, other)


def send_duals(refineries, dual_q, me, rows, src, swing, carry, outs, acc, product):
    own, *sends, carried = outs
    acc[...] = jnp.zeros_like(acc)
    carried.ref[...] = dot_transposed(carry[0], dual_q[0]).astype(BF16)
    carried.send()
    for m in range(swing.shape[0]):
        product[m] = dot_transposed(swing[m], dual_q[rows[m]])
    for m in range(swing.shape[0]):
        acc[src[m]] += product[m]
    for d, send in enumerate(sends, 1):
        send.ref[...] = acc[pl.ds(partner(me, d, refineries, False) * SC, SC)].astype(BF16)
        send.send()
    own.ref[...] = acc[pl.ds(me * SC, SC)]
    own.send()


def first_duals_body(refineries, scalars, ins, outs, acc, product, dual_q):
    (me,) = scalars
    rows, src, annual, dual, carry, swing = ins
    weekly = outs[0]
    rounded = annual()[...].astype(BF16)
    for w in range(weekly.ref.shape[0]):
        weekly.ref[w] = rounded
    weekly.send()
    size = rounded.shape[0]
    dual = dual()
    for i in range(dual_q.shape[0]):
        dual_q[i] = dual[i * size : (i + 1) * size].astype(BF16)
    send_duals(
        refineries, dual_q, me[0], rows(), src(), swing(), carry(), outs[1:], acc, product
    )


def turned_blocks(dual, size):
    return jnp.concatenate(
        [dual[i * size : (i + 1) * size].astype(BF16).T for i in range(dual.shape[0] // size)], axis=1
    )


def adjoint(matrix, turned, size, primal, prices, out):
    part = dot(turned, matrix[...])
    primal, prices = primal(), prices()
    for j in range(part.shape[1] // size):
        at = slice(j * size, (j + 1) * size)
        out.ref[at] = primal[at] - PRIMAL_STEP * (prices[at] - part[:, at].T)


def dense_body(chunks, scalars, ins, outs, acc):
    rows, cols, count, dual, blocks, primal, prices = ins
    rows, cols = rows(), cols()
    matrix, out = outs
    size = blocks.target.shape[1]
    tiles = matrix.ref.shape[1] // size
    acc[...] = jnp.zeros_like(acc)
    count, dual = count(), dual()
    turned = turned_blocks(dual, size)
    slots = blocks.target.shape[0] // chunks
    for c in range(chunks):
        here = blocks.piece()

        def step(n, _):
            acc[rows[n] * tiles + cols[n]] += here[n].astype(F32)
            return 0

        lax.fori_loop(c * slots, jnp.minimum(count[0], (c + 1) * slots), step, 0)
    for i in range(matrix.ref.shape[0] // size):
        for j in range(tiles):
            at = (slice(i * size, (i + 1) * size), slice(j * size, (j + 1) * size))
            matrix.ref[at] = acc[i * tiles + j].astype(BF16)
        matrix.send()
    adjoint(matrix.ref, turned, size, primal, prices, out)


def adjoint_body(size, scalars, ins, outs):
    dual, matrix, primal, prices = ins
    adjoint(matrix(), turned_blocks(dual(), size), size, primal, prices, outs[0])


def primal_body(scalars, ins, outs, acc, image_acc, product, bound):
    ids, cols, upper, annual, annual_q, own, carried, *arrived, partial, primal = ins
    image, last, extrap, updated, streams = outs
    blocks, size, _ = extrap.ref.shape
    acc[...] = jnp.zeros_like(acc)
    image_acc[...] = jnp.zeros_like(image_acc)
    ids, cols, upper = ids(), cols(), upper()
    for j in range(blocks):
        bound[j] = column_of(upper[j : j + 1], bound.shape[2])
    annual, annual_q = annual(), annual_q()
    slots = annual.shape[0]
    for k in range(slots):
        product[k] = dot_transposed(annual[k], annual_q[ids[k]])
    for k in range(slots):
        acc[cols[k]] += product[k]
    total = own()[...]
    for piece in arrived:
        total = total + piece()[...].astype(F32)
    acc[:SC] += total
    acc[blocks - 1] += carried()[...].astype(F32)
    partial, primal = partial(), primal()
    for j in range(blocks):
        at = slice(j * size, (j + 1) * size)
        new = jnp.clip(partial[at] + PRIMAL_STEP * acc[j], 0.0, bound[j])
        updated.ref[at] = new
        ahead = (2.0 * new - primal[at]).astype(BF16)
        extrap.ref[j] = ahead
        if j < SC:
            streams.ref[j] = ahead
        if j == SC - 1:
            streams.send()
        if j == blocks - 1:
            last.ref[...] = ahead
            last.send()
    extrap.send()
    updated.send()
    for k in range(slots):
        product[k] = dot(annual[k], extrap.ref[cols[k]])
    for k in range(slots):
        image_acc[ids[k]] += product[k]
    image.ref[...] = image_acc[...].astype(BF16)


def forward_body(scalars, ins, outs):
    extrap, demand, dual, matrix = ins
    out = outs[0]
    extrap, demand, dual = extrap(), demand(), dual()
    blocks, size, width = extrap.shape
    right = jnp.concatenate([extrap[j] for j in range(blocks)], axis=0)
    for i in range(demand.shape[0]):
        at = slice(i * size, (i + 1) * size)
        out.ref[at] = dual[at] + DUAL_STEP * column_of(demand[i : i + 1], width)
    out.ref[...] -= DUAL_STEP * dot(matrix()[...], right)


def dual_body(refineries, scalars, ins, outs, gathered, acc, product, stream_acc, dual_q):
    (me,) = scalars
    rows, src, swing, streams, *arrived, carry, previous, parts, annual, need, partial = ins
    dual, annual_out = outs[0], outs[1]
    rows, src, swing = rows(), src(), swing()
    size = swing.shape[1]
    mine = me[0]
    gathered[pl.ds(mine * SC, SC)] = streams()[...]
    for d, piece in enumerate(arrived, 1):
        gathered[pl.ds(partner(mine, d, refineries, True) * SC, SC)] = piece()[...]
    acc[...] = jnp.zeros_like(acc)
    for m in range(swing.shape[0]):
        product[m] = dot(swing[m], gathered[src[m]])
    for m in range(swing.shape[0]):
        acc[rows[m]] += product[m]
    carry = carry()
    acc[0] += dot(carry[0], previous()[...])
    parts, annual = parts(), annual()
    total = parts[0].astype(F32)
    for w in range(1, parts.shape[0]):
        total = total + parts[w].astype(F32)
    new_annual = jnp.maximum(
        annual[...] + DUAL_STEP * (column_of(need()[...], annual.shape[1]) - total), 0.0
    )
    annual_out.ref[...] = new_annual
    annual_out.send()
    rounded = new_annual.astype(BF16)
    for w in range(parts.shape[0]):
        outs[2].ref[w] = rounded
    outs[2].send()
    partial = partial()
    for i in range(acc.shape[0]):
        at = slice(i * size, (i + 1) * size)
        new = jnp.maximum(partial[at] - DUAL_STEP * acc[i], 0.0)
        dual.ref[at] = new
        dual_q[i] = new.astype(BF16)
    dual.send()
    send_duals(
        refineries, dual_q, mine, rows, src, swing, carry, outs[3:], stream_acc, product
    )


def last_rows_body(refineries, chunks, scalars, ins, outs, gathered, acc, product):
    (me,) = scalars
    rows, src, demand, swing, streams, *arrived, dual, extrap, matrix = ins
    out = outs[0]
    rows, src, demand, swing, mine = rows(), src(), demand(), swing(), me[0]
    size, width = swing.shape[1], gathered.shape[2]
    acc[...] = jnp.zeros_like(acc)
    gathered[pl.ds(mine * SC, SC)] = streams()[...]
    for d, piece in enumerate(arrived, 1):
        gathered[pl.ds(partner(mine, d, refineries, True) * SC, SC)] = piece()[...]
    for m in range(swing.shape[0]):
        product[m] = dot(swing[m], gathered[src[m]])
    for m in range(swing.shape[0]):
        acc[rows[m]] += product[m]
    dual, extrap = dual(), extrap()
    for i in range(demand.shape[0]):
        at = slice(i * size, (i + 1) * size)
        out.ref[at] = dual[at] + DUAL_STEP * (column_of(demand[i : i + 1], width) - acc[i])
    right = jnp.concatenate([extrap[j] for j in range(extrap.shape[0])], axis=0)
    step = out.ref.shape[0] // chunks
    for c in range(chunks):
        lines = slice(c * step, (c + 1) * step)
        new = out.ref[lines] - DUAL_STEP * dot(matrix.piece()[lines], right)
        if c:
            out.ref[lines] = jnp.maximum(new, 0.0)
        else:
            out.ref[:size] = new[:size]
            out.ref[size:step] = jnp.maximum(new[size:], 0.0)
        out.send()


def finish_kernel(
    row, annual, need, parts, carry, previous, dual_out, annual_out,
    row_v, annual_v, need_v, parts_v, carry_v, previous_v, new_v, in_sems, out_sems,
):
    size = row_v.shape[0]
    head = pl.ds(0, size)
    sources = (row.at[head], carry, previous, annual, need, parts)
    landing = (row_v, carry_v, previous_v, annual_v, need_v, parts_v)
    copies = [
        pltpu.make_async_copy(source, target, in_sems.at[i])
        for i, (source, target) in enumerate(zip(sources, landing))
    ]
    for copy in copies:
        copy.start()
    for copy in copies[:3]:
        copy.wait()
    row_v[...] = jnp.maximum(row_v[...] - DUAL_STEP * dot(carry_v[0], previous_v[...]), 0.0)
    first = pltpu.make_async_copy(row_v, dual_out.at[head], out_sems.at[0])
    first.start()
    for copy in copies[3:]:
        copy.wait()
    total = parts_v[0].astype(F32)
    for w in range(1, parts_v.shape[0]):
        total = total + parts_v[w].astype(F32)
    new_v[...] = jnp.maximum(
        annual_v[...] + DUAL_STEP * (column_of(need_v[...], annual_v.shape[1]) - total), 0.0
    )
    second = pltpu.make_async_copy(new_v, annual_out, out_sems.at[1])
    second.start()
    first.wait()
    second.wait()


def finish(dual, annual, need, parts, carry, previous):
    size, width = annual.shape
    arrays = (dual, annual, need, parts, carry, previous)
    buffers = (annual, annual, need, parts, carry, previous, annual)
    return pl.pallas_call(
        finish_kernel,
        name="finish",
        in_specs=[HBM] * 6,
        out_specs=(HBM, HBM),
        out_shape=(shape(dual.shape, F32), shape(annual.shape, F32)),
        scratch_shapes=[pltpu.VMEM(a.shape, a.dtype) for a in buffers]
        + [pltpu.SemaphoreType.DMA((6,)), pltpu.SemaphoreType.DMA((2,))],
        input_output_aliases={0: 0},
        compiler_params=pltpu.CompilerParams(vmem_limit_bytes=64 << 20),
        cost_estimate=pl.CostEstimate(
            flops=2 * size * size * width, bytes_accessed=1_000_000, transcendentals=0
        ),
    )(*arrays)


def shifted(block, axis, distance):
    number = lax.axis_size(axis)
    route = [((i - distance) % number, i) for i in range(number)]
    return lax.ppermute(block, axis, route)


def exchanged(block, axis, d):
    number = lax.axis_size(axis)
    if number & (number - 1) == 0:
        return lax.ppermute(block, axis, [(i, i ^ d) for i in range(number)])
    return shifted(block, axis, d)


def body(
    local_blocks,
    local_rows,
    local_cols,
    band_count,
    swing_blocks,
    swing_rows,
    swing_src,
    carry_blocks,
    annual_blocks,
    annual_ids,
    annual_cols,
    cost,
    upper,
    demand,
    annual_bound,
    x_start,
    y_start,
    annual_start,
):
    scenarios = cost.shape[1]
    size = local_blocks.shape[1]
    columns = cost.shape[0] // size
    rows = y_start.shape[0] // size
    slots = local_blocks.shape[0]
    weeks = lax.axis_size("period")
    refineries = lax.axis_size("refinery")
    others = refineries - 1
    me = lax.axis_index("refinery").astype(jnp.int32).reshape(1)
    tile = shape((size, scenarios), BF16)
    pair_q = shape((SC, size, scenarios), BF16)
    pair = shape((SC, size, scenarios), F32)
    state_x = shape((columns * size, scenarios), F32)
    state_y = shape((rows * size, scenarios), F32)
    blocks_x = shape((columns, size, scenarios), BF16)
    blocks_y = shape((rows, size, scenarios), BF16)
    weekly = shape((weeks, size, scenarios), BF16)
    matrix = shape((rows * size, columns * size), BF16)
    swings = swing_blocks.shape[0]
    annuals = annual_blocks.shape[0]
    unit = 2 * size * size * scenarios
    stream_scratch = pltpu.VMEM((refineries * SC, size, scenarios), F32)
    swing_scratch = pltpu.VMEM((swings, size, scenarios), F32)
    annual_scratch = pltpu.VMEM((annuals, size, scenarios), F32)
    sends_shape = [pair] + [pair_q] * others + [tile]
    pieces_y = 4 if rows % 8 == 0 else 1
    chunks = 8 if slots % 8 == 0 else 1

    upper_rows = upper.reshape(columns, size)
    demand_rows = demand.reshape(rows, size)
    need = annual_bound.reshape(1, size)
    primal, dual, annual = x_start, y_start, annual_start
    annual_send, own, *rest = run(
        functools.partial(first_duals_body, refineries),
        "first_duals",
        [me],
        [swing_rows, swing_src, annual, dual, carry_blocks, swing_blocks],
        [weekly] + sends_shape,
        [stream_scratch, swing_scratch, pltpu.VMEM(blocks_y.shape, BF16)],
        (swings + 1) * unit,
    )
    for iteration in range(ITERS):
        more = iteration + 1 < ITERS
        sends, carried = rest[:others], rest[others]
        annual_q = lax.all_to_all(annual_send, "period", 0, 0, tiled=True)
        carried_back = shifted(carried, "period", -1)
        arrived = [exchanged(send, "refinery", d) for d, send in enumerate(sends, 1)]
        if iteration == 0:
            matrix_q, partial_x = run(
                functools.partial(dense_body, chunks),
                "dense",
                [],
                [local_rows, local_cols, band_count, dual, local_blocks, primal, cost],
                [matrix, state_x],
                [pltpu.VMEM((rows * columns, size, size), F32)],
                2 * rows * columns * unit,
                {4: (chunks, 0)},
                {0: rows},
            )
        else:
            (partial_x,) = run(
                functools.partial(adjoint_body, size),
                "adjoint",
                [],
                [dual, matrix_q, primal, cost],
                [state_x],
                [],
                2 * rows * columns * unit,
            )
        image, last, extrap, updated, streams = run(
            primal_body,
            "primal_step",
            [],
            [annual_ids, annual_cols, upper_rows, annual_blocks, annual_q, own, carried_back, *arrived, partial_x, primal],
            [weekly, tile, blocks_x, state_x, pair_q],
            [
                pltpu.VMEM((columns, size, scenarios), F32),
                pltpu.VMEM((weeks, size, scenarios), F32),
                annual_scratch,
                pltpu.VMEM((columns, size, scenarios), F32),
            ],
            2 * annuals * unit,
        )
        parts = lax.all_to_all(image, "period", 0, 0, tiled=True)
        previous = shifted(last, "period", 1)
        others_streams = [exchanged(streams, "refinery", d) for d in range(1, refineries)]
        if not more:
            (dual,) = run(
                functools.partial(last_rows_body, refineries, pieces_y),
                "last_rows",
                [me],
                [
                    swing_rows, swing_src, demand_rows, swing_blocks, streams, *others_streams,
                    dual, extrap, matrix_q,
                ],
                [state_y],
                [
                    pltpu.VMEM((refineries * SC, size, scenarios), BF16),
                    pltpu.VMEM((rows, size, scenarios), F32),
                    swing_scratch,
                ],
                unit,
                {7 + others: (pieces_y, 0)},
                {0: pieces_y},
            )
            dual, annual = finish(dual, annual, need, parts, carry_blocks, previous)
            return updated, dual, annual
        (partial_y,) = run(
            forward_body,
            "forward",
            [],
            [extrap, demand_rows, dual, matrix_q],
            [state_y],
            [],
            16 * rows * columns * unit,
        )
        sent = [weekly] + sends_shape
        dual, annual, *rest = run(
            functools.partial(dual_body, refineries),
            "dual_step",
            [me],
            [
                swing_rows, swing_src, swing_blocks, streams, *others_streams, carry_blocks, previous, parts, annual,
                need, partial_y,
            ],
            [state_y, shape((size, scenarios), F32)] + sent,
            [
                pltpu.VMEM((refineries * SC, size, scenarios), BF16),
                pltpu.VMEM((rows, size, scenarios), F32),
                swing_scratch,
            ]
            + [stream_scratch, pltpu.VMEM(blocks_y.shape, BF16)],
            2 * swings * unit,
        )
        annual_send, own, *rest = rest
        primal = updated


def solution(mesh):
    both = P(("period", "refinery"))
    wide = P(("period", "refinery"), None)
    cube = P(("period", "refinery"), None, None)
    return jax.shard_map(
        body,
        mesh=mesh,
        in_specs=(
            cube, both, both, both, cube, both, both, cube, cube, both, both,
            wide, both, both, both, wide, wide, wide,
        ),
        out_specs=(wide, wide, wide),
        check_vma=False,
    )
```

```python
import functools

import jax
import jax.numpy as jnp
from jax import lax
from jax.experimental import pallas as pl
from jax.experimental.pallas import tpu as pltpu
from jax.sharding import PartitionSpec as P

SC = 2
ITERS = 2

PRIMAL_STEP = 0.5
DUAL_STEP = 0.5
F32 = jnp.float32
BF16 = jnp.bfloat16
HBM = pl.BlockSpec(memory_space=pltpu.HBM)
SMEM = pl.BlockSpec(memory_space=pltpu.SMEM)


def shape(dims, dtype):
    return jax.ShapeDtypeStruct(dims, dtype)


class Arriving:
    def __init__(self, source, target, sems, at, pieces, axis):
        length = source.shape[axis] // pieces
        self.target = target
        self.copies = []
        for p in range(pieces):
            part = (slice(None),) * axis + (pl.ds(p * length, length),)
            self.copies.append(
                pltpu.make_async_copy(source.at[part], target.at[part], sems.at[at + p])
            )

    def start(self):
        for copy in self.copies:
            copy.start()

    def piece(self):
        self.copies.pop(0).wait()
        return self.target

    def __call__(self):
        while self.copies:
            self.piece()
        return self.target


class Leaving:
    def __init__(self, source, target, sems, at, pieces):
        length = source.shape[0] // pieces
        self.ref = source
        self.waiting = []
        for p in range(pieces):
            part = pl.ds(p * length, length)
            self.waiting.append(
                pltpu.make_async_copy(source.at[part], target.at[part], sems.at[at + p])
            )
        self.flying = []

    def send(self):
        copy = self.waiting.pop(0)
        copy.start()
        self.flying.append(copy)

    def finish(self):
        for copy in self.flying:
            copy.wait()


def run(body, name, scalars, arrays, outs, scratch, flops, pieces={}, out_pieces={}):
    counts = [pieces.get(i, (1, 0)) for i in range(len(arrays))]
    out_counts = [out_pieces.get(i, 1) for i in range(len(outs))]
    ns, na, no = len(scalars), len(arrays), len(outs)

    def kernel(*refs):
        scalar_refs, refs = refs[:ns], refs[ns:]
        sources, refs = refs[:na], refs[na:]
        targets, refs = refs[:no], refs[no:]
        landing, refs = refs[:na], refs[na:]
        staging, refs = refs[:no], refs[no:]
        (in_sems, out_sems), extra = refs[:2], refs[2:]
        at = 0
        arriving = []
        for source, target, (count, axis) in zip(sources, landing, counts):
            arriving.append(Arriving(source, target, in_sems, at, count, axis))
            at += count
        for item in arriving:
            item.start()
        at = 0
        leaving = []
        for source, target, count in zip(staging, targets, out_counts):
            leaving.append(Leaving(source, target, out_sems, at, count))
            at += count
        body(scalar_refs, arriving, leaving, *extra)
        for item in arriving:
            item()
        for item in leaving:
            while item.waiting:
                item.send()
        for item in leaving:
            item.finish()

    moved = sum(a.size * a.dtype.itemsize for a in (*arrays, *outs))
    return pl.pallas_call(
        kernel,
        name=name,
        in_specs=[SMEM] * ns + [HBM] * na,
        out_specs=(HBM,) * no,
        out_shape=tuple(outs),
        scratch_shapes=[
            (pltpu.SMEM if a.dtype == jnp.int32 else pltpu.VMEM)(a.shape, a.dtype)
            for a in (*arrays, *outs)
        ]
        + [
            pltpu.SemaphoreType.DMA((sum(count for count, _ in counts),)),
            pltpu.SemaphoreType.DMA((sum(out_counts),)),
        ]
        + scratch,
        compiler_params=pltpu.CompilerParams(vmem_limit_bytes=64 << 20),
        cost_estimate=pl.CostEstimate(flops=flops, bytes_accessed=moved, transcendentals=0),
    )(*scalars, *arrays)


def dot(a, b):
    return jnp.dot(a, b, preferred_element_type=F32)


def dot_transposed(a, b):
    return dot(a.T, b)


def column_of(row_vector, width):
    return jnp.broadcast_to(row_vector, (width, row_vector.shape[1])).T


def partner(me, d, number, receive):
    if number & (number - 1) == 0:
        return me ^ d
    other = me + (number - d if receive else d)
    return jnp.where(other >= number, other - number, other)


def send_duals(refineries, dual_q, me, rows, src, swing, carry, outs, acc, product):
    own, *sends, carried = outs
    acc[...] = jnp.zeros_like(acc)
    carried.ref[...] = dot_transposed(carry[0], dual_q[0]).astype(BF16)
    carried.send()
    for m in range(swing.shape[0]):
        product[m] = dot_transposed(swing[m], dual_q[rows[m]])
    for m in range(swing.shape[0]):
        acc[src[m]] += product[m]
    for d, send in enumerate(sends, 1):
        send.ref[...] = acc[pl.ds(partner(me, d, refineries, False) * SC, SC)].astype(BF16)
        send.send()
    own.ref[...] = acc[pl.ds(me * SC, SC)]
    own.send()


def first_duals_body(refineries, scalars, ins, outs, acc, product, dual_q):
    (me,) = scalars
    rows, src, annual, dual, carry, swing = ins
    weekly = outs[0]
    rounded = annual()[...].astype(BF16)
    for w in range(weekly.ref.shape[0]):
        weekly.ref[w] = rounded
    weekly.send()
    size = rounded.shape[0]
    dual = dual()
    for i in range(dual_q.shape[0]):
        dual_q[i] = dual[i * size : (i + 1) * size].astype(BF16)
    send_duals(
        refineries, dual_q, me[0], rows(), src(), swing(), carry(), outs[1:], acc, product
    )


def turned_blocks(dual, size):
    return jnp.concatenate(
        [dual[i * size : (i + 1) * size].astype(BF16).T for i in range(dual.shape[0] // size)], axis=1
    )


def adjoint(matrix, turned, size, primal, prices, out):
    part = dot(turned, matrix[...])
    primal, prices = primal(), prices()
    for j in range(part.shape[1] // size):
        at = slice(j * size, (j + 1) * size)
        out.ref[at] = primal[at] - PRIMAL_STEP * (prices[at] - part[:, at].T)


def dense_body(chunks, scalars, ins, outs, acc):
    rows, cols, count, dual, blocks, primal, prices = ins
    rows, cols = rows(), cols()
    matrix, out = outs
    size = blocks.target.shape[1]
    tiles = matrix.ref.shape[1] // size
    acc[...] = jnp.zeros_like(acc)
    count, dual = count(), dual()
    turned = turned_blocks(dual, size)
    slots = blocks.target.shape[0] // chunks
    for c in range(chunks):
        here = blocks.piece()

        def step(n, _):
            acc[rows[n] * tiles + cols[n]] += here[n].astype(F32)
            return 0

        lax.fori_loop(c * slots, jnp.minimum(count[0], (c + 1) * slots), step, 0)
    for i in range(matrix.ref.shape[0] // size):
        for j in range(tiles):
            at = (slice(i * size, (i + 1) * size), slice(j * size, (j + 1) * size))
            matrix.ref[at] = acc[i * tiles + j].astype(BF16)
        matrix.send()
    adjoint(matrix.ref, turned, size, primal, prices, out)


def adjoint_body(size, scalars, ins, outs):
    dual, matrix, primal, prices, carried = ins
    adjoint(matrix(), turned_blocks(dual(), size), size, primal, prices, outs[0])
    outs[0].ref[-size:] += PRIMAL_STEP * carried()[...].astype(F32)


def primal_body(with_carry, scalars, ins, outs, acc, image_acc, product, bound):
    ids, cols, upper, annual, annual_q, own, *arrived, partial, primal = ins
    image, last, extrap, updated, streams = outs
    blocks, size, _ = extrap.ref.shape
    acc[...] = jnp.zeros_like(acc)
    image_acc[...] = jnp.zeros_like(image_acc)
    ids, cols, upper = ids(), cols(), upper()
    for j in range(blocks):
        bound[j] = column_of(upper[j : j + 1], bound.shape[2])
    annual, annual_q = annual(), annual_q()
    slots = annual.shape[0]
    for k in range(slots):
        product[k] = dot_transposed(annual[k], annual_q[ids[k]])
    for k in range(slots):
        acc[cols[k]] += product[k]
    if with_carry:
        acc[blocks - 1] += arrived.pop(0)()[...].astype(F32)
    total = own()[...]
    for piece in arrived:
        total = total + piece()[...].astype(F32)
    acc[:SC] += total
    partial, primal = partial(), primal()
    for j in range(blocks):
        at = slice(j * size, (j + 1) * size)
        new = jnp.clip(partial[at] + PRIMAL_STEP * acc[j], 0.0, bound[j])
        updated.ref[at] = new
        ahead = (2.0 * new - primal[at]).astype(BF16)
        extrap.ref[j] = ahead
        if j < SC:
            streams.ref[j] = ahead
        if j == SC - 1:
            streams.send()
        if j == blocks - 1:
            last.ref[...] = ahead
            last.send()
    extrap.send()
    updated.send()
    for k in range(slots):
        product[k] = dot(annual[k], extrap.ref[cols[k]])
    for k in range(slots):
        image_acc[ids[k]] += product[k]
    image.ref[...] = image_acc[...].astype(BF16)


def forward_body(scalars, ins, outs):
    extrap, demand, dual, matrix = ins
    out = outs[0]
    extrap, demand, dual = extrap(), demand(), dual()
    blocks, size, width = extrap.shape
    right = jnp.concatenate([extrap[j] for j in range(blocks)], axis=0)
    for i in range(demand.shape[0]):
        at = slice(i * size, (i + 1) * size)
        out.ref[at] = dual[at] + DUAL_STEP * column_of(demand[i : i + 1], width)
    out.ref[...] -= DUAL_STEP * dot(matrix()[...], right)


def dual_body(refineries, scalars, ins, outs, gathered, acc, product, stream_acc, dual_q):
    (me,) = scalars
    rows, src, swing, streams, *arrived, carry, previous, parts, annual, need, partial = ins
    dual, annual_out = outs[0], outs[1]
    rows, src, swing = rows(), src(), swing()
    size = swing.shape[1]
    mine = me[0]
    gathered[pl.ds(mine * SC, SC)] = streams()[...]
    for d, piece in enumerate(arrived, 1):
        gathered[pl.ds(partner(mine, d, refineries, True) * SC, SC)] = piece()[...]
    acc[...] = jnp.zeros_like(acc)
    for m in range(swing.shape[0]):
        product[m] = dot(swing[m], gathered[src[m]])
    for m in range(swing.shape[0]):
        acc[rows[m]] += product[m]
    carry = carry()
    acc[0] += dot(carry[0], previous()[...])
    parts, annual = parts(), annual()
    total = parts[0].astype(F32)
    for w in range(1, parts.shape[0]):
        total = total + parts[w].astype(F32)
    new_annual = jnp.maximum(
        annual[...] + DUAL_STEP * (column_of(need()[...], annual.shape[1]) - total), 0.0
    )
    annual_out.ref[...] = new_annual
    annual_out.send()
    rounded = new_annual.astype(BF16)
    for w in range(parts.shape[0]):
        outs[2].ref[w] = rounded
    outs[2].send()
    partial = partial()
    for i in range(acc.shape[0]):
        at = slice(i * size, (i + 1) * size)
        new = jnp.maximum(partial[at] - DUAL_STEP * acc[i], 0.0)
        dual.ref[at] = new
        dual_q[i] = new.astype(BF16)
    dual.send()
    send_duals(
        refineries, dual_q, mine, rows, src, swing, carry, outs[3:], stream_acc, product
    )


def last_rows_body(refineries, chunks, scalars, ins, outs, gathered, acc, product):
    (me,) = scalars
    rows, src, demand, swing, streams, *arrived, dual, extrap, matrix = ins
    out = outs[0]
    rows, src, demand, swing, mine = rows(), src(), demand(), swing(), me[0]
    size, width = swing.shape[1], gathered.shape[2]
    acc[...] = jnp.zeros_like(acc)
    gathered[pl.ds(mine * SC, SC)] = streams()[...]
    for d, piece in enumerate(arrived, 1):
        gathered[pl.ds(partner(mine, d, refineries, True) * SC, SC)] = piece()[...]
    for m in range(swing.shape[0]):
        product[m] = dot(swing[m], gathered[src[m]])
    for m in range(swing.shape[0]):
        acc[rows[m]] += product[m]
    dual, extrap = dual(), extrap()
    for i in range(demand.shape[0]):
        at = slice(i * size, (i + 1) * size)
        out.ref[at] = dual[at] + DUAL_STEP * (column_of(demand[i : i + 1], width) - acc[i])
    right = jnp.concatenate([extrap[j] for j in range(extrap.shape[0])], axis=0)
    step = out.ref.shape[0] // chunks
    for c in range(chunks):
        lines = slice(c * step, (c + 1) * step)
        new = out.ref[lines] - DUAL_STEP * dot(matrix.piece()[lines], right)
        if c:
            out.ref[lines] = jnp.maximum(new, 0.0)
        else:
            out.ref[:size] = new[:size]
            out.ref[size:step] = jnp.maximum(new[size:], 0.0)
        out.send()


def finish_kernel(
    row, annual, need, parts, carry, previous, dual_out, annual_out,
    row_v, annual_v, need_v, parts_v, carry_v, previous_v, new_v, in_sems, out_sems,
):
    size = row_v.shape[0]
    head = pl.ds(0, size)
    sources = (row.at[head], carry, previous, annual, need, parts)
    landing = (row_v, carry_v, previous_v, annual_v, need_v, parts_v)
    copies = [
        pltpu.make_async_copy(source, target, in_sems.at[i])
        for i, (source, target) in enumerate(zip(sources, landing))
    ]
    for copy in copies:
        copy.start()
    for copy in copies[:3]:
        copy.wait()
    row_v[...] = jnp.maximum(row_v[...] - DUAL_STEP * dot(carry_v[0], previous_v[...]), 0.0)
    first = pltpu.make_async_copy(row_v, dual_out.at[head], out_sems.at[0])
    first.start()
    for copy in copies[3:]:
        copy.wait()
    total = parts_v[0].astype(F32)
    for w in range(1, parts_v.shape[0]):
        total = total + parts_v[w].astype(F32)
    new_v[...] = jnp.maximum(
        annual_v[...] + DUAL_STEP * (column_of(need_v[...], annual_v.shape[1]) - total), 0.0
    )
    second = pltpu.make_async_copy(new_v, annual_out, out_sems.at[1])
    second.start()
    first.wait()
    second.wait()


def finish(dual, annual, need, parts, carry, previous):
    size, width = annual.shape
    arrays = (dual, annual, need, parts, carry, previous)
    buffers = (annual, annual, need, parts, carry, previous, annual)
    return pl.pallas_call(
        finish_kernel,
        name="finish",
        in_specs=[HBM] * 6,
        out_specs=(HBM, HBM),
        out_shape=(shape(dual.shape, F32), shape(annual.shape, F32)),
        scratch_shapes=[pltpu.VMEM(a.shape, a.dtype) for a in buffers]
        + [pltpu.SemaphoreType.DMA((6,)), pltpu.SemaphoreType.DMA((2,))],
        input_output_aliases={0: 0},
        compiler_params=pltpu.CompilerParams(vmem_limit_bytes=64 << 20),
        cost_estimate=pl.CostEstimate(
            flops=2 * size * size * width, bytes_accessed=1_000_000, transcendentals=0
        ),
    )(*arrays)


def shifted(block, axis, distance):
    number = lax.axis_size(axis)
    route = [((i - distance) % number, i) for i in range(number)]
    return lax.ppermute(block, axis, route)


def exchanged(block, axis, d):
    number = lax.axis_size(axis)
    if number & (number - 1) == 0:
        return lax.ppermute(block, axis, [(i, i ^ d) for i in range(number)])
    return shifted(block, axis, d)


def body(
    local_blocks,
    local_rows,
    local_cols,
    band_count,
    swing_blocks,
    swing_rows,
    swing_src,
    carry_blocks,
    annual_blocks,
    annual_ids,
    annual_cols,
    cost,
    upper,
    demand,
    annual_bound,
    x_start,
    y_start,
    annual_start,
):
    scenarios = cost.shape[1]
    size = local_blocks.shape[1]
    columns = cost.shape[0] // size
    rows = y_start.shape[0] // size
    slots = local_blocks.shape[0]
    weeks = lax.axis_size("period")
    refineries = lax.axis_size("refinery")
    others = refineries - 1
    me = lax.axis_index("refinery").astype(jnp.int32).reshape(1)
    tile = shape((size, scenarios), BF16)
    pair_q = shape((SC, size, scenarios), BF16)
    pair = shape((SC, size, scenarios), F32)
    state_x = shape((columns * size, scenarios), F32)
    state_y = shape((rows * size, scenarios), F32)
    blocks_x = shape((columns, size, scenarios), BF16)
    blocks_y = shape((rows, size, scenarios), BF16)
    weekly = shape((weeks, size, scenarios), BF16)
    matrix = shape((rows * size, columns * size), BF16)
    swings = swing_blocks.shape[0]
    annuals = annual_blocks.shape[0]
    unit = 2 * size * size * scenarios
    stream_scratch = pltpu.VMEM((refineries * SC, size, scenarios), F32)
    swing_scratch = pltpu.VMEM((swings, size, scenarios), F32)
    annual_scratch = pltpu.VMEM((annuals, size, scenarios), F32)
    sends_shape = [pair] + [pair_q] * others + [tile]
    pieces_y = 4 if rows % 8 == 0 else 1
    chunks = 8 if slots % 8 == 0 else 1

    upper_rows = upper.reshape(columns, size)
    demand_rows = demand.reshape(rows, size)
    need = annual_bound.reshape(1, size)
    primal, dual, annual = x_start, y_start, annual_start
    annual_send, own, *rest = run(
        functools.partial(first_duals_body, refineries),
        "first_duals",
        [me],
        [swing_rows, swing_src, annual, dual, carry_blocks, swing_blocks],
        [weekly] + sends_shape,
        [stream_scratch, swing_scratch, pltpu.VMEM(blocks_y.shape, BF16)],
        (swings + 1) * unit,
    )
    for iteration in range(ITERS):
        more = iteration + 1 < ITERS
        sends, carried = rest[:others], rest[others]
        annual_q = lax.all_to_all(annual_send, "period", 0, 0, tiled=True)
        carried_back = shifted(carried, "period", -1)
        carries = [carried_back] if iteration == 0 else []
        arrived = carries + [exchanged(send, "refinery", d) for d, send in enumerate(sends, 1)]
        if iteration == 0:
            matrix_q, partial_x = run(
                functools.partial(dense_body, chunks),
                "dense",
                [],
                [local_rows, local_cols, band_count, dual, local_blocks, primal, cost],
                [matrix, state_x],
                [pltpu.VMEM((rows * columns, size, size), F32)],
                2 * rows * columns * unit,
                {4: (chunks, 0)},
                {0: rows},
            )
        else:
            (partial_x,) = run(
                functools.partial(adjoint_body, size),
                "adjoint",
                [],
                [dual, matrix_q, primal, cost, carried_back],
                [state_x],
                [],
                90 * rows * columns * unit,
            )
        image, last, extrap, updated, streams = run(
            functools.partial(primal_body, iteration == 0),
            "primal_step",
            [],
            [annual_ids, annual_cols, upper_rows, annual_blocks, annual_q, own, *arrived, partial_x, primal],
            [weekly, tile, blocks_x, state_x, pair_q],
            [
                pltpu.VMEM((columns, size, scenarios), F32),
                pltpu.VMEM((weeks, size, scenarios), F32),
                annual_scratch,
                pltpu.VMEM((columns, size, scenarios), F32),
            ],
            2 * annuals * unit,
        )
        parts = lax.all_to_all(image, "period", 0, 0, tiled=True)
        previous = shifted(last, "period", 1)
        others_streams = [exchanged(streams, "refinery", d) for d in range(1, refineries)]
        if not more:
            (dual,) = run(
                functools.partial(last_rows_body, refineries, pieces_y),
                "last_rows",
                [me],
                [
                    swing_rows, swing_src, demand_rows, swing_blocks, streams, *others_streams,
                    dual, extrap, matrix_q,
                ],
                [state_y],
                [
                    pltpu.VMEM((refineries * SC, size, scenarios), BF16),
                    pltpu.VMEM((rows, size, scenarios), F32),
                    swing_scratch,
                ],
                unit,
                {7 + others: (pieces_y, 0)},
                {0: pieces_y},
            )
            dual, annual = finish(dual, annual, need, parts, carry_blocks, previous)
            return updated, dual, annual
        (partial_y,) = run(
            forward_body,
            "forward",
            [],
            [extrap, demand_rows, dual, matrix_q],
            [state_y],
            [],
            16 * rows * columns * unit,
        )
        sent = [weekly] + sends_shape
        dual, annual, *rest = run(
            functools.partial(dual_body, refineries),
            "dual_step",
            [me],
            [
                swing_rows, swing_src, swing_blocks, streams, *others_streams, carry_blocks, previous, parts, annual,
                need, partial_y,
            ],
            [state_y, shape((size, scenarios), F32)] + sent,
            [
                pltpu.VMEM((refineries * SC, size, scenarios), BF16),
                pltpu.VMEM((rows, size, scenarios), F32),
                swing_scratch,
            ]
            + [stream_scratch, pltpu.VMEM(blocks_y.shape, BF16)],
            2 * swings * unit,
        )
        annual_send, own, *rest = rest
        primal = updated


def solution(mesh):
    both = P(("period", "refinery"))
    wide = P(("period", "refinery"), None)
    cube = P(("period", "refinery"), None, None)
    return jax.shard_map(
        body,
        mesh=mesh,
        in_specs=(
            cube, both, both, both, cube, both, both, cube, cube, both, both,
            wide, both, both, both, wide, wide, wide,
        ),
        out_specs=(wide, wide, wide),
        check_vma=False,
    )
```
